32 devices in a mesh: groups: 2 (over y), tm: 4 (over z), head: 4 (over x, core).
Axes of the slice: x: 2, y: 2, z: 4, core: 2. Of those that a mesh axis runs over, the one named last changes fastest.
Arguments:
- queries: bfloat16 [3072, 24, 128], P(('groups', 'tm'), 'head'), parts along dimension 0, may hold values from -6 to 6
- key_rows: bfloat16 [3072, 24, 128], P(('groups', 'tm'), 'head'), parts along dimension 0, may hold values from -6 to 6
- value_rows: bfloat16 [3072, 24, 128], P(('groups', 'tm'), 'head'), parts along dimension 0, may hold values from -6 to 6
- keep_tiles: int32 [24, 9], P(('groups', 'tm')), parts along dimension 0, may hold values from 0 to 1, as said below
- out_weight: bfloat16 [3072, 5120], P('head', 'tm'), may hold values from -0.109375 to 0.109375
- gate_scale: float32 [10240], P(('groups', 'head')), parts along dimension 0, may hold values from 1 to 3
Outputs:
- gated_branch: bfloat16 [3072, 5120], P(('groups', 'tm'), 'head'), parts along dimension 0
The draws below stay inside these ranges and needn't reach their ends.
There are 2 independent parts, one for each index of `groups`. The reference program is written for one: setup_inputs(seed, part) draws one part's arguments, and reference() takes and returns one part's arrays. A program takes and returns all parts, laid end to end along the dimension named above; an argument that names none is the same for every part. Nothing has to cross between parts.
Inputs may be any that keep to these rules, and one draw needn't show every extreme that they name: `keep_tiles`: each row is one query tile; the query tile itself is always kept; each row keeps 3 to 6 tiles, and some row keeps exactly 6.
All inputs are finite; a program needn't handle non-finite values.
Results may differ from the reference program's by a relative error of at most 0.014.
Values may be sent and summed in bfloat16 or wider, within the bound.
A program may use at most 64 MiB of HBM per device.

```python
import math
import jax
import jax.numpy as jnp
from jax import lax

D = 5120
HEADS = 24
HD = 128
TILE = 128
TILES_DEV = 3
KEEP_MIN = 3
KEEP_MAX = 6
TOK_DEV = 384
TOKENS = 1536
TILES = 12
REACH = 1
CAND = 9
N_TM = 4
N_HEAD = 4


def shared_rows(key, which):
    shape = (TOKENS, HEADS, HD)
    base = jax.random.normal(jax.random.fold_in(key, 11 + which), shape, jnp.float32) * 1.5
    return jnp.clip(base, -6.0, 6.0)


def draw_queries(key, part):
    return shared_rows(key, 0).astype(jnp.bfloat16)


def draw_key_rows(key, part):
    return shared_rows(key, 1).astype(jnp.bfloat16)


def draw_keep_tiles(key, part):
    counts = jax.random.randint(jax.random.fold_in(key, 1), (TILES,), KEEP_MIN, KEEP_MAX + 1)
    special = jax.random.randint(jax.random.fold_in(key, 2), (), 0, TILES)
    row_ids = jnp.arange(TILES, dtype=jnp.int32)
    counts = jnp.where(row_ids == special, KEEP_MAX, counts)
    row_keys = jax.random.split(jax.random.fold_in(key, 3), TILES)
    ranking = jax.vmap(lambda row_key: jax.random.permutation(row_key, CAND))(row_keys).astype(jnp.int32)
    own_index = REACH * TILES_DEV + row_ids % TILES_DEV
    cand_ids = jnp.arange(CAND, dtype=jnp.int32)
    own_rank = jnp.sum(jnp.where(cand_ids[None, :] == own_index[:, None], ranking, 0), axis=1)
    other_rank = ranking - (ranking > own_rank[:, None]).astype(jnp.int32)
    is_own = cand_ids[None, :] == own_index[:, None]
    kept = is_own | ~is_own & (other_rank < counts[:, None] - 1)
    return kept.astype(jnp.int32)


def shard_levels(rng, extent, cuts, smallest, top_value):
    gain, own = 1.0, jax.random.fold_in(rng, 6)
    for position, shards_of in cuts:
        heights = jnp.exp(jax.random.uniform(jax.random.fold_in(own, position), (shards_of,), jnp.float32, smallest / len(cuts), top_value / len(cuts)))
        gain = gain * jnp.repeat(heights, extent[position] // shards_of).reshape([-1 if axis == position else 1 for axis in range(len(extent))])
    return gain


def centred(rng, shape, scale, limit, pieces=(), kind=jnp.bfloat16):
    level = shard_levels(rng, shape, pieces, -0.22, 0.18) if pieces else 1.0
    values = jax.random.normal(rng, shape, jnp.float32) * scale * level
    return jnp.minimum(jnp.maximum(values, -limit), limit).astype(kind)


def setup_inputs(seed: int = 0, part: int = 0) -> dict:
    streams_of = jax.random.split(jax.random.key(seed), 7)
    own_keys = jax.random.split(jax.random.fold_in(streams_of[6], part), 7)
    queries = draw_queries(jax.random.fold_in(jax.random.fold_in(streams_of[6], part), 71), part)
    key_rows = draw_key_rows(jax.random.fold_in(jax.random.fold_in(streams_of[6], part), 71), part)
    value_rows = centred(own_keys[2], (TOKENS, HEADS, HD), 1.0, 6.0, ((0, 4), (1, 4)))
    keep_tiles = draw_keep_tiles(jax.random.fold_in(jax.random.fold_in(streams_of[6], part), 71), part)
    out_weight = centred(streams_of[4], (HEADS * HD, D), (HEADS * HD) ** -0.5, 0.109375, ((0, 4), (1, 4)))
    gate_scale = jnp.clip(1.0 + 2.0 * jax.random.uniform(own_keys[5], (D,), jnp.float32) ** shard_levels(own_keys[5], (D,), ((0, 4),), -0.2, 0.2), 1.0, 3.0)
    return {"queries": queries, "key_rows": key_rows, "value_rows": value_rows, "keep_tiles": keep_tiles, "out_weight": out_weight, "gate_scale": gate_scale}


def expand_mask(keep_rows, tile_len):
    tile_count, cand_count = keep_rows.shape
    wide = jnp.broadcast_to(keep_rows[:, None, :, None], (tile_count, tile_len, cand_count, tile_len))
    return wide.reshape(tile_count * tile_len, cand_count * tile_len)

def softmax_attend(query_block, key_block, value_block, allowed):
    score_scale = 1.0 / math.sqrt(HD)
    scores = jnp.einsum('qhd,khd->hqk', query_block.astype(jnp.float32), key_block.astype(jnp.float32)) * score_scale
    scores = jnp.where(allowed[None] > 0, scores, -jnp.inf)
    row_peak = lax.optimization_barrier(jnp.max(scores, axis=-1, keepdims=True))
    exp_scores = jnp.exp(scores - row_peak)
    row_total = lax.optimization_barrier(jnp.sum(exp_scores, axis=-1, keepdims=True))
    weights = (exp_scores / row_total).astype(jnp.bfloat16)
    attended = jnp.einsum('hqk,khd->qhd', weights.astype(jnp.float32), value_block.astype(jnp.float32))
    return attended.astype(jnp.bfloat16)

def reference(queries, key_rows, value_rows, keep_tiles, out_weight, gate_scale):
    slab_queries = queries.reshape(N_TM, TOK_DEV, HEADS, HD)
    slab_keys = key_rows.reshape(N_TM, TOK_DEV, HEADS, HD)
    slab_values = value_rows.reshape(N_TM, TOK_DEV, HEADS, HD)
    keep_slabs = keep_tiles.reshape(N_TM, TILES_DEV, CAND)
    offsets = jnp.arange(-REACH, REACH + 1, dtype=jnp.int32)

    def one_slab(slab_index):
        order = ((slab_index + offsets) % N_TM).astype(jnp.int32)
        cand_keys = jnp.take(slab_keys, order, axis=0).reshape(CAND * TILE, HEADS, HD)
        cand_values = jnp.take(slab_values, order, axis=0).reshape(CAND * TILE, HEADS, HD)
        allowed = expand_mask(keep_slabs[slab_index], TILE)
        return softmax_attend(slab_queries[slab_index], cand_keys, cand_values, allowed)
    attended = lax.map(one_slab, jnp.arange(N_TM, dtype=jnp.int32)).reshape(TOKENS, HEADS * HD)
    group_rows = HEADS * HD // N_HEAD
    projected = jnp.zeros((TOKENS, D), jnp.float32)
    for group_index in range(N_HEAD):
        lower_row = group_index * group_rows
        group_term = jnp.dot(attended[:, lower_row:lower_row + group_rows], out_weight[lower_row:lower_row + group_rows], preferred_element_type=jnp.float32)
        projected = projected + lax.optimization_barrier(group_term.astype(jnp.bfloat16)).astype(jnp.float32)
    return (gate_scale[None, :] * projected).astype(jnp.bfloat16)
```

```python
import functools
import math

import jax
import jax.numpy as jnp
from jax import lax
from jax.experimental import pallas as pl
from jax.experimental.pallas import tpu as pltpu
from jax.sharding import PartitionSpec as P

HD = 128
TILE = 128
MESH = pl.DeviceIdType.MESH


def layer_kernel(
    sizes, q_ref, k_ref, v_ref, keep_ref, w_ref, gate_ref, out_ref,
    q_own, k_all, v_all, w_all, attended, part, got,
    kv_send, kv_recv, z_send, z_recv, y_send, y_recv, r_send, r_recv, own_sem, in_sem,
):
    groups, n, heads, reach, pieces = sizes
    g, t, me = lax.axis_index("groups"), lax.axis_index("tm"), lax.axis_index("head")
    rows, cols = w_ref.shape
    wide = cols // pieces
    per_head = n // heads
    part_rows = rows // groups
    head_count, tokens = q_ref.shape[0], q_ref.shape[1]
    slabs = 2 * reach + 1

    barrier = pltpu.get_barrier_semaphore()
    partners = []
    for d in range(1, reach + 1):
        partners += [{"tm": lax.rem(t + d, n)}, {"tm": lax.rem(t + n - d, n)}]
    for o in range(1, groups):
        partners.append({"groups": lax.rem(g + o, groups)})
    for o in range(1, heads):
        partners.append({"head": lax.rem(me + o, heads)})
    for partner in partners:
        pl.semaphore_signal(barrier, inc=1, device_id=partner, device_id_type=MESH)
    pl.semaphore_wait(barrier, len(partners))

    def remote(src, dst, send, recv, device):
        return pltpu.make_async_remote_copy(
            src_ref=src, dst_ref=dst, send_sem=send, recv_sem=recv,
            device_id=device, device_id_type=MESH,
        )

    kv_copies = []
    for d in range(1, reach + 1):
        for slot, to in ((reach - d, lax.rem(t + d, n)), (reach + d, lax.rem(t + n - d, n))):
            for which, (src, dst) in enumerate(((k_ref, k_all), (v_ref, v_all))):
                kv_copies.append(
                    remote(src, dst.at[slot], kv_send.at[slot, which], kv_recv.at[slot, which], {"tm": to})
                )
    @pl.when(t == 0)
    def _():
        for copy in reversed(kv_copies):
            copy.start()

    @pl.when(t != 0)
    def _():
        for copy in kv_copies:
            copy.start()

    in_copies = [
        pltpu.make_async_copy(src, dst, in_sem.at[i])
        for i, (src, dst) in enumerate(
            ((q_ref, q_own), (k_ref, k_all.at[reach]), (v_ref, v_all.at[reach]))
        )
    ]
    for copy in in_copies:
        copy.start()

    my_rows = pl.ds(pl.multiple_of(g * part_rows, part_rows), part_rows)

    def own_copy(c):
        return pltpu.make_async_copy(
            w_ref.at[:, c * wide:(c + 1) * wide], w_all.at[t, c], own_sem.at[c]
        )

    def first_send(c, side):
        to = jnp.minimum(t + 1, n - 1) if side else jnp.maximum(t - 1, 0)
        return remote(
            w_ref.at[my_rows, c * wide:(c + 1) * wide], w_all.at[t, c, my_rows],
            z_send.at[side, t, c], z_recv.at[t, c], {"tm": to},
        )

    def relay(b, c, side):
        to = jnp.minimum(t + 1, n - 1) if side else jnp.maximum(t - 1, 0)
        return remote(
            w_all.at[b, c, my_rows], w_all.at[b, c, my_rows],
            z_send.at[side, b, c], z_recv.at[b, c], {"tm": to},
        )

    def across(b, c, o):
        return remote(
            w_all.at[b, c, my_rows], w_all.at[b, c, my_rows],
            y_send.at[o - 1, b, c], y_recv.at[o - 1, b, c],
            {"groups": lax.rem(g + o, groups)},
        )

    def across_arrival(b, c, o):
        sender = lax.rem(g + groups - o, groups)
        their_rows = pl.ds(pl.multiple_of(sender * part_rows, part_rows), part_rows)
        return remote(
            w_all.at[b, c, their_rows], w_all.at[b, c, their_rows],
            y_send.at[o - 1, b, c], y_recv.at[o - 1, b, c],
            {"groups": lax.rem(g + o, groups)},
        )

    def term_send(b, c, o):
        return remote(
            part.at[b, c], got.at[o - 1, b % per_head, c],
            r_send.at[b, c], r_recv.at[o - 1, b % per_head, c],
            {"head": lax.rem(me + o, heads)},
        )

    for c in range(pieces):
        own_copy(c).start()
        @pl.when(t < n - 1)
        def _(c=c):
            first_send(c, 1).start()
        @pl.when(t > 0)
        def _(c=c):
            first_send(c, 0).start()

    for copy in in_copies:
        copy.wait()
    for copy in kv_copies:
        copy.wait_recv()

    scale = 1.0 / math.sqrt(HD)
    per_slab = tokens // TILE

    early = min(pieces, head_count - 1)

    def pass_on(j, side):
        step, c = j // pieces, j % pieces
        b = (t - 1 - step) if side else (t + 1 + step)
        @pl.when((b >= 0) & (b <= n - 1))
        def _():
            relay(b, c, side).wait_recv()
            @pl.when((t < n - 1) if side else (t > 0))
            def _():
                relay(b, c, side).start()
            for o in range(1, groups):
                across(b, c, o).start()

    def one_head(h, carry):
        lanes = pl.ds(pl.multiple_of(h * HD, HD), HD)
        for i in range(per_slab):
            q = q_own[h, i * TILE:(i + 1) * TILE, :]
            scores = []
            for j in range(slabs):
                s = lax.dot_general(
                    q, k_all[j, h], (((1,), (1,)), ((), ())), preferred_element_type=jnp.float32
                )
                bias = jnp.concatenate(
                    [
                        jnp.full(
                            (1, TILE),
                            jnp.where(keep_ref[i, j * per_slab + u] > 0, 0.0, -jnp.inf),
                            jnp.float32,
                        )
                        for u in range(per_slab)
                    ],
                    axis=1,
                )
                scores.append(s * scale + bias)
            peak = functools.reduce(
                jnp.maximum, [jnp.max(s, axis=1, keepdims=True) for s in scores]
            )
            exps = [jnp.exp(s - peak) for s in scores]
            total = functools.reduce(jnp.add, [jnp.sum(e, axis=1, keepdims=True) for e in exps])
            inverse = 1.0 / total
            acc = None
            for j in range(slabs):
                term = jnp.dot(
                    (exps[j] * inverse).astype(jnp.bfloat16), v_all[j, h],
                    preferred_element_type=jnp.float32,
                )
                acc = term if acc is None else acc + term
            attended[i * TILE:(i + 1) * TILE, lanes] = acc.astype(jnp.bfloat16)
        @pl.when(h >= head_count - early)
        def _():
            for side in (1, 0):
                pass_on(h - (head_count - early), side)
        return carry

    lax.fori_loop(0, head_count, one_head, 0)

    def project(b, c):
        def tile(i, carry):
            at = pl.ds(pl.multiple_of(i * TILE, TILE), TILE)
            part[b, c, at, :] = jnp.dot(
                attended[at, :], w_all[b, c], preferred_element_type=jnp.float32
            ).astype(jnp.bfloat16)
            return carry

        lax.fori_loop(0, tokens // TILE, tile, 0)
        owner = b // per_head
        for o in range(1, heads):
            @pl.when(owner == lax.rem(me + o, heads))
            def _():
                term_send(b, c, o).start()

    for c in range(pieces):
        own_copy(c).wait()
        project(t, c)

    def use(j, side):
        step, c = j // pieces, j % pieces
        b = (t - 1 - step) if side else (t + 1 + step)
        @pl.when((b >= 0) & (b <= n - 1))
        def _():
            for o in range(1, groups):
                across_arrival(b, c, o).wait_recv()
            project(b, c)

    count = (n - 1) * pieces

    def use_both(j, carry):
        for side in (1, 0):
            use(j, side)
        return carry

    def step(j, carry):
        for side in (1, 0):
            pass_on(j, side)
        first = jnp.minimum(2 * (j - early), j - 1)
        last = jnp.minimum(2 * (j - early) + 2, j)
        return lax.fori_loop(first, last, use_both, carry)

    lax.fori_loop(early, count, step, 0)
    lax.fori_loop(min(2 * (count - early), count - 1), count, use_both, 0)

    for cb in range(per_head):
        for c in range(pieces):
            b = me * per_head + cb
            for o in range(1, heads):
                term_send(b, c, o).wait_recv()
            span = wide if gate_ref.shape[0] == 1 else gate_ref.shape[1]
            for u in range(wide // span):
                lanes = slice(u * span, (u + 1) * span)
                summed = part[b, c, :, lanes].astype(jnp.float32)
                for o in range(1, heads):
                    summed = summed + got[o - 1, cb, c, :, lanes].astype(jnp.float32)
                at = cb * cols + c * wide + u * span
                gate = gate_ref[:, at:at + span] if span == wide else gate_ref[at // span:at // span + 1, :]
                out_ref[:, at:at + span] = (gate * summed).astype(out_ref.dtype)

    for copy in kv_copies:
        copy.wait_send()
    for c in range(pieces):
        @pl.when(t < n - 1)
        def _(c=c):
            first_send(c, 1).wait_send()
        @pl.when(t > 0)
        def _(c=c):
            first_send(c, 0).wait_send()

    def drain(b, carry):
        for c in range(pieces):
            @pl.when(b != t)
            def _(c=c):
                for o in range(1, groups):
                    across(b, c, o).wait_send()
            @pl.when((b < t) & (t < n - 1))
            def _(c=c):
                relay(b, c, 1).wait_send()
            @pl.when((b > t) & (t > 0))
            def _(c=c):
                relay(b, c, 0).wait_send()
            @pl.when(b // per_head != me)
            def _(c=c):
                term_send(b, c, 1).wait_send()
        return carry

    lax.fori_loop(0, n, drain, 0)


def shards(queries, key_rows, value_rows, keep_tiles, out_weight, gate_scale):
    n, heads, groups = lax.axis_size("tm"), lax.axis_size("head"), lax.axis_size("groups")
    reach = min(2, (n - 1) // 2)
    tokens = queries.shape[0]
    head_count = queries.shape[1]
    flat = head_count * HD
    rows, cols = out_weight.shape
    pieces = cols // 256 if cols % 256 == 0 else 1
    wide = cols // pieces
    per_head = n // heads
    slabs = 2 * reach + 1
    gate_lanes = 128 if wide % 128 == 0 else gate_scale.shape[0]
    vmem = pl.BlockSpec(memory_space=pltpu.VMEM)
    hbm = pl.BlockSpec(memory_space=pl.ANY)
    dma = pltpu.SemaphoreType.DMA
    bf16 = jnp.bfloat16
    return pl.pallas_call(
        functools.partial(layer_kernel, (groups, n, heads, reach, pieces)),
        out_shape=jax.ShapeDtypeStruct((tokens, gate_scale.shape[0]), bf16),
        in_specs=[hbm, hbm, hbm, pl.BlockSpec(memory_space=pltpu.SMEM), hbm, vmem],
        out_specs=vmem,
        scratch_shapes=[
            pltpu.VMEM((head_count, tokens, HD), bf16),
            pltpu.VMEM((slabs, head_count, tokens, HD), bf16),
            pltpu.VMEM((slabs, head_count, tokens, HD), bf16),
            pltpu.VMEM((n, pieces, rows, wide), bf16),
            pltpu.VMEM((tokens, flat), bf16),
            pltpu.VMEM((n, pieces, tokens, wide), bf16),
            pltpu.VMEM((heads - 1, per_head, pieces, tokens, wide), bf16),
            dma((slabs, 2)),
            dma((slabs, 2)),
            dma((2, n, pieces)),
            dma((n, pieces)),
            dma((groups - 1, n, pieces)),
            dma((groups - 1, n, pieces)),
            dma((n, pieces)),
            dma((heads - 1, per_head, pieces)),
            dma((pieces,)),
            dma((3,)),
        ],
        compiler_params=pltpu.CompilerParams(
            collective_id=0, has_side_effects=True, vmem_limit_bytes=56 * 1024 * 1024
        ),
    )(
        queries.transpose(1, 0, 2),
        key_rows.transpose(1, 0, 2),
        value_rows.transpose(1, 0, 2),
        keep_tiles,
        out_weight,
        gate_scale.reshape(-1, gate_lanes),
    )


def chain_kernel(
    sizes, q_ref, k_ref, v_ref, keep_ref, w_ref, gate_ref, out_ref,
    q_own, q_far, k_all, v_all, w_all, attended, far_att, part, got, keep_far, bias,
    kv_send, kv_recv, q_send, q_recv, keep_sem, att_send, att_recv,
    z_send, z_recv, y_send, y_recv, r_send, r_recv, own_sem, in_sem,
):
    groups, n, heads, pieces = sizes
    g, t, me = lax.axis_index("groups"), lax.axis_index("tm"), lax.axis_index("head")
    rows, cols = w_ref.shape
    wide = cols // pieces
    per_head = n // heads
    part_rows = rows // groups
    head_count, tokens = q_ref.shape[0], q_ref.shape[1]
    per_slab = tokens // TILE
    total_pieces = n * pieces

    left = t < n // 2
    inner = (t > 0) & (t < n - 1)
    outer = jnp.logical_not(inner)
    end = jnp.where(left, 0, n - 1)
    near = jnp.where(left, 1, n - 2)
    across_mid = n - 1 - t
    far_end = n - 1 - end
    mate = jnp.where(inner, end, near)
    mate_id = {"tm": mate}
    mid_id = {"tm": across_mid}

    barrier = pltpu.get_barrier_semaphore()

    def greet(partner):
        pl.semaphore_signal(barrier, inc=1, device_id=partner, device_id_type=MESH)

    greet(mate_id)
    @pl.when(inner)
    def _():
        greet(mid_id)
    for o in range(1, groups):
        greet({"groups": lax.rem(g + o, groups)})
    for o in range(1, heads):
        greet({"head": lax.rem(me + o, heads)})
    @pl.when(inner)
    def _():
        pl.semaphore_wait(barrier, groups + heads)
    @pl.when(outer)
    def _():
        pl.semaphore_wait(barrier, groups + heads - 1)

    def remote(src, dst, send, recv, device):
        return pltpu.make_async_remote_copy(
            src_ref=src, dst_ref=dst, send_sem=send, recv_sem=recv,
            device_id=device, device_id_type=MESH,
        )

    kv = ((k_ref, k_all), (v_ref, v_all))

    def kv_first(h, which, device):
        src, dst = kv[which]
        return remote(
            src.at[h], dst.at[t, h], kv_send.at[0, which, h], kv_recv.at[t, which, h], device
        )

    def kv_relay(h, which):
        buf = kv[which][1]
        return remote(
            buf.at[end, h], buf.at[end, h], kv_send.at[1, which, h], kv_recv.at[end, which, h],
            mid_id,
        )

    def kv_arrival(slab, h, which):
        buf = kv[which][1]
        return remote(
            buf.at[slab, h], buf.at[slab, h], kv_send.at[1, which, h],
            kv_recv.at[slab, which, h], mid_id,
        )

    def q_copy(h):
        return remote(q_ref.at[h], q_far.at[h], q_send.at[h], q_recv.at[h], mate_id)

    keep_copy = remote(keep_ref, keep_far, keep_sem.at[0], keep_sem.at[1], mate_id)

    def lanes_of(h):
        return pl.ds(pl.multiple_of(h * HD, HD), HD)

    def att_copy(h):
        return remote(
            far_att.at[:, lanes_of(h)], attended.at[:, lanes_of(h)],
            att_send.at[h], att_recv.at[h], mate_id,
        )

    my_rows = pl.ds(pl.multiple_of(g * part_rows, part_rows), part_rows)

    def own_copy(c):
        return pltpu.make_async_copy(
            w_ref.at[:, c * wide:(c + 1) * wide], w_all.at[t, c], own_sem.at[c]
        )

    def first_send(c, way):
        return remote(
            w_ref.at[my_rows, c * wide:(c + 1) * wide], w_all.at[t, c, my_rows],
            z_send.at[way, t, c], z_recv.at[t, c], mid_id if way else mate_id,
        )

    def relay(b, c, way):
        return remote(
            w_all.at[b, c, my_rows], w_all.at[b, c, my_rows],
            z_send.at[way, b, c], z_recv.at[b, c], mid_id if way else mate_id,
        )

    def across(b, c, o):
        return remote(
            w_all.at[b, c, my_rows], w_all.at[b, c, my_rows],
            y_send.at[o - 1, b, c], y_recv.at[o - 1, b, c],
            {"groups": lax.rem(g + o, groups)},
        )

    def across_arrival(b, c, o):
        sender = lax.rem(g + groups - o, groups)
        their_rows = pl.ds(pl.multiple_of(sender * part_rows, part_rows), part_rows)
        return remote(
            w_all.at[b, c, their_rows], w_all.at[b, c, their_rows],
            y_send.at[o - 1, b, c], y_recv.at[o - 1, b, c],
            {"groups": lax.rem(g + o, groups)},
        )

    def term_send(b, c, o):
        return remote(
            part.at[b, c], got.at[o - 1, b % per_head, c],
            r_send.at[b, c], r_recv.at[o - 1, b % per_head, c],
            {"head": lax.rem(me + o, heads)},
        )

    in_copies = [
        pltpu.make_async_copy(src, dst, in_sem.at[i])
        for i, (src, dst) in enumerate(
            ((q_ref, q_own), (k_ref, k_all.at[t]), (v_ref, v_all.at[t]))
        )
    ]

    @pl.when(outer)
    def _():
        for h in range(head_count):
            for which in range(2):
                kv_first(h, which, mate_id).start()
        keep_copy.start()
        for h in range(head_count):
            q_copy(h).start()

    @pl.when(inner)
    def _():
        for h in range(head_count):
            for which in range(2):
                kv_first(h, which, mid_id).start()
        for copy in in_copies:
            copy.start()

    for c in range(pieces):
        first_send(c, 0).start()
    for c in range(pieces):
        own_copy(c).start()

    def block_of(k):
        place = jnp.where(left, t, n - 1 - t)
        b = jnp.where(k == 0, place, jnp.where(k == 1, 1 - place, k))
        return jnp.where(left, b, n - 1 - b)

    def pass_on(j):
        b, c = block_of(j // pieces), lax.rem(j, pieces)
        relay(b, c, 0).wait_recv()
        @pl.when(inner & (b == end))
        def _():
            relay(b, c, 1).start()
        @pl.when(inner & (b != end))
        def _():
            relay(b, c, 0).start()
        for o in range(1, groups):
            across(b, c, o).start()

    scale = math.log2(math.e) / math.sqrt(HD)
    reach_slabs = keep_ref.shape[1] // per_slab

    def set_bias(at, ref):
        kept = ref[...]
        spread = jnp.concatenate(
            [jnp.broadcast_to(kept[:, c:c + 1], (per_slab, TILE)) for c in range(kept.shape[1])],
            axis=1,
        )
        bias[at] = jnp.where(spread > 0, 0.0, -jnp.inf).astype(jnp.float32)

    def attend(h, slab, queries, at, dst):
        for i in range(per_slab):
            q = queries[h, i * TILE:(i + 1) * TILE, :]
            scores = []
            for j in range(reach_slabs):
                other = lax.rem(slab + j - reach_slabs // 2 + n, n)
                s = lax.dot_general(
                    q, k_all[other, h], (((1,), (1,)), ((), ())),
                    preferred_element_type=jnp.float32,
                )
                scores.append(s * scale + bias[at, i:i + 1, j * tokens:(j + 1) * tokens])
            peak = functools.reduce(
                jnp.maximum, [jnp.max(s, axis=1, keepdims=True) for s in scores]
            )
            exps = [jnp.exp2(s - peak) for s in scores]
            total = functools.reduce(jnp.add, [jnp.sum(e, axis=1, keepdims=True) for e in exps])
            acc = None
            for j in range(reach_slabs):
                other = lax.rem(slab + j - reach_slabs // 2 + n, n)
                term = jnp.dot(
                    exps[j].astype(jnp.bfloat16), v_all[other, h],
                    preferred_element_type=jnp.float32,
                )
                acc = term if acc is None else acc + term
            dst[i * TILE:(i + 1) * TILE, lanes_of(h)] = (acc * (1.0 / total)).astype(jnp.bfloat16)

    def project(b, c):
        def tile(i, carry):
            at = pl.ds(pl.multiple_of(i * TILE, TILE), TILE)
            part[b, c, at, :] = jnp.dot(
                attended[at, :], w_all[b, c], preferred_element_type=jnp.float32
            ).astype(jnp.bfloat16)
            return carry

        lax.fori_loop(0, tokens // TILE, tile, 0)
        owner = b // per_head
        for o in range(1, heads):
            @pl.when(owner == lax.rem(me + o, heads))
            def _():
                term_send(b, c, o).start()

    def use(j):
        b, c = block_of(j // pieces), lax.rem(j, pieces)
        for o in range(1, groups):
            across_arrival(b, c, o).wait_recv()
        project(b, c)

    def finish(j):
        b, c = block_of(j // pieces), lax.rem(j, pieces)
        cb = lax.rem(b, per_head)
        @pl.when(b // per_head == me)
        def _():
            for o in range(1, heads):
                term_send(b, c, o).wait_recv()
            summed = part[b, c].astype(jnp.float32)
            for o in range(1, heads):
                summed = summed + got[o - 1, cb, c].astype(jnp.float32)
            at = pl.ds(pl.multiple_of(cb * cols + c * wide, wide), wide)
            out_ref[:, at] = (gate_ref[:, at] * summed).astype(out_ref.dtype)

    def do_use(j, carry):
        use(j)
        return carry

    def do_finish(j, carry):
        finish(j)
        return carry

    def own_block(c, carry):
        project(t, c)
        return carry

    @pl.when(inner)
    def _():
        set_bias(0, keep_ref)
        for copy in in_copies:
            copy.wait()

        def own_slab(h, carry):
            for which in range(2):
                kv_arrival(end, h, which).wait_recv()
                kv_relay(h, which).start()
            for which in range(2):
                kv_arrival(across_mid, h, which).wait_recv()
            attend(h, t, q_own, 0, attended)
            return carry

        lax.fori_loop(0, head_count, own_slab, 0)
        for c in range(pieces):
            first_send(c, 1).start()
        for c in range(pieces):
            own_copy(c).wait()
        lax.fori_loop(0, pieces, own_block, 0)
        keep_copy.wait_recv()
        set_bias(1, keep_far)

        def end_slab(h, carry):
            q_copy(h).wait_recv()
            for which in range(2):
                kv_arrival(far_end, h, which).wait_recv()
            attend(h, end, q_far, 1, far_att)
            att_copy(h).start()
            return carry

        lax.fori_loop(0, head_count, end_slab, 0)

    def early_pass(j, carry):
        pass_on(j)
        return carry

    lax.fori_loop(pieces, 2 * pieces, early_pass, 0)

    @pl.when(outer)
    def _():
        for c in range(pieces):
            own_copy(c).wait()
        for h in range(head_count):
            att_copy(h).wait_recv()
        lax.fori_loop(0, pieces, own_block, 0)

    lax.fori_loop(pieces, 2 * pieces, do_use, 0)
    lax.fori_loop(0, 2 * pieces - 2, do_finish, 0)

    def step(j, carry):
        pass_on(j)
        @pl.when(j > 2 * pieces)
        def _():
            use(j - 1)
        finish(j - 2)
        return carry

    lax.fori_loop(2 * pieces, total_pieces, step, 0)
    use(total_pieces - 1)
    finish(total_pieces - 2)
    finish(total_pieces - 1)

    @pl.when(outer)
    def _():
        for h in range(head_count):
            for which in range(2):
                kv_first(h, which, mate_id).wait_send()
            q_copy(h).wait_send()
        keep_copy.wait_send()

    @pl.when(inner)
    def _():
        for h in range(head_count):
            for which in range(2):
                kv_first(h, which, mid_id).wait_send()
                kv_relay(h, which).wait_send()
            att_copy(h).wait_send()
        for c in range(pieces):
            first_send(c, 1).wait_send()

    def drain(b, carry):
        for c in range(pieces):
            @pl.when(b == t)
            def _(c=c):
                first_send(c, 0).wait_send()
            @pl.when(b != t)
            def _(c=c):
                for o in range(1, groups):
                    across(b, c, o).wait_send()
            @pl.when(inner & (b == end))
            def _(c=c):
                relay(b, c, 1).wait_send()
            @pl.when(inner & (b != end) & (b != t))
            def _(c=c):
                relay(b, c, 0).wait_send()
            @pl.when(b // per_head != me)
            def _(c=c):
                term_send(b, c, 1).wait_send()
        return carry

    lax.fori_loop(0, n, drain, 0)


def chain_shards(queries, key_rows, value_rows, keep_tiles, out_weight, gate_scale):
    n, heads, groups = lax.axis_size("tm"), lax.axis_size("head"), lax.axis_size("groups")
    tokens = queries.shape[0]
    head_count = queries.shape[1]
    flat = head_count * HD
    rows, cols = out_weight.shape
    pieces = cols // 256 if cols % 256 == 0 else 1
    wide = cols // pieces
    per_head = n // heads
    vmem = pl.BlockSpec(memory_space=pltpu.VMEM)
    hbm = pl.BlockSpec(memory_space=pl.ANY)
    dma = pltpu.SemaphoreType.DMA
    bf16 = jnp.bfloat16
    return pl.pallas_call(
        functools.partial(chain_kernel, (groups, n, heads, pieces)),
        out_shape=jax.ShapeDtypeStruct((tokens, gate_scale.shape[0]), bf16),
        in_specs=[hbm, hbm, hbm, vmem, hbm, vmem],
        out_specs=vmem,
        scratch_shapes=[
            pltpu.VMEM((head_count, tokens, HD), bf16),
            pltpu.VMEM((head_count, tokens, HD), bf16),
            pltpu.VMEM((n, head_count, tokens, HD), bf16),
            pltpu.VMEM((n, head_count, tokens, HD), bf16),
            pltpu.VMEM((n, pieces, rows, wide), bf16),
            pltpu.VMEM((tokens, flat), bf16),
            pltpu.VMEM((tokens, flat), bf16),
            pltpu.VMEM((n, pieces, tokens, wide), bf16),
            pltpu.VMEM((heads - 1, per_head, pieces, tokens, wide), bf16),
            pltpu.VMEM(keep_tiles.shape, jnp.int32),
            pltpu.VMEM((2, keep_tiles.shape[0], keep_tiles.shape[1] * TILE), jnp.float32),
            dma((2, 2, head_count)),
            dma((n, 2, head_count)),
            dma((head_count,)),
            dma((head_count,)),
            dma((2,)),
            dma((head_count,)),
            dma((head_count,)),
            dma((2, n, pieces)),
            dma((n, pieces)),
            dma((groups - 1, n, pieces)),
            dma((groups - 1, n, pieces)),
            dma((n, pieces)),
            dma((heads - 1, per_head, pieces)),
            dma((pieces,)),
            dma((3,)),
        ],
        compiler_params=pltpu.CompilerParams(
            collective_id=0, has_side_effects=True, vmem_limit_bytes=56 * 1024 * 1024
        ),
    )(
        queries.transpose(1, 0, 2),
        key_rows.transpose(1, 0, 2),
        value_rows.transpose(1, 0, 2),
        keep_tiles,
        out_weight,
        gate_scale.reshape(1, -1),
    )


def solution(mesh):
    placed = (
        P(("groups", "tm"), "head", None),
        P(("groups", "tm"), "head", None),
        P(("groups", "tm"), "head", None),
        P(("groups", "tm"), None),
        P("head", "tm"),
        P(("groups", "head")),
    )
    n, heads = mesh.shape["tm"], mesh.shape["head"]
    body = chain_shards if n == 4 and n % heads == 0 and mesh.shape["groups"] > 1 else shards
    return jax.shard_map(
        body, mesh=mesh, in_specs=placed, out_specs=P(("groups", "tm"), "head"), check_vma=False
    )
```

```python
import functools
import math

import jax
import jax.numpy as jnp
from jax import lax
from jax.experimental import pallas as pl
from jax.experimental.pallas import tpu as pltpu
from jax.sharding import PartitionSpec as P

HD = 128
TILE = 128
MESH = pl.DeviceIdType.MESH


def layer_kernel(
    sizes, q_ref, k_ref, v_ref, keep_ref, w_ref, gate_ref, out_ref,
    q_own, k_all, v_all, w_all, attended, part, got,
    kv_send, kv_recv, z_send, z_recv, y_send, y_recv, r_send, r_recv, own_sem, in_sem,
):
    groups, n, heads, reach, pieces = sizes
    g, t, me = lax.axis_index("groups"), lax.axis_index("tm"), lax.axis_index("head")
    rows, cols = w_ref.shape
    wide = cols // pieces
    per_head = n // heads
    part_rows = rows // groups
    head_count, tokens = q_ref.shape[0], q_ref.shape[1]
    slabs = 2 * reach + 1

    barrier = pltpu.get_barrier_semaphore()
    partners = []
    for d in range(1, reach + 1):
        partners += [{"tm": lax.rem(t + d, n)}, {"tm": lax.rem(t + n - d, n)}]
    for o in range(1, groups):
        partners.append({"groups": lax.rem(g + o, groups)})
    for o in range(1, heads):
        partners.append({"head": lax.rem(me + o, heads)})
    for partner in partners:
        pl.semaphore_signal(barrier, inc=1, device_id=partner, device_id_type=MESH)
    pl.semaphore_wait(barrier, len(partners))

    def remote(src, dst, send, recv, device):
        return pltpu.make_async_remote_copy(
            src_ref=src, dst_ref=dst, send_sem=send, recv_sem=recv,
            device_id=device, device_id_type=MESH,
        )

    kv_copies = []
    for d in range(1, reach + 1):
        for slot, to in ((reach - d, lax.rem(t + d, n)), (reach + d, lax.rem(t + n - d, n))):
            for which, (src, dst) in enumerate(((k_ref, k_all), (v_ref, v_all))):
                kv_copies.append(
                    remote(src, dst.at[slot], kv_send.at[slot, which], kv_recv.at[slot, which], {"tm": to})
                )
    @pl.when(t == 0)
    def _():
        for copy in reversed(kv_copies):
            copy.start()

    @pl.when(t != 0)
    def _():
        for copy in kv_copies:
            copy.start()

    in_copies = [
        pltpu.make_async_copy(src, dst, in_sem.at[i])
        for i, (src, dst) in enumerate(
            ((q_ref, q_own), (k_ref, k_all.at[reach]), (v_ref, v_all.at[reach]))
        )
    ]
    for copy in in_copies:
        copy.start()

    my_rows = pl.ds(pl.multiple_of(g * part_rows, part_rows), part_rows)

    def own_copy(c):
        return pltpu.make_async_copy(
            w_ref.at[:, c * wide:(c + 1) * wide], w_all.at[t, c], own_sem.at[c]
        )

    def first_send(c, side):
        to = jnp.minimum(t + 1, n - 1) if side else jnp.maximum(t - 1, 0)
        return remote(
            w_ref.at[my_rows, c * wide:(c + 1) * wide], w_all.at[t, c, my_rows],
            z_send.at[side, t, c], z_recv.at[t, c], {"tm": to},
        )

    def relay(b, c, side):
        to = jnp.minimum(t + 1, n - 1) if side else jnp.maximum(t - 1, 0)
        return remote(
            w_all.at[b, c, my_rows], w_all.at[b, c, my_rows],
            z_send.at[side, b, c], z_recv.at[b, c], {"tm": to},
        )

    def across(b, c, o):
        return remote(
            w_all.at[b, c, my_rows], w_all.at[b, c, my_rows],
            y_send.at[o - 1, b, c], y_recv.at[o - 1, b, c],
            {"groups": lax.rem(g + o, groups)},
        )

    def across_arrival(b, c, o):
        sender = lax.rem(g + groups - o, groups)
        their_rows = pl.ds(pl.multiple_of(sender * part_rows, part_rows), part_rows)
        return remote(
            w_all.at[b, c, their_rows], w_all.at[b, c, their_rows],
            y_send.at[o - 1, b, c], y_recv.at[o - 1, b, c],
            {"groups": lax.rem(g + o, groups)},
        )

    def term_send(b, c, o):
        return remote(
            part.at[b, c], got.at[o - 1, b % per_head, c],
            r_send.at[b, c], r_recv.at[o - 1, b % per_head, c],
            {"head": lax.rem(me + o, heads)},
        )

    for c in range(pieces):
        own_copy(c).start()
        @pl.when(t < n - 1)
        def _(c=c):
            first_send(c, 1).start()
        @pl.when(t > 0)
        def _(c=c):
            first_send(c, 0).start()

    for copy in in_copies:
        copy.wait()
    for copy in kv_copies:
        copy.wait_recv()

    scale = 1.0 / math.sqrt(HD)
    per_slab = tokens // TILE

    early = min(pieces, head_count - 1)

    def pass_on(j, side):
        step, c = j // pieces, j % pieces
        b = (t - 1 - step) if side else (t + 1 + step)
        @pl.when((b >= 0) & (b <= n - 1))
        def _():
            relay(b, c, side).wait_recv()
            @pl.when((t < n - 1) if side else (t > 0))
            def _():
                relay(b, c, side).start()
            for o in range(1, groups):
                across(b, c, o).start()

    def one_head(h, carry):
        lanes = pl.ds(pl.multiple_of(h * HD, HD), HD)
        for i in range(per_slab):
            q = q_own[h, i * TILE:(i + 1) * TILE, :]
            scores = []
            for j in range(slabs):
                s = lax.dot_general(
                    q, k_all[j, h], (((1,), (1,)), ((), ())), preferred_element_type=jnp.float32
                )
                bias = jnp.concatenate(
                    [
                        jnp.full(
                            (1, TILE),
                            jnp.where(keep_ref[i, j * per_slab + u] > 0, 0.0, -jnp.inf),
                            jnp.float32,
                        )
                        for u in range(per_slab)
                    ],
                    axis=1,
                )
                scores.append(s * scale + bias)
            peak = functools.reduce(
                jnp.maximum, [jnp.max(s, axis=1, keepdims=True) for s in scores]
            )
            exps = [jnp.exp(s - peak) for s in scores]
            total = functools.reduce(jnp.add, [jnp.sum(e, axis=1, keepdims=True) for e in exps])
            inverse = 1.0 / total
            acc = None
            for j in range(slabs):
                term = jnp.dot(
                    (exps[j] * inverse).astype(jnp.bfloat16), v_all[j, h],
                    preferred_element_type=jnp.float32,
                )
                acc = term if acc is None else acc + term
            attended[i * TILE:(i + 1) * TILE, lanes] = acc.astype(jnp.bfloat16)
        @pl.when(h >= head_count - early)
        def _():
            for side in (1, 0):
                pass_on(h - (head_count - early), side)
        return carry

    lax.fori_loop(0, head_count, one_head, 0)

    def project(b, c):
        def tile(i, carry):
            at = pl.ds(pl.multiple_of(i * TILE, TILE), TILE)
            part[b, c, at, :] = jnp.dot(
                attended[at, :], w_all[b, c], preferred_element_type=jnp.float32
            ).astype(jnp.bfloat16)
            return carry

        lax.fori_loop(0, tokens // TILE, tile, 0)
        owner = b // per_head
        for o in range(1, heads):
            @pl.when(owner == lax.rem(me + o, heads))
            def _():
                term_send(b, c, o).start()

    for c in range(pieces):
        own_copy(c).wait()
        project(t, c)

    def use(j, side):
        step, c = j // pieces, j % pieces
        b = (t - 1 - step) if side else (t + 1 + step)
        @pl.when((b >= 0) & (b <= n - 1))
        def _():
            for o in range(1, groups):
                across_arrival(b, c, o).wait_recv()
            project(b, c)

    count = (n - 1) * pieces

    def use_both(j, carry):
        for side in (1, 0):
            use(j, side)
        return carry

    def step(j, carry):
        for side in (1, 0):
            pass_on(j, side)
        first = jnp.minimum(2 * (j - early), j - 1)
        last = jnp.minimum(2 * (j - early) + 2, j)
        return lax.fori_loop(first, last, use_both, carry)

    lax.fori_loop(early, count, step, 0)
    lax.fori_loop(min(2 * (count - early), count - 1), count, use_both, 0)

    for cb in range(per_head):
        for c in range(pieces):
            b = me * per_head + cb
            for o in range(1, heads):
                term_send(b, c, o).wait_recv()
            span = wide if gate_ref.shape[0] == 1 else gate_ref.shape[1]
            for u in range(wide // span):
                lanes = slice(u * span, (u + 1) * span)
                summed = part[b, c, :, lanes].astype(jnp.float32)
                for o in range(1, heads):
                    summed = summed + got[o - 1, cb, c, :, lanes].astype(jnp.float32)
                at = cb * cols + c * wide + u * span
                gate = gate_ref[:, at:at + span] if span == wide else gate_ref[at // span:at // span + 1, :]
                out_ref[:, at:at + span] = (gate * summed).astype(out_ref.dtype)

    for copy in kv_copies:
        copy.wait_send()
    for c in range(pieces):
        @pl.when(t < n - 1)
        def _(c=c):
            first_send(c, 1).wait_send()
        @pl.when(t > 0)
        def _(c=c):
            first_send(c, 0).wait_send()

    def drain(b, carry):
        for c in range(pieces):
            @pl.when(b != t)
            def _(c=c):
                for o in range(1, groups):
                    across(b, c, o).wait_send()
            @pl.when((b < t) & (t < n - 1))
            def _(c=c):
                relay(b, c, 1).wait_send()
            @pl.when((b > t) & (t > 0))
            def _(c=c):
                relay(b, c, 0).wait_send()
            @pl.when(b // per_head != me)
            def _(c=c):
                term_send(b, c, 1).wait_send()
        return carry

    lax.fori_loop(0, n, drain, 0)


def shards(queries, key_rows, value_rows, keep_tiles, out_weight, gate_scale):
    n, heads, groups = lax.axis_size("tm"), lax.axis_size("head"), lax.axis_size("groups")
    reach = min(2, (n - 1) // 2)
    tokens = queries.shape[0]
    head_count = queries.shape[1]
    flat = head_count * HD
    rows, cols = out_weight.shape
    pieces = cols // 256 if cols % 256 == 0 else 1
    wide = cols // pieces
    per_head = n // heads
    slabs = 2 * reach + 1
    gate_lanes = 128 if wide % 128 == 0 else gate_scale.shape[0]
    vmem = pl.BlockSpec(memory_space=pltpu.VMEM)
    hbm = pl.BlockSpec(memory_space=pl.ANY)
    dma = pltpu.SemaphoreType.DMA
    bf16 = jnp.bfloat16
    return pl.pallas_call(
        functools.partial(layer_kernel, (groups, n, heads, reach, pieces)),
        out_shape=jax.ShapeDtypeStruct((tokens, gate_scale.shape[0]), bf16),
        in_specs=[hbm, hbm, hbm, pl.BlockSpec(memory_space=pltpu.SMEM), hbm, vmem],
        out_specs=vmem,
        scratch_shapes=[
            pltpu.VMEM((head_count, tokens, HD), bf16),
            pltpu.VMEM((slabs, head_count, tokens, HD), bf16),
            pltpu.VMEM((slabs, head_count, tokens, HD), bf16),
            pltpu.VMEM((n, pieces, rows, wide), bf16),
            pltpu.VMEM((tokens, flat), bf16),
            pltpu.VMEM((n, pieces, tokens, wide), bf16),
            pltpu.VMEM((heads - 1, per_head, pieces, tokens, wide), bf16),
            dma((slabs, 2)),
            dma((slabs, 2)),
            dma((2, n, pieces)),
            dma((n, pieces)),
            dma((groups - 1, n, pieces)),
            dma((groups - 1, n, pieces)),
            dma((n, pieces)),
            dma((heads - 1, per_head, pieces)),
            dma((pieces,)),
            dma((3,)),
        ],
        compiler_params=pltpu.CompilerParams(
            collective_id=0, has_side_effects=True, vmem_limit_bytes=56 * 1024 * 1024
        ),
    )(
        queries.transpose(1, 0, 2),
        key_rows.transpose(1, 0, 2),
        value_rows.transpose(1, 0, 2),
        keep_tiles,
        out_weight,
        gate_scale.reshape(-1, gate_lanes),
    )


def chain_kernel(
    sizes, q_ref, k_ref, v_ref, keep_ref, w_ref, gate_ref, out_ref,
    q_own, q_far, k_all, v_all, w_all, attended, far_att, part, got, pair, keep_far, bias,
    kv_send, kv_recv, q_send, q_recv, keep_sem, att_send, att_recv,
    z_send, z_recv, y_send, y_recv, r_send, r_recv, pair_recv, own_sem, in_sem,
):
    groups, n, heads, pieces = sizes
    g, t, me = lax.axis_index("groups"), lax.axis_index("tm"), lax.axis_index("head")
    rows, cols = w_ref.shape
    wide = cols // pieces
    per_head = n // heads
    part_rows = rows // groups
    head_count, tokens = q_ref.shape[0], q_ref.shape[1]
    per_slab = tokens // TILE
    total_pieces = n * pieces
    chips = heads // 2
    my_chip, my_core = me // 2, lax.rem(me, 2)
    partner = me + 1 - 2 * my_core

    left = t < n // 2
    inner = (t > 0) & (t < n - 1)
    outer = jnp.logical_not(inner)
    end = jnp.where(left, 0, n - 1)
    near = jnp.where(left, 1, n - 2)
    across_mid = n - 1 - t
    far_end = n - 1 - end
    mate = jnp.where(inner, end, near)
    mate_id = {"tm": mate}
    mid_id = {"tm": across_mid}

    barrier = pltpu.get_barrier_semaphore()

    def greet(partner):
        pl.semaphore_signal(barrier, inc=1, device_id=partner, device_id_type=MESH)

    greet(mate_id)
    @pl.when(inner)
    def _():
        greet(mid_id)
    for o in range(1, groups):
        greet({"groups": lax.rem(g + o, groups)})
    for o in range(1, heads):
        greet({"head": lax.rem(me + o, heads)})
    @pl.when(inner)
    def _():
        pl.semaphore_wait(barrier, groups + heads)
    @pl.when(outer)
    def _():
        pl.semaphore_wait(barrier, groups + heads - 1)

    def remote(src, dst, send, recv, device):
        return pltpu.make_async_remote_copy(
            src_ref=src, dst_ref=dst, send_sem=send, recv_sem=recv,
            device_id=device, device_id_type=MESH,
        )

    kv = ((k_ref, k_all), (v_ref, v_all))

    def kv_first(h, which, device):
        src, dst = kv[which]
        return remote(
            src.at[h], dst.at[t, h], kv_send.at[0, which, h], kv_recv.at[t, which, h], device
        )

    def kv_relay(h, which):
        buf = kv[which][1]
        return remote(
            buf.at[end, h], buf.at[end, h], kv_send.at[1, which, h], kv_recv.at[end, which, h],
            mid_id,
        )

    def kv_arrival(slab, h, which):
        buf = kv[which][1]
        return remote(
            buf.at[slab, h], buf.at[slab, h], kv_send.at[1, which, h],
            kv_recv.at[slab, which, h], mid_id,
        )

    def q_copy(h):
        return remote(q_ref.at[h], q_far.at[h], q_send.at[h], q_recv.at[h], mate_id)

    keep_copy = remote(keep_ref, keep_far, keep_sem.at[0], keep_sem.at[1], mate_id)

    def lanes_of(h):
        return pl.ds(pl.multiple_of(h * HD, HD), HD)

    def att_copy(h):
        return remote(
            far_att.at[:, lanes_of(h)], attended.at[:, lanes_of(h)],
            att_send.at[h], att_recv.at[h], mate_id,
        )

    my_rows = pl.ds(pl.multiple_of(g * part_rows, part_rows), part_rows)

    def own_copy(c):
        return pltpu.make_async_copy(
            w_ref.at[:, c * wide:(c + 1) * wide], w_all.at[t, c], own_sem.at[c]
        )

    def first_send(c, way):
        return remote(
            w_ref.at[my_rows, c * wide:(c + 1) * wide], w_all.at[t, c, my_rows],
            z_send.at[way, t, c], z_recv.at[t, c], mid_id if way else mate_id,
        )

    def rows_of(sender):
        return pl.ds(pl.multiple_of(sender * part_rows, part_rows), part_rows)

    def rest_send(c, o):
        theirs = rows_of(lax.rem(g + groups - o, groups))
        return remote(
            w_ref.at[theirs, c * wide:(c + 1) * wide], w_all.at[t, c, theirs],
            y_send.at[o - 1, t, c], y_recv.at[o - 1, t, c], mate_id,
        )

    def relay(b, c, way):
        return remote(
            w_all.at[b, c, my_rows], w_all.at[b, c, my_rows],
            z_send.at[way, b, c], z_recv.at[b, c], mid_id if way else mate_id,
        )

    def across(b, c, o):
        return remote(
            w_all.at[b, c, my_rows], w_all.at[b, c, my_rows],
            y_send.at[o - 1, b, c], y_recv.at[o - 1, b, c],
            {"groups": lax.rem(g + o, groups)},
        )

    def across_arrival(b, c, o):
        sender = lax.rem(g + groups - o, groups)
        their_rows = pl.ds(pl.multiple_of(sender * part_rows, part_rows), part_rows)
        return remote(
            w_all.at[b, c, their_rows], w_all.at[b, c, their_rows],
            y_send.at[o - 1, b, c], y_recv.at[o - 1, b, c],
            {"groups": lax.rem(g + o, groups)},
        )

    def partner_send(b, c):
        at = lax.rem(b, per_head)
        return remote(
            part.at[b, c], got.at[0, at, c], r_send.at[b, c], r_recv.at[0, at, c],
            {"head": partner},
        )

    def give_send(b, c):
        owner, at = b // per_head, lax.rem(b, per_head)
        return remote(
            part.at[b, c], pair.at[owner // 2, at, c], r_send.at[b, c],
            pair_recv.at[owner // 2, at, c], {"head": partner},
        )

    def sum_send(b, c):
        owner, at = b // per_head, lax.rem(b, per_head)
        slot = lax.rem(my_chip - owner // 2 + chips, chips)
        return remote(
            part.at[b, c], got.at[slot, at, c], r_send.at[b, c], r_recv.at[slot, at, c],
            {"head": owner},
        )

    def term_arrival(b, c, slot):
        at = lax.rem(b, per_head)
        return remote(
            part.at[b, c], got.at[slot, at, c], r_send.at[b, c], r_recv.at[slot, at, c],
            {"head": partner},
        )

    in_copies = [
        pltpu.make_async_copy(src, dst, in_sem.at[i])
        for i, (src, dst) in enumerate(
            ((q_ref, q_own), (k_ref, k_all.at[t]), (v_ref, v_all.at[t]))
        )
    ]

    @pl.when(outer)
    def _():
        for h in range(head_count):
            for which in range(2):
                kv_first(h, which, mate_id).start()
        keep_copy.start()
        for h in range(head_count):
            q_copy(h).start()

    @pl.when(inner)
    def _():
        for h in range(head_count):
            for which in range(2):
                kv_first(h, which, mid_id).start()
        for copy in in_copies:
            copy.start()

    for c in range(pieces):
        first_send(c, 0).start()
    @pl.when(outer)
    def _():
        for c in range(pieces):
            for o in range(1, groups):
                rest_send(c, o).start()
    for c in range(pieces):
        own_copy(c).start()

    def block_of(k):
        place = jnp.where(left, t, n - 1 - t)
        b = jnp.where(k == 0, place, jnp.where(k == 1, 1 - place, k))
        return jnp.where(left, b, n - 1 - b)

    def pass_on(j):
        b, c = block_of(j // pieces), lax.rem(j, pieces)
        relay(b, c, 0).wait_recv()
        @pl.when(inner & (b == end))
        def _():
            relay(b, c, 1).start()
        @pl.when(inner & (b != end))
        def _():
            relay(b, c, 0).start()
        @pl.when(outer | (b != end))
        def _():
            for o in range(1, groups):
                across(b, c, o).start()

    scale = math.log2(math.e) / math.sqrt(HD)
    reach_slabs = keep_ref.shape[1] // per_slab

    def set_bias(at, ref):
        kept = ref[...]
        spread = jnp.concatenate(
            [jnp.broadcast_to(kept[:, c:c + 1], (per_slab, TILE)) for c in range(kept.shape[1])],
            axis=1,
        )
        bias[at] = jnp.where(spread > 0, 0.0, -jnp.inf).astype(jnp.float32)

    def attend(h, slab, queries, at, dst):
        for i in range(per_slab):
            q = queries[h, i * TILE:(i + 1) * TILE, :]
            scores = []
            for j in range(reach_slabs):
                other = lax.rem(slab + j - reach_slabs // 2 + n, n)
                s = lax.dot_general(
                    q, k_all[other, h], (((1,), (1,)), ((), ())),
                    preferred_element_type=jnp.float32,
                )
                scores.append(s * scale + bias[at, i:i + 1, j * tokens:(j + 1) * tokens])
            peak = functools.reduce(
                jnp.maximum, [jnp.max(s, axis=1, keepdims=True) for s in scores]
            )
            exps = [jnp.exp2(s - peak) for s in scores]
            total = functools.reduce(jnp.add, [jnp.sum(e, axis=1, keepdims=True) for e in exps])
            acc = None
            for j in range(reach_slabs):
                other = lax.rem(slab + j - reach_slabs // 2 + n, n)
                term = jnp.dot(
                    exps[j].astype(jnp.bfloat16), v_all[other, h],
                    preferred_element_type=jnp.float32,
                )
                acc = term if acc is None else acc + term
            dst[i * TILE:(i + 1) * TILE, lanes_of(h)] = (acc * (1.0 / total)).astype(jnp.bfloat16)

    def project(b, c):
        def tile(i, carry):
            at = pl.ds(pl.multiple_of(i * TILE, TILE), TILE)
            part[b, c, at, :] = jnp.dot(
                attended[at, :], w_all[b, c], preferred_element_type=jnp.float32
            ).astype(jnp.bfloat16)
            return carry

        lax.fori_loop(0, tokens // TILE, tile, 0)
        owner = b // per_head
        @pl.when(owner == partner)
        def _():
            partner_send(b, c).start()
        @pl.when((owner // 2 != my_chip) & (lax.rem(owner, 2) != my_core))
        def _():
            give_send(b, c).start()

    def collect(j):
        b, c = block_of(j // pieces), lax.rem(j, pieces)
        owner, at = b // per_head, lax.rem(b, per_head)
        @pl.when((owner // 2 != my_chip) & (lax.rem(owner, 2) == my_core))
        def _():
            give_send(b, c).wait_recv()

            def tile(i, carry):
                now = pl.ds(pl.multiple_of(i * TILE, TILE), TILE)
                part[b, c, now, :] = (
                    part[b, c, now, :].astype(jnp.float32)
                    + pair[owner // 2, at, c, now, :].astype(jnp.float32)
                ).astype(jnp.bfloat16)
                return carry

            lax.fori_loop(0, tokens // TILE, tile, 0)
            sum_send(b, c).start()

    def use(j):
        b, c = block_of(j // pieces), lax.rem(j, pieces)
        for o in range(1, groups):
            across_arrival(b, c, o).wait_recv()
        project(b, c)

    def finish(j):
        b, c = block_of(j // pieces), lax.rem(j, pieces)
        cb = lax.rem(b, per_head)
        @pl.when(b // per_head == me)
        def _():
            for slot in range(chips):
                term_arrival(b, c, slot).wait_recv()
            span = gate_ref.shape[1]
            for u in range(wide // span):
                lanes = slice(u * span, (u + 1) * span)
                summed = part[b, c, :, lanes].astype(jnp.float32)
                for slot in range(chips):
                    summed = summed + got[slot, cb, c, :, lanes].astype(jnp.float32)
                block = cb * (cols // span) + c * (wide // span) + u
                at = pl.ds(pl.multiple_of(block * span, span), span)
                out_ref[:, at] = (gate_ref[pl.ds(block, 1), :] * summed).astype(out_ref.dtype)

    def do_use(j, carry):
        use(j)
        collect(j - 1)
        return carry

    def use_last(j, carry):
        use(j)
        collect(j)
        return carry

    def do_finish(j, carry):
        finish(j)
        return carry

    def own_block(c, carry):
        project(t, c)
        @pl.when(c > 0)
        def _():
            collect(c - 1)
        return carry

    @pl.when(inner)
    def _():
        set_bias(0, keep_ref)
        for copy in in_copies:
            copy.wait()

        def own_slab(h, carry):
            for which in range(2):
                kv_arrival(end, h, which).wait_recv()
                kv_relay(h, which).start()
            for which in range(2):
                kv_arrival(across_mid, h, which).wait_recv()
            attend(h, t, q_own, 0, attended)
            return carry

        lax.fori_loop(0, head_count, own_slab, 0)
        for c in range(pieces):
            first_send(c, 1).start()
        for c in range(pieces):
            own_copy(c).wait()
        lax.fori_loop(0, pieces, own_block, 0)
        keep_copy.wait_recv()
        set_bias(1, keep_far)

        def end_slab(h, carry):
            q_copy(h).wait_recv()
            for which in range(2):
                kv_arrival(far_end, h, which).wait_recv()
            attend(h, end, q_far, 1, far_att)
            att_copy(h).start()
            return carry

        lax.fori_loop(0, head_count, end_slab, 0)

    def early_pass(j, carry):
        pass_on(j)
        return carry

    lax.fori_loop(pieces, 2 * pieces, early_pass, 0)

    @pl.when(outer)
    def _():
        for c in range(pieces):
            own_copy(c).wait()
        for h in range(head_count):
            att_copy(h).wait_recv()
        lax.fori_loop(0, pieces, own_block, 0)

    @pl.when(outer)
    def _():
        lax.fori_loop(pieces, 2 * pieces, do_use, 0)

    def used_by(j):
        lagging = jnp.maximum(jnp.maximum(j - pieces - 1, 2 * j - 4 * pieces), pieces)
        return jnp.where(inner, jnp.minimum(lagging, j - 1), jnp.maximum(j - 2, 2 * pieces))

    def step(j, carry):
        pass_on(j)
        return lax.fori_loop(used_by(j - 1), used_by(j), do_use, carry)

    lax.fori_loop(2 * pieces, total_pieces, step, 0)
    lax.fori_loop(0, pieces, do_finish, 0)
    ready = used_by(total_pieces - 1)
    collect(ready - 1)
    lax.fori_loop(ready, total_pieces, use_last, 0)
    lax.fori_loop(pieces, total_pieces, do_finish, 0)

    @pl.when(outer)
    def _():
        for h in range(head_count):
            for which in range(2):
                kv_first(h, which, mate_id).wait_send()
            q_copy(h).wait_send()
        keep_copy.wait_send()

    @pl.when(inner)
    def _():
        for h in range(head_count):
            for which in range(2):
                kv_first(h, which, mid_id).wait_send()
                kv_relay(h, which).wait_send()
            att_copy(h).wait_send()
        for c in range(pieces):
            first_send(c, 1).wait_send()

    def drain(b, carry):
        for c in range(pieces):
            @pl.when(b == t)
            def _(c=c):
                first_send(c, 0).wait_send()
            @pl.when((b == t) & outer)
            def _(c=c):
                for o in range(1, groups):
                    rest_send(c, o).wait_send()
            @pl.when((b != t) & (outer | (b != end)))
            def _(c=c):
                for o in range(1, groups):
                    across(b, c, o).wait_send()
            @pl.when(inner & (b == end))
            def _(c=c):
                relay(b, c, 1).wait_send()
            @pl.when(inner & (b != end) & (b != t))
            def _(c=c):
                relay(b, c, 0).wait_send()
            @pl.when(b // per_head != me)
            def _(c=c):
                partner_send(b, c).wait_send()
        return carry

    lax.fori_loop(0, n, drain, 0)


def chain_shards(queries, key_rows, value_rows, keep_tiles, out_weight, gate_scale):
    n, heads, groups = lax.axis_size("tm"), lax.axis_size("head"), lax.axis_size("groups")
    tokens = queries.shape[0]
    head_count = queries.shape[1]
    flat = head_count * HD
    rows, cols = out_weight.shape
    pieces = cols // 256 if cols % 256 == 0 else 1
    wide = cols // pieces
    per_head = n // heads
    gate_lanes = 128 if wide % 128 == 0 else wide
    vmem = pl.BlockSpec(memory_space=pltpu.VMEM)
    hbm = pl.BlockSpec(memory_space=pl.ANY)
    dma = pltpu.SemaphoreType.DMA
    bf16 = jnp.bfloat16
    return pl.pallas_call(
        functools.partial(chain_kernel, (groups, n, heads, pieces)),
        out_shape=jax.ShapeDtypeStruct((tokens, gate_scale.shape[0]), bf16),
        in_specs=[hbm, hbm, hbm, vmem, hbm, vmem],
        out_specs=vmem,
        scratch_shapes=[
            pltpu.VMEM((head_count, tokens, HD), bf16),
            pltpu.VMEM((head_count, tokens, HD), bf16),
            pltpu.VMEM((n, head_count, tokens, HD), bf16),
            pltpu.VMEM((n, head_count, tokens, HD), bf16),
            pltpu.VMEM((n, pieces, rows, wide), bf16),
            pltpu.VMEM((tokens, flat), bf16),
            pltpu.VMEM((tokens, flat), bf16),
            pltpu.VMEM((n, pieces, tokens, wide), bf16),
            pltpu.VMEM((heads // 2, per_head, pieces, tokens, wide), bf16),
            pltpu.VMEM((heads // 2, per_head, pieces, tokens, wide), bf16),
            pltpu.VMEM(keep_tiles.shape, jnp.int32),
            pltpu.VMEM((2, keep_tiles.shape[0], keep_tiles.shape[1] * TILE), jnp.float32),
            dma((2, 2, head_count)),
            dma((n, 2, head_count)),
            dma((head_count,)),
            dma((head_count,)),
            dma((2,)),
            dma((head_count,)),
            dma((head_count,)),
            dma((2, n, pieces)),
            dma((n, pieces)),
            dma((groups - 1, n, pieces)),
            dma((groups - 1, n, pieces)),
            dma((n, pieces)),
            dma((heads // 2, per_head, pieces)),
            dma((heads // 2, per_head, pieces)),
            dma((pieces,)),
            dma((3,)),
        ],
        compiler_params=pltpu.CompilerParams(
            collective_id=0, has_side_effects=True, vmem_limit_bytes=56 * 1024 * 1024
        ),
    )(
        queries.transpose(1, 0, 2),
        key_rows.transpose(1, 0, 2),
        value_rows.transpose(1, 0, 2),
        keep_tiles,
        out_weight,
        gate_scale.reshape(-1, gate_lanes),
    )


def solution(mesh):
    placed = (
        P(("groups", "tm"), "head", None),
        P(("groups", "tm"), "head", None),
        P(("groups", "tm"), "head", None),
        P(("groups", "tm"), None),
        P("head", "tm"),
        P(("groups", "head")),
    )
    n, heads = mesh.shape["tm"], mesh.shape["head"]
    chain = n == 4 and n % heads == 0 and heads % 2 == 0 and mesh.shape["groups"] > 1
    body = chain_shards if chain else shards
    return jax.shard_map(
        body, mesh=mesh, in_specs=placed, out_specs=P(("groups", "tm"), "head"), check_vma=False
    )
```

```python
import functools
import math

import jax
import jax.numpy as jnp
from jax import lax
from jax.experimental import pallas as pl
from jax.experimental.pallas import tpu as pltpu
from jax.sharding import PartitionSpec as P

HD = 128
TILE = 128
MESH = pl.DeviceIdType.MESH


def layer_kernel(
    sizes, q_ref, k_ref, v_ref, keep_ref, w_ref, gate_ref, out_ref,
    q_own, k_all, v_all, w_all, attended, part, got,
    kv_send, kv_recv, z_send, z_recv, y_send, y_recv, r_send, r_recv, own_sem, in_sem,
):
    groups, n, heads, reach, pieces = sizes
    g, t, me = lax.axis_index("groups"), lax.axis_index("tm"), lax.axis_index("head")
    rows, cols = w_ref.shape
    wide = cols // pieces
    per_head = n // heads
    part_rows = rows // groups
    head_count, tokens = q_ref.shape[0], q_ref.shape[1]
    slabs = 2 * reach + 1

    barrier = pltpu.get_barrier_semaphore()
    partners = []
    for d in range(1, reach + 1):
        partners += [{"tm": lax.rem(t + d, n)}, {"tm": lax.rem(t + n - d, n)}]
    for o in range(1, groups):
        partners.append({"groups": lax.rem(g + o, groups)})
    for o in range(1, heads):
        partners.append({"head": lax.rem(me + o, heads)})
    for partner in partners:
        pl.semaphore_signal(barrier, inc=1, device_id=partner, device_id_type=MESH)
    pl.semaphore_wait(barrier, len(partners))

    def remote(src, dst, send, recv, device):
        return pltpu.make_async_remote_copy(
            src_ref=src, dst_ref=dst, send_sem=send, recv_sem=recv,
            device_id=device, device_id_type=MESH,
        )

    kv_copies = []
    for d in range(1, reach + 1):
        for slot, to in ((reach - d, lax.rem(t + d, n)), (reach + d, lax.rem(t + n - d, n))):
            for which, (src, dst) in enumerate(((k_ref, k_all), (v_ref, v_all))):
                kv_copies.append(
                    remote(src, dst.at[slot], kv_send.at[slot, which], kv_recv.at[slot, which], {"tm": to})
                )
    @pl.when(t == 0)
    def _():
        for copy in reversed(kv_copies):
            copy.start()

    @pl.when(t != 0)
    def _():
        for copy in kv_copies:
            copy.start()

    in_copies = [
        pltpu.make_async_copy(src, dst, in_sem.at[i])
        for i, (src, dst) in enumerate(
            ((q_ref, q_own), (k_ref, k_all.at[reach]), (v_ref, v_all.at[reach]))
        )
    ]
    for copy in in_copies:
        copy.start()

    my_rows = pl.ds(pl.multiple_of(g * part_rows, part_rows), part_rows)

    def own_copy(c):
        return pltpu.make_async_copy(
            w_ref.at[:, c * wide:(c + 1) * wide], w_all.at[t, c], own_sem.at[c]
        )

    def first_send(c, side):
        to = jnp.minimum(t + 1, n - 1) if side else jnp.maximum(t - 1, 0)
        return remote(
            w_ref.at[my_rows, c * wide:(c + 1) * wide], w_all.at[t, c, my_rows],
            z_send.at[side, t, c], z_recv.at[t, c], {"tm": to},
        )

    def relay(b, c, side):
        to = jnp.minimum(t + 1, n - 1) if side else jnp.maximum(t - 1, 0)
        return remote(
            w_all.at[b, c, my_rows], w_all.at[b, c, my_rows],
            z_send.at[side, b, c], z_recv.at[b, c], {"tm": to},
        )

    def across(b, c, o):
        return remote(
            w_all.at[b, c, my_rows], w_all.at[b, c, my_rows],
            y_send.at[o - 1, b, c], y_recv.at[o - 1, b, c],
            {"groups": lax.rem(g + o, groups)},
        )

    def across_arrival(b, c, o):
        sender = lax.rem(g + groups - o, groups)
        their_rows = pl.ds(pl.multiple_of(sender * part_rows, part_rows), part_rows)
        return remote(
            w_all.at[b, c, their_rows], w_all.at[b, c, their_rows],
            y_send.at[o - 1, b, c], y_recv.at[o - 1, b, c],
            {"groups": lax.rem(g + o, groups)},
        )

    def term_send(b, c, o):
        return remote(
            part.at[b, c], got.at[o - 1, b % per_head, c],
            r_send.at[b, c], r_recv.at[o - 1, b % per_head, c],
            {"head": lax.rem(me + o, heads)},
        )

    for c in range(pieces):
        own_copy(c).start()
        @pl.when(t < n - 1)
        def _(c=c):
            first_send(c, 1).start()
        @pl.when(t > 0)
        def _(c=c):
            first_send(c, 0).start()

    for copy in in_copies:
        copy.wait()
    for copy in kv_copies:
        copy.wait_recv()

    scale = 1.0 / math.sqrt(HD)
    per_slab = tokens // TILE

    early = min(pieces, head_count - 1)

    def pass_on(j, side):
        step, c = j // pieces, j % pieces
        b = (t - 1 - step) if side else (t + 1 + step)
        @pl.when((b >= 0) & (b <= n - 1))
        def _():
            relay(b, c, side).wait_recv()
            @pl.when((t < n - 1) if side else (t > 0))
            def _():
                relay(b, c, side).start()
            for o in range(1, groups):
                across(b, c, o).start()

    def one_head(h, carry):
        lanes = pl.ds(pl.multiple_of(h * HD, HD), HD)
        for i in range(per_slab):
            q = q_own[h, i * TILE:(i + 1) * TILE, :]
            scores = []
            for j in range(slabs):
                s = lax.dot_general(
                    q, k_all[j, h], (((1,), (1,)), ((), ())), preferred_element_type=jnp.float32
                )
                bias = jnp.concatenate(
                    [
                        jnp.full(
                            (1, TILE),
                            jnp.where(keep_ref[i, j * per_slab + u] > 0, 0.0, -jnp.inf),
                            jnp.float32,
                        )
                        for u in range(per_slab)
                    ],
                    axis=1,
                )
                scores.append(s * scale + bias)
            peak = functools.reduce(
                jnp.maximum, [jnp.max(s, axis=1, keepdims=True) for s in scores]
            )
            exps = [jnp.exp(s - peak) for s in scores]
            total = functools.reduce(jnp.add, [jnp.sum(e, axis=1, keepdims=True) for e in exps])
            inverse = 1.0 / total
            acc = None
            for j in range(slabs):
                term = jnp.dot(
                    (exps[j] * inverse).astype(jnp.bfloat16), v_all[j, h],
                    preferred_element_type=jnp.float32,
                )
                acc = term if acc is None else acc + term
            attended[i * TILE:(i + 1) * TILE, lanes] = acc.astype(jnp.bfloat16)
        @pl.when(h >= head_count - early)
        def _():
            for side in (1, 0):
                pass_on(h - (head_count - early), side)
        return carry

    lax.fori_loop(0, head_count, one_head, 0)

    def project(b, c):
        def tile(i, carry):
            at = pl.ds(pl.multiple_of(i * TILE, TILE), TILE)
            part[b, c, at, :] = jnp.dot(
                attended[at, :], w_all[b, c], preferred_element_type=jnp.float32
            ).astype(jnp.bfloat16)
            return carry

        lax.fori_loop(0, tokens // TILE, tile, 0)
        owner = b // per_head
        for o in range(1, heads):
            @pl.when(owner == lax.rem(me + o, heads))
            def _():
                term_send(b, c, o).start()

    for c in range(pieces):
        own_copy(c).wait()
        project(t, c)

    def use(j, side):
        step, c = j // pieces, j % pieces
        b = (t - 1 - step) if side else (t + 1 + step)
        @pl.when((b >= 0) & (b <= n - 1))
        def _():
            for o in range(1, groups):
                across_arrival(b, c, o).wait_recv()
            project(b, c)

    count = (n - 1) * pieces

    def use_both(j, carry):
        for side in (1, 0):
            use(j, side)
        return carry

    def step(j, carry):
        for side in (1, 0):
            pass_on(j, side)
        first = jnp.minimum(2 * (j - early), j - 1)
        last = jnp.minimum(2 * (j - early) + 2, j)
        return lax.fori_loop(first, last, use_both, carry)

    lax.fori_loop(early, count, step, 0)
    lax.fori_loop(min(2 * (count - early), count - 1), count, use_both, 0)

    for cb in range(per_head):
        for c in range(pieces):
            b = me * per_head + cb
            for o in range(1, heads):
                term_send(b, c, o).wait_recv()
            span = wide if gate_ref.shape[0] == 1 else gate_ref.shape[1]
            for u in range(wide // span):
                lanes = slice(u * span, (u + 1) * span)
                summed = part[b, c, :, lanes].astype(jnp.float32)
                for o in range(1, heads):
                    summed = summed + got[o - 1, cb, c, :, lanes].astype(jnp.float32)
                at = cb * cols + c * wide + u * span
                gate = gate_ref[:, at:at + span] if span == wide else gate_ref[at // span:at // span + 1, :]
                out_ref[:, at:at + span] = (gate * summed).astype(out_ref.dtype)

    for copy in kv_copies:
        copy.wait_send()
    for c in range(pieces):
        @pl.when(t < n - 1)
        def _(c=c):
            first_send(c, 1).wait_send()
        @pl.when(t > 0)
        def _(c=c):
            first_send(c, 0).wait_send()

    def drain(b, carry):
        for c in range(pieces):
            @pl.when(b != t)
            def _(c=c):
                for o in range(1, groups):
                    across(b, c, o).wait_send()
            @pl.when((b < t) & (t < n - 1))
            def _(c=c):
                relay(b, c, 1).wait_send()
            @pl.when((b > t) & (t > 0))
            def _(c=c):
                relay(b, c, 0).wait_send()
            @pl.when(b // per_head != me)
            def _(c=c):
                term_send(b, c, 1).wait_send()
        return carry

    lax.fori_loop(0, n, drain, 0)


def shards(queries, key_rows, value_rows, keep_tiles, out_weight, gate_scale):
    n, heads, groups = lax.axis_size("tm"), lax.axis_size("head"), lax.axis_size("groups")
    reach = min(2, (n - 1) // 2)
    tokens = queries.shape[0]
    head_count = queries.shape[1]
    flat = head_count * HD
    rows, cols = out_weight.shape
    pieces = cols // 256 if cols % 256 == 0 else 1
    wide = cols // pieces
    per_head = n // heads
    slabs = 2 * reach + 1
    gate_lanes = 128 if wide % 128 == 0 else gate_scale.shape[0]
    vmem = pl.BlockSpec(memory_space=pltpu.VMEM)
    hbm = pl.BlockSpec(memory_space=pl.ANY)
    dma = pltpu.SemaphoreType.DMA
    bf16 = jnp.bfloat16
    return pl.pallas_call(
        functools.partial(layer_kernel, (groups, n, heads, reach, pieces)),
        out_shape=jax.ShapeDtypeStruct((tokens, gate_scale.shape[0]), bf16),
        in_specs=[hbm, hbm, hbm, pl.BlockSpec(memory_space=pltpu.SMEM), hbm, vmem],
        out_specs=vmem,
        scratch_shapes=[
            pltpu.VMEM((head_count, tokens, HD), bf16),
            pltpu.VMEM((slabs, head_count, tokens, HD), bf16),
            pltpu.VMEM((slabs, head_count, tokens, HD), bf16),
            pltpu.VMEM((n, pieces, rows, wide), bf16),
            pltpu.VMEM((tokens, flat), bf16),
            pltpu.VMEM((n, pieces, tokens, wide), bf16),
            pltpu.VMEM((heads - 1, per_head, pieces, tokens, wide), bf16),
            dma((slabs, 2)),
            dma((slabs, 2)),
            dma((2, n, pieces)),
            dma((n, pieces)),
            dma((groups - 1, n, pieces)),
            dma((groups - 1, n, pieces)),
            dma((n, pieces)),
            dma((heads - 1, per_head, pieces)),
            dma((pieces,)),
            dma((3,)),
        ],
        compiler_params=pltpu.CompilerParams(
            collective_id=0, has_side_effects=True, vmem_limit_bytes=56 * 1024 * 1024
        ),
    )(
        queries.transpose(1, 0, 2),
        key_rows.transpose(1, 0, 2),
        value_rows.transpose(1, 0, 2),
        keep_tiles,
        out_weight,
        gate_scale.reshape(-1, gate_lanes),
    )


def chain_kernel(
    sizes, q_ref, k_ref, v_ref, keep_hbm, w_ref, gate_hbm, out_ref,
    q_own, q_far, k_all, v_all, w_all, attended, far_att, part, got, pair, keep_own, keep_far, gate_ref, bias,
    kv_send, kv_recv, q_send, q_recv, keep_sem, att_send, att_recv,
    z_send, z_recv, y_send, y_recv, r_send, r_recv, pair_recv, own_sem, in_sem, gate_sem,
):
    groups, n, heads, pieces = sizes
    g, t, me = lax.axis_index("groups"), lax.axis_index("tm"), lax.axis_index("head")
    rows, cols = w_ref.shape
    wide = cols // pieces
    per_head = n // heads
    part_rows = rows // groups
    halves = 2 if part_rows % 32 == 0 else 1
    sub_rows = part_rows // halves
    head_count, tokens = q_ref.shape[0], q_ref.shape[1]
    per_slab = tokens // TILE
    total_pieces = n * pieces
    chips = heads // 2
    my_chip, my_core = me // 2, lax.rem(me, 2)
    partner = me + 1 - 2 * my_core

    left = t < n // 2
    inner = (t > 0) & (t < n - 1)
    outer = jnp.logical_not(inner)
    end = jnp.where(left, 0, n - 1)
    near = jnp.where(left, 1, n - 2)
    across_mid = n - 1 - t
    far_end = n - 1 - end
    mate = jnp.where(inner, end, near)
    mate_id = {"tm": mate}
    mid_id = {"tm": across_mid}

    barrier = pltpu.get_barrier_semaphore()

    def greet(partner):
        pl.semaphore_signal(barrier, inc=1, device_id=partner, device_id_type=MESH)

    greet(mate_id)
    @pl.when(inner)
    def _():
        greet(mid_id)
    for o in range(1, groups):
        greet({"groups": lax.rem(g + o, groups)})
    for o in range(1, heads):
        greet({"head": lax.rem(me + o, heads)})
    @pl.when(inner)
    def _():
        pl.semaphore_wait(barrier, groups + heads)
    @pl.when(outer)
    def _():
        pl.semaphore_wait(barrier, groups + heads - 1)

    def remote(src, dst, send, recv, device):
        return pltpu.make_async_remote_copy(
            src_ref=src, dst_ref=dst, send_sem=send, recv_sem=recv,
            device_id=device, device_id_type=MESH,
        )

    kv = ((k_ref, k_all), (v_ref, v_all))

    def kv_first(h, which, device):
        src, dst = kv[which]
        return remote(
            src.at[h], dst.at[t, h], kv_send.at[0, which, h], kv_recv.at[t, which, h], device
        )

    def kv_relay(h, which):
        buf = kv[which][1]
        return remote(
            buf.at[end, h], buf.at[end, h], kv_send.at[1, which, h], kv_recv.at[end, which, h],
            mid_id,
        )

    def kv_arrival(slab, h, which):
        buf = kv[which][1]
        return remote(
            buf.at[slab, h], buf.at[slab, h], kv_send.at[1, which, h],
            kv_recv.at[slab, which, h], mid_id,
        )

    def q_copy(h):
        return remote(q_ref.at[h], q_far.at[h], q_send.at[h], q_recv.at[h], mate_id)

    keep_copy = remote(keep_hbm, keep_far, keep_sem.at[0], keep_sem.at[1], mate_id)

    def lanes_of(h):
        return pl.ds(pl.multiple_of(h * HD, HD), HD)

    def att_copy(h):
        return remote(
            far_att.at[:, lanes_of(h)], attended.at[:, lanes_of(h)],
            att_send.at[h], att_recv.at[h], mate_id,
        )

    def rows_of(sender, s):
        return pl.ds(pl.multiple_of(sender * part_rows + s * sub_rows, sub_rows), sub_rows)

    def own_copy(c):
        return pltpu.make_async_copy(
            w_ref.at[:, c * wide:(c + 1) * wide], w_all.at[t, c], own_sem.at[c]
        )

    def first_send(c, s, way):
        mine = rows_of(g, s)
        return remote(
            w_ref.at[mine, c * wide:(c + 1) * wide], w_all.at[t, c, mine],
            z_send.at[way, t, c, s], z_recv.at[t, c, s], mid_id if way else mate_id,
        )

    def rest_send(c, s, o):
        theirs = rows_of(lax.rem(g + groups - o, groups), s)
        return remote(
            w_ref.at[theirs, c * wide:(c + 1) * wide], w_all.at[t, c, theirs],
            y_send.at[o - 1, t, c, s], y_recv.at[o - 1, t, c, s], mate_id,
        )

    def relay(b, c, s, way):
        mine = rows_of(g, s)
        return remote(
            w_all.at[b, c, mine], w_all.at[b, c, mine],
            z_send.at[way, b, c, s], z_recv.at[b, c, s], mid_id if way else mate_id,
        )

    def across(b, c, s, o):
        mine = rows_of(g, s)
        return remote(
            w_all.at[b, c, mine], w_all.at[b, c, mine],
            y_send.at[o - 1, b, c, s], y_recv.at[o - 1, b, c, s],
            {"groups": lax.rem(g + o, groups)},
        )

    def across_arrival(b, c, s, o):
        theirs = rows_of(lax.rem(g + groups - o, groups), s)
        return remote(
            w_all.at[b, c, theirs], w_all.at[b, c, theirs],
            y_send.at[o - 1, b, c, s], y_recv.at[o - 1, b, c, s],
            {"groups": lax.rem(g + o, groups)},
        )

    def partner_send(b, c):
        at = lax.rem(b, per_head)
        return remote(
            part.at[b, c], got.at[0, at, c], r_send.at[b, c], r_recv.at[0, at, c],
            {"head": partner},
        )

    def give_send(b, c):
        owner, at = b // per_head, lax.rem(b, per_head)
        return remote(
            part.at[b, c], pair.at[owner // 2, at, c], r_send.at[b, c],
            pair_recv.at[owner // 2, at, c], {"head": partner},
        )

    def sum_send(b, c):
        owner, at = b // per_head, lax.rem(b, per_head)
        slot = lax.rem(my_chip - owner // 2 + chips, chips)
        return remote(
            part.at[b, c], got.at[slot, at, c], r_send.at[b, c], r_recv.at[slot, at, c],
            {"head": owner},
        )

    def term_arrival(b, c, slot):
        at = lax.rem(b, per_head)
        return remote(
            part.at[b, c], got.at[slot, at, c], r_send.at[b, c], r_recv.at[slot, at, c],
            {"head": partner},
        )

    in_copies = [
        pltpu.make_async_copy(src, dst, in_sem.at[i])
        for i, (src, dst) in enumerate(
            ((keep_hbm, keep_own), (q_ref, q_own), (k_ref, k_all.at[t]), (v_ref, v_all.at[t]))
        )
    ]

    gate_copy = pltpu.make_async_copy(gate_hbm, gate_ref, gate_sem.at[0])

    @pl.when(outer)
    def _():
        for h in range(head_count):
            for which in range(2):
                kv_first(h, which, mate_id).start()
        keep_copy.start()
        for h in range(head_count):
            q_copy(h).start()

    @pl.when(inner)
    def _():
        for h in range(head_count):
            for which in range(2):
                kv_first(h, which, mid_id).start()
        for copy in in_copies:
            copy.start()

    for c in range(pieces):
        for s in range(halves):
            first_send(c, s, 0).start()
        @pl.when(outer)
        def _(c=c):
            for s in range(halves):
                for o in range(1, groups):
                    rest_send(c, s, o).start()
    for c in range(pieces):
        own_copy(c).start()
    gate_copy.start()

    def block_of(k):
        place = jnp.where(left, t, n - 1 - t)
        b = jnp.where(k == 0, place, jnp.where(k == 1, 1 - place, k))
        return jnp.where(left, b, n - 1 - b)

    def pass_on(j):
        b, c = block_of(j // pieces), lax.rem(j, pieces)
        for s in range(halves):
            relay(b, c, s, 0).wait_recv()
            @pl.when(inner & (b == end))
            def _(s=s):
                relay(b, c, s, 1).start()
            @pl.when(inner & (b != end))
            def _(s=s):
                relay(b, c, s, 0).start()
            @pl.when(outer | (b != end))
            def _(s=s):
                for o in range(1, groups):
                    across(b, c, s, o).start()

    scale = math.log2(math.e) / math.sqrt(HD)
    reach_slabs = keep_own.shape[1] // per_slab

    def set_bias(at, ref):
        kept = ref[...]
        spread = jnp.concatenate(
            [jnp.broadcast_to(kept[:, c:c + 1], (per_slab, TILE)) for c in range(kept.shape[1])],
            axis=1,
        )
        bias[at] = jnp.where(spread > 0, 0.0, -jnp.inf).astype(jnp.float32)

    def attend(h, slab, queries, at, dst):
        for i in range(per_slab):
            q = queries[h, i * TILE:(i + 1) * TILE, :]
            scores = []
            for j in range(reach_slabs):
                other = lax.rem(slab + j - reach_slabs // 2 + n, n)
                s = lax.dot_general(
                    q, k_all[other, h], (((1,), (1,)), ((), ())),
                    preferred_element_type=jnp.float32,
                )
                scores.append(s * scale + bias[at, i:i + 1, j * tokens:(j + 1) * tokens])
            peak = functools.reduce(
                jnp.maximum, [jnp.max(s, axis=1, keepdims=True) for s in scores]
            )
            exps = [jnp.exp2(s - peak) for s in scores]
            total = functools.reduce(jnp.add, [jnp.sum(e, axis=1, keepdims=True) for e in exps])
            acc = None
            for j in range(reach_slabs):
                other = lax.rem(slab + j - reach_slabs // 2 + n, n)
                term = jnp.dot(
                    exps[j].astype(jnp.bfloat16), v_all[other, h],
                    preferred_element_type=jnp.float32,
                )
                acc = term if acc is None else acc + term
            dst[i * TILE:(i + 1) * TILE, lanes_of(h)] = (acc * (1.0 / total)).astype(jnp.bfloat16)

    def project(b, c):
        def tile(i, carry):
            at = pl.ds(pl.multiple_of(i * TILE, TILE), TILE)
            part[b, c, at, :] = jnp.dot(
                attended[at, :], w_all[b, c], preferred_element_type=jnp.float32
            ).astype(jnp.bfloat16)
            return carry

        lax.fori_loop(0, tokens // TILE, tile, 0)
        owner = b // per_head
        @pl.when(owner == partner)
        def _():
            partner_send(b, c).start()
        @pl.when((owner // 2 != my_chip) & (lax.rem(owner, 2) != my_core))
        def _():
            give_send(b, c).start()

    def collect(j):
        b, c = block_of(j // pieces), lax.rem(j, pieces)
        owner, at = b // per_head, lax.rem(b, per_head)
        @pl.when((owner // 2 != my_chip) & (lax.rem(owner, 2) == my_core))
        def _():
            give_send(b, c).wait_recv()

            def tile(i, carry):
                now = pl.ds(pl.multiple_of(i * TILE, TILE), TILE)
                part[b, c, now, :] = (
                    part[b, c, now, :].astype(jnp.float32)
                    + pair[owner // 2, at, c, now, :].astype(jnp.float32)
                ).astype(jnp.bfloat16)
                return carry

            lax.fori_loop(0, tokens // TILE, tile, 0)
            sum_send(b, c).start()

    def use(j):
        b, c = block_of(j // pieces), lax.rem(j, pieces)
        for s in range(halves):
            for o in range(1, groups):
                across_arrival(b, c, s, o).wait_recv()
        project(b, c)

    def finish(j):
        b, c = block_of(j // pieces), lax.rem(j, pieces)
        cb = lax.rem(b, per_head)
        @pl.when(b // per_head == me)
        def _():
            for slot in range(chips):
                term_arrival(b, c, slot).wait_recv()
            span = gate_ref.shape[1]
            for u in range(wide // span):
                lanes = slice(u * span, (u + 1) * span)
                summed = part[b, c, :, lanes].astype(jnp.float32)
                for slot in range(chips):
                    summed = summed + got[slot, cb, c, :, lanes].astype(jnp.float32)
                block = cb * (cols // span) + c * (wide // span) + u
                at = pl.ds(pl.multiple_of(block * span, span), span)
                out_ref[:, at] = (gate_ref[pl.ds(block, 1), :] * summed).astype(out_ref.dtype)

    def do_use(j, carry):
        use(j)
        collect(j - 1)
        return carry

    def use_last(j, carry):
        use(j)
        collect(j)
        return carry

    def do_finish(j, carry):
        finish(j)
        return carry

    def own_block(c, carry):
        project(t, c)
        @pl.when(c > 0)
        def _():
            collect(c - 1)
        return carry

    @pl.when(inner)
    def _():
        for copy in in_copies:
            copy.wait()
        set_bias(0, keep_own)

        def own_slab(h, carry):
            for which in range(2):
                kv_arrival(end, h, which).wait_recv()
                kv_relay(h, which).start()
            for which in range(2):
                kv_arrival(across_mid, h, which).wait_recv()
            attend(h, t, q_own, 0, attended)
            return carry

        lax.fori_loop(0, head_count, own_slab, 0)
        for c in range(pieces):
            for s in range(halves):
                first_send(c, s, 1).start()
        for c in range(pieces):
            own_copy(c).wait()
        lax.fori_loop(0, pieces, own_block, 0)
        keep_copy.wait_recv()
        set_bias(1, keep_far)

        def end_slab(h, carry):
            q_copy(h).wait_recv()
            for which in range(2):
                kv_arrival(far_end, h, which).wait_recv()
            attend(h, end, q_far, 1, far_att)
            att_copy(h).start()
            return carry

        lax.fori_loop(0, head_count, end_slab, 0)

    def early_pass(j, carry):
        pass_on(j)
        return carry

    @pl.when(outer)
    def _():
        lax.fori_loop(pieces, 2 * pieces, early_pass, 0)
        for c in range(pieces):
            own_copy(c).wait()
        for h in range(head_count):
            att_copy(h).wait_recv()
        lax.fori_loop(0, pieces, own_block, 0)

    @pl.when(outer)
    def _():
        lax.fori_loop(pieces, 2 * pieces, do_use, 0)

    def used_by(j):
        lagging = jnp.maximum(jnp.maximum(j - pieces - 1, 2 * j - 4 * pieces - 1), pieces)
        lagging = lagging + jnp.where(j >= total_pieces - 2, 1, 0)
        return jnp.where(inner, jnp.minimum(lagging, j - 1), jnp.maximum(j - 2, 2 * pieces))

    def step(j, carry):
        pass_on(j)
        @pl.when(inner & (j < 3 * pieces))
        def _():
            pass_on(j - pieces)
        return lax.fori_loop(used_by(j - 1), used_by(j), do_use, carry)

    lax.fori_loop(2 * pieces, total_pieces, step, 0)
    ready = used_by(total_pieces - 1)
    gate_copy.wait()
    lax.fori_loop(0, total_pieces - 4, do_finish, 0)
    collect(ready - 1)
    lax.fori_loop(ready, total_pieces, use_last, 0)
    lax.fori_loop(total_pieces - 4, total_pieces, do_finish, 0)

    @pl.when(outer)
    def _():
        for h in range(head_count):
            for which in range(2):
                kv_first(h, which, mate_id).wait_send()
            q_copy(h).wait_send()
        keep_copy.wait_send()

    @pl.when(inner)
    def _():
        for h in range(head_count):
            for which in range(2):
                kv_first(h, which, mid_id).wait_send()
                kv_relay(h, which).wait_send()
            att_copy(h).wait_send()
        for c in range(pieces):
            for s in range(halves):
                first_send(c, s, 1).wait_send()

    def drain(b, carry):
        for c in range(pieces):
            for s in range(halves):
                @pl.when(b == t)
                def _(c=c, s=s):
                    first_send(c, s, 0).wait_send()
                @pl.when((b == t) & outer)
                def _(c=c, s=s):
                    for o in range(1, groups):
                        rest_send(c, s, o).wait_send()
                @pl.when((b != t) & (outer | (b != end)))
                def _(c=c, s=s):
                    for o in range(1, groups):
                        across(b, c, s, o).wait_send()
                @pl.when(inner & (b == end))
                def _(c=c, s=s):
                    relay(b, c, s, 1).wait_send()
                @pl.when(inner & (b != end) & (b != t))
                def _(c=c, s=s):
                    relay(b, c, s, 0).wait_send()
            @pl.when(b // per_head != me)
            def _(c=c):
                partner_send(b, c).wait_send()
        return carry

    lax.fori_loop(0, n, drain, 0)


def chain_shards(queries, key_rows, value_rows, keep_tiles, out_weight, gate_scale):
    n, heads, groups = lax.axis_size("tm"), lax.axis_size("head"), lax.axis_size("groups")
    tokens = queries.shape[0]
    head_count = queries.shape[1]
    flat = head_count * HD
    rows, cols = out_weight.shape
    pieces = cols // 256 if cols % 256 == 0 else 1
    wide = cols // pieces
    per_head = n // heads
    gate_lanes = 128 if wide % 128 == 0 else wide
    vmem = pl.BlockSpec(memory_space=pltpu.VMEM)
    hbm = pl.BlockSpec(memory_space=pl.ANY)
    dma = pltpu.SemaphoreType.DMA
    bf16 = jnp.bfloat16
    return pl.pallas_call(
        functools.partial(chain_kernel, (groups, n, heads, pieces)),
        out_shape=pltpu.VMEM((tokens, gate_scale.shape[0]), bf16),
        in_specs=[hbm, hbm, hbm, hbm, hbm, hbm],
        out_specs=vmem,
        scratch_shapes=[
            pltpu.VMEM((head_count, tokens, HD), bf16),
            pltpu.VMEM((head_count, tokens, HD), bf16),
            pltpu.VMEM((n, head_count, tokens, HD), bf16),
            pltpu.VMEM((n, head_count, tokens, HD), bf16),
            pltpu.VMEM((n, pieces, rows, wide), bf16),
            pltpu.VMEM((tokens, flat), bf16),
            pltpu.VMEM((tokens, flat), bf16),
            pltpu.VMEM((n, pieces, tokens, wide), bf16),
            pltpu.VMEM((heads // 2, per_head, pieces, tokens, wide), bf16),
            pltpu.VMEM((heads // 2, per_head, pieces, tokens, wide), bf16),
            pltpu.VMEM(keep_tiles.shape, jnp.int32),
            pltpu.VMEM(keep_tiles.shape, jnp.int32),
            pltpu.VMEM((gate_scale.shape[0] // gate_lanes, gate_lanes), jnp.float32),
            pltpu.VMEM((2, keep_tiles.shape[0], keep_tiles.shape[1] * TILE), jnp.float32),
            dma((2, 2, head_count)),
            dma((n, 2, head_count)),
            dma((head_count,)),
            dma((head_count,)),
            dma((2,)),
            dma((head_count,)),
            dma((head_count,)),
            dma((2, n, pieces, 2)),
            dma((n, pieces, 2)),
            dma((groups - 1, n, pieces, 2)),
            dma((groups - 1, n, pieces, 2)),
            dma((n, pieces)),
            dma((heads // 2, per_head, pieces)),
            dma((heads // 2, per_head, pieces)),
            dma((pieces,)),
            dma((4,)),
            dma((1,)),
        ],
        compiler_params=pltpu.CompilerParams(
            collective_id=0, has_side_effects=True, vmem_limit_bytes=56 * 1024 * 1024
        ),
    )(
        queries.transpose(1, 0, 2),
        key_rows.transpose(1, 0, 2),
        value_rows.transpose(1, 0, 2),
        keep_tiles,
        out_weight,
        gate_scale.reshape(-1, gate_lanes),
    )


def solution(mesh):
    placed = (
        P(("groups", "tm"), "head", None),
        P(("groups", "tm"), "head", None),
        P(("groups", "tm"), "head", None),
        P(("groups", "tm"), None),
        P("head", "tm"),
        P(("groups", "head")),
    )
    n, heads = mesh.shape["tm"], mesh.shape["head"]
    chain = n == 4 and n % heads == 0 and heads % 2 == 0 and mesh.shape["groups"] > 1
    body = chain_shards if chain else shards
    return jax.shard_map(
        body, mesh=mesh, in_specs=placed, out_specs=P(("groups", "tm"), "head"), check_vma=False
    )
```

```python
import functools
import math

import jax
import jax.numpy as jnp
from jax import lax
from jax.experimental import pallas as pl
from jax.experimental.pallas import tpu as pltpu
from jax.sharding import PartitionSpec as P

HD = 128
TILE = 128
MESH = pl.DeviceIdType.MESH


def layer_kernel(
    sizes, q_ref, k_ref, v_ref, keep_ref, w_ref, gate_ref, out_ref,
    q_own, k_all, v_all, w_all, attended, part, got,
    kv_send, kv_recv, z_send, z_recv, y_send, y_recv, r_send, r_recv, own_sem, in_sem,
):
    groups, n, heads, reach, pieces = sizes
    g, t, me = lax.axis_index("groups"), lax.axis_index("tm"), lax.axis_index("head")
    rows, cols = w_ref.shape
    wide = cols // pieces
    per_head = n // heads
    part_rows = rows // groups
    head_count, tokens = q_ref.shape[0], q_ref.shape[1]
    slabs = 2 * reach + 1

    barrier = pltpu.get_barrier_semaphore()
    partners = []
    for d in range(1, reach + 1):
        partners += [{"tm": lax.rem(t + d, n)}, {"tm": lax.rem(t + n - d, n)}]
    for o in range(1, groups):
        partners.append({"groups": lax.rem(g + o, groups)})
    for o in range(1, heads):
        partners.append({"head": lax.rem(me + o, heads)})
    for partner in partners:
        pl.semaphore_signal(barrier, inc=1, device_id=partner, device_id_type=MESH)
    pl.semaphore_wait(barrier, len(partners))

    def remote(src, dst, send, recv, device):
        return pltpu.make_async_remote_copy(
            src_ref=src, dst_ref=dst, send_sem=send, recv_sem=recv,
            device_id=device, device_id_type=MESH,
        )

    kv_copies = []
    for d in range(1, reach + 1):
        for slot, to in ((reach - d, lax.rem(t + d, n)), (reach + d, lax.rem(t + n - d, n))):
            for which, (src, dst) in enumerate(((k_ref, k_all), (v_ref, v_all))):
                kv_copies.append(
                    remote(src, dst.at[slot], kv_send.at[slot, which], kv_recv.at[slot, which], {"tm": to})
                )
    @pl.when(t == 0)
    def _():
        for copy in reversed(kv_copies):
            copy.start()

    @pl.when(t != 0)
    def _():
        for copy in kv_copies:
            copy.start()

    in_copies = [
        pltpu.make_async_copy(src, dst, in_sem.at[i])
        for i, (src, dst) in enumerate(
            ((q_ref, q_own), (k_ref, k_all.at[reach]), (v_ref, v_all.at[reach]))
        )
    ]
    for copy in in_copies:
        copy.start()

    my_rows = pl.ds(pl.multiple_of(g * part_rows, part_rows), part_rows)

    def own_copy(c):
        return pltpu.make_async_copy(
            w_ref.at[:, c * wide:(c + 1) * wide], w_all.at[t, c], own_sem.at[c]
        )

    def first_send(c, side):
        to = jnp.minimum(t + 1, n - 1) if side else jnp.maximum(t - 1, 0)
        return remote(
            w_ref.at[my_rows, c * wide:(c + 1) * wide], w_all.at[t, c, my_rows],
            z_send.at[side, t, c], z_recv.at[t, c], {"tm": to},
        )

    def relay(b, c, side):
        to = jnp.minimum(t + 1, n - 1) if side else jnp.maximum(t - 1, 0)
        return remote(
            w_all.at[b, c, my_rows], w_all.at[b, c, my_rows],
            z_send.at[side, b, c], z_recv.at[b, c], {"tm": to},
        )

    def across(b, c, o):
        return remote(
            w_all.at[b, c, my_rows], w_all.at[b, c, my_rows],
            y_send.at[o - 1, b, c], y_recv.at[o - 1, b, c],
            {"groups": lax.rem(g + o, groups)},
        )

    def across_arrival(b, c, o):
        sender = lax.rem(g + groups - o, groups)
        their_rows = pl.ds(pl.multiple_of(sender * part_rows, part_rows), part_rows)
        return remote(
            w_all.at[b, c, their_rows], w_all.at[b, c, their_rows],
            y_send.at[o - 1, b, c], y_recv.at[o - 1, b, c],
            {"groups": lax.rem(g + o, groups)},
        )

    def term_send(b, c, o):
        return remote(
            part.at[b, c], got.at[o - 1, b % per_head, c],
            r_send.at[b, c], r_recv.at[o - 1, b % per_head, c],
            {"head": lax.rem(me + o, heads)},
        )

    for c in range(pieces):
        own_copy(c).start()
        @pl.when(t < n - 1)
        def _(c=c):
            first_send(c, 1).start()
        @pl.when(t > 0)
        def _(c=c):
            first_send(c, 0).start()

    for copy in in_copies:
        copy.wait()
    for copy in kv_copies:
        copy.wait_recv()

    scale = 1.0 / math.sqrt(HD)
    per_slab = tokens // TILE

    early = min(pieces, head_count - 1)

    def pass_on(j, side):
        step, c = j // pieces, j % pieces
        b = (t - 1 - step) if side else (t + 1 + step)
        @pl.when((b >= 0) & (b <= n - 1))
        def _():
            relay(b, c, side).wait_recv()
            @pl.when((t < n - 1) if side else (t > 0))
            def _():
                relay(b, c, side).start()
            for o in range(1, groups):
                across(b, c, o).start()

    def one_head(h, carry):
        lanes = pl.ds(pl.multiple_of(h * HD, HD), HD)
        for i in range(per_slab):
            q = q_own[h, i * TILE:(i + 1) * TILE, :]
            scores = []
            for j in range(slabs):
                s = lax.dot_general(
                    q, k_all[j, h], (((1,), (1,)), ((), ())), preferred_element_type=jnp.float32
                )
                bias = jnp.concatenate(
                    [
                        jnp.full(
                            (1, TILE),
                            jnp.where(keep_ref[i, j * per_slab + u] > 0, 0.0, -jnp.inf),
                            jnp.float32,
                        )
                        for u in range(per_slab)
                    ],
                    axis=1,
                )
                scores.append(s * scale + bias)
            peak = functools.reduce(
                jnp.maximum, [jnp.max(s, axis=1, keepdims=True) for s in scores]
            )
            exps = [jnp.exp(s - peak) for s in scores]
            total = functools.reduce(jnp.add, [jnp.sum(e, axis=1, keepdims=True) for e in exps])
            inverse = 1.0 / total
            acc = None
            for j in range(slabs):
                term = jnp.dot(
                    (exps[j] * inverse).astype(jnp.bfloat16), v_all[j, h],
                    preferred_element_type=jnp.float32,
                )
                acc = term if acc is None else acc + term
            attended[i * TILE:(i + 1) * TILE, lanes] = acc.astype(jnp.bfloat16)
        @pl.when(h >= head_count - early)
        def _():
            for side in (1, 0):
                pass_on(h - (head_count - early), side)
        return carry

    lax.fori_loop(0, head_count, one_head, 0)

    def project(b, c):
        def tile(i, carry):
            at = pl.ds(pl.multiple_of(i * TILE, TILE), TILE)
            part[b, c, at, :] = jnp.dot(
                attended[at, :], w_all[b, c], preferred_element_type=jnp.float32
            ).astype(jnp.bfloat16)
            return carry

        lax.fori_loop(0, tokens // TILE, tile, 0)
        owner = b // per_head
        for o in range(1, heads):
            @pl.when(owner == lax.rem(me + o, heads))
            def _():
                term_send(b, c, o).start()

    for c in range(pieces):
        own_copy(c).wait()
        project(t, c)

    def use(j, side):
        step, c = j // pieces, j % pieces
        b = (t - 1 - step) if side else (t + 1 + step)
        @pl.when((b >= 0) & (b <= n - 1))
        def _():
            for o in range(1, groups):
                across_arrival(b, c, o).wait_recv()
            project(b, c)

    count = (n - 1) * pieces

    def use_both(j, carry):
        for side in (1, 0):
            use(j, side)
        return carry

    def step(j, carry):
        for side in (1, 0):
            pass_on(j, side)
        first = jnp.minimum(2 * (j - early), j - 1)
        last = jnp.minimum(2 * (j - early) + 2, j)
        return lax.fori_loop(first, last, use_both, carry)

    lax.fori_loop(early, count, step, 0)
    lax.fori_loop(min(2 * (count - early), count - 1), count, use_both, 0)

    for cb in range(per_head):
        for c in range(pieces):
            b = me * per_head + cb
            for o in range(1, heads):
                term_send(b, c, o).wait_recv()
            span = wide if gate_ref.shape[0] == 1 else gate_ref.shape[1]
            for u in range(wide // span):
                lanes = slice(u * span, (u + 1) * span)
                summed = part[b, c, :, lanes].astype(jnp.float32)
                for o in range(1, heads):
                    summed = summed + got[o - 1, cb, c, :, lanes].astype(jnp.float32)
                at = cb * cols + c * wide + u * span
                gate = gate_ref[:, at:at + span] if span == wide else gate_ref[at // span:at // span + 1, :]
                out_ref[:, at:at + span] = (gate * summed).astype(out_ref.dtype)

    for copy in kv_copies:
        copy.wait_send()
    for c in range(pieces):
        @pl.when(t < n - 1)
        def _(c=c):
            first_send(c, 1).wait_send()
        @pl.when(t > 0)
        def _(c=c):
            first_send(c, 0).wait_send()

    def drain(b, carry):
        for c in range(pieces):
            @pl.when(b != t)
            def _(c=c):
                for o in range(1, groups):
                    across(b, c, o).wait_send()
            @pl.when((b < t) & (t < n - 1))
            def _(c=c):
                relay(b, c, 1).wait_send()
            @pl.when((b > t) & (t > 0))
            def _(c=c):
                relay(b, c, 0).wait_send()
            @pl.when(b // per_head != me)
            def _(c=c):
                term_send(b, c, 1).wait_send()
        return carry

    lax.fori_loop(0, n, drain, 0)


def shards(queries, key_rows, value_rows, keep_tiles, out_weight, gate_scale):
    n, heads, groups = lax.axis_size("tm"), lax.axis_size("head"), lax.axis_size("groups")
    reach = min(2, (n - 1) // 2)
    tokens = queries.shape[0]
    head_count = queries.shape[1]
    flat = head_count * HD
    rows, cols = out_weight.shape
    pieces = cols // 256 if cols % 256 == 0 else 1
    wide = cols // pieces
    per_head = n // heads
    slabs = 2 * reach + 1
    gate_lanes = 128 if wide % 128 == 0 else gate_scale.shape[0]
    vmem = pl.BlockSpec(memory_space=pltpu.VMEM)
    hbm = pl.BlockSpec(memory_space=pl.ANY)
    dma = pltpu.SemaphoreType.DMA
    bf16 = jnp.bfloat16
    return pl.pallas_call(
        functools.partial(layer_kernel, (groups, n, heads, reach, pieces)),
        out_shape=jax.ShapeDtypeStruct((tokens, gate_scale.shape[0]), bf16),
        in_specs=[hbm, hbm, hbm, pl.BlockSpec(memory_space=pltpu.SMEM), hbm, vmem],
        out_specs=vmem,
        scratch_shapes=[
            pltpu.VMEM((head_count, tokens, HD), bf16),
            pltpu.VMEM((slabs, head_count, tokens, HD), bf16),
            pltpu.VMEM((slabs, head_count, tokens, HD), bf16),
            pltpu.VMEM((n, pieces, rows, wide), bf16),
            pltpu.VMEM((tokens, flat), bf16),
            pltpu.VMEM((n, pieces, tokens, wide), bf16),
            pltpu.VMEM((heads - 1, per_head, pieces, tokens, wide), bf16),
            dma((slabs, 2)),
            dma((slabs, 2)),
            dma((2, n, pieces)),
            dma((n, pieces)),
            dma((groups - 1, n, pieces)),
            dma((groups - 1, n, pieces)),
            dma((n, pieces)),
            dma((heads - 1, per_head, pieces)),
            dma((pieces,)),
            dma((3,)),
        ],
        compiler_params=pltpu.CompilerParams(
            collective_id=0, has_side_effects=True, vmem_limit_bytes=56 * 1024 * 1024
        ),
    )(
        queries.transpose(1, 0, 2),
        key_rows.transpose(1, 0, 2),
        value_rows.transpose(1, 0, 2),
        keep_tiles,
        out_weight,
        gate_scale.reshape(-1, gate_lanes),
    )


def chain_kernel(
    sizes, q_ref, k_ref, v_ref, keep_hbm, w_ref, gate_hbm, out_ref,
    q_own, q_far, k_all, v_all, w_all, attended, far_att, part, got, pair, keep_own, keep_far, gate_ref, bias,
    kv_send, kv_recv, q_send, q_recv, keep_sem, att_send, att_recv,
    z_send, z_recv, y_send, y_recv, r_send, r_recv, pair_recv, t_send, t_recv, t_pair, own_sem, in_sem, gate_sem,
):
    groups, n, heads, pieces = sizes
    g, t, me = lax.axis_index("groups"), lax.axis_index("tm"), lax.axis_index("head")
    rows, cols = w_ref.shape
    wide = cols // pieces
    per_head = n // heads
    part_rows = rows // groups
    halves = 2 if wide % 256 == 0 else 1
    sub_cols = wide // halves
    head_count, tokens = q_ref.shape[0], q_ref.shape[1]
    per_slab = tokens // TILE
    total_pieces = n * pieces
    chips = heads // 2
    my_chip, my_core = me // 2, lax.rem(me, 2)
    partner = me + 1 - 2 * my_core

    left = t < n // 2
    inner = (t > 0) & (t < n - 1)
    outer = jnp.logical_not(inner)
    end = jnp.where(left, 0, n - 1)
    near = jnp.where(left, 1, n - 2)
    across_mid = n - 1 - t
    far_end = n - 1 - end
    mate = jnp.where(inner, end, near)
    mate_id = {"tm": mate}
    mid_id = {"tm": across_mid}

    barrier = pltpu.get_barrier_semaphore()

    def greet(partner):
        pl.semaphore_signal(barrier, inc=1, device_id=partner, device_id_type=MESH)

    greet(mate_id)
    @pl.when(inner)
    def _():
        greet(mid_id)
    for o in range(1, groups):
        greet({"groups": lax.rem(g + o, groups)})
    for o in range(1, heads):
        greet({"head": lax.rem(me + o, heads)})
    @pl.when(inner)
    def _():
        pl.semaphore_wait(barrier, groups + heads)
    @pl.when(outer)
    def _():
        pl.semaphore_wait(barrier, groups + heads - 1)

    def remote(src, dst, send, recv, device):
        return pltpu.make_async_remote_copy(
            src_ref=src, dst_ref=dst, send_sem=send, recv_sem=recv,
            device_id=device, device_id_type=MESH,
        )

    kv = ((k_ref, k_all), (v_ref, v_all))

    def kv_first(h, which, device):
        src, dst = kv[which]
        return remote(
            src.at[h], dst.at[t, h], kv_send.at[0, which, h], kv_recv.at[t, which, h], device
        )

    def kv_relay(h, which):
        buf = kv[which][1]
        return remote(
            buf.at[end, h], buf.at[end, h], kv_send.at[1, which, h], kv_recv.at[end, which, h],
            mid_id,
        )

    def kv_arrival(slab, h, which):
        buf = kv[which][1]
        return remote(
            buf.at[slab, h], buf.at[slab, h], kv_send.at[1, which, h],
            kv_recv.at[slab, which, h], mid_id,
        )

    def q_copy(h):
        return remote(q_ref.at[h], q_far.at[h], q_send.at[h], q_recv.at[h], mate_id)

    keep_copy = remote(keep_hbm, keep_far, keep_sem.at[0], keep_sem.at[1], mate_id)

    def lanes_of(h):
        return pl.ds(pl.multiple_of(h * HD, HD), HD)

    def att_copy(h):
        return remote(
            far_att.at[:, lanes_of(h)], attended.at[:, lanes_of(h)],
            att_send.at[h], att_recv.at[h], mate_id,
        )

    def rows_of(sender):
        return pl.ds(pl.multiple_of(sender * part_rows, part_rows), part_rows)

    def lanes_in(s, c=0):
        return slice(c * wide + s * sub_cols, c * wide + (s + 1) * sub_cols)

    def own_copy(c):
        return pltpu.make_async_copy(
            w_ref.at[:, c * wide:(c + 1) * wide], w_all.at[t, c], own_sem.at[c]
        )

    def first_send(c, s, way):
        mine = rows_of(g)
        return remote(
            w_ref.at[mine, lanes_in(s, c)], w_all.at[t, c, mine, lanes_in(s)],
            z_send.at[way, t, c, s], z_recv.at[t, c, s], mid_id if way else mate_id,
        )

    def rest_send(c, s, o):
        theirs = rows_of(lax.rem(g + groups - o, groups))
        return remote(
            w_ref.at[theirs, lanes_in(s, c)], w_all.at[t, c, theirs, lanes_in(s)],
            y_send.at[o - 1, t, c, s], y_recv.at[o - 1, t, c, s], mate_id,
        )

    def relay(b, c, s, way):
        mine = rows_of(g)
        return remote(
            w_all.at[b, c, mine, lanes_in(s)], w_all.at[b, c, mine, lanes_in(s)],
            z_send.at[way, b, c, s], z_recv.at[b, c, s], mid_id if way else mate_id,
        )

    def across(b, c, s, o):
        mine = rows_of(g)
        return remote(
            w_all.at[b, c, mine, lanes_in(s)], w_all.at[b, c, mine, lanes_in(s)],
            y_send.at[o - 1, b, c, s], y_recv.at[o - 1, b, c, s],
            {"groups": lax.rem(g + o, groups)},
        )

    def theirs_on(b, o, device):
        c, s = pieces - 1, halves - 1
        theirs = rows_of(lax.rem(g + groups - o, groups))
        return remote(
            w_all.at[b, c, theirs, lanes_in(s)], w_all.at[b, c, theirs, lanes_in(s)],
            y_send.at[o - 1, b, c, s], y_recv.at[o - 1, b, c, s], device,
        )

    def across_arrival(b, c, s, o):
        theirs = rows_of(lax.rem(g + groups - o, groups))
        return remote(
            w_all.at[b, c, theirs, lanes_in(s)], w_all.at[b, c, theirs, lanes_in(s)],
            y_send.at[o - 1, b, c, s], y_recv.at[o - 1, b, c, s],
            {"groups": lax.rem(g + o, groups)},
        )

    def partner_send(b, c):
        at = lax.rem(b, per_head)
        return remote(
            part.at[b, c], got.at[0, at, c], r_send.at[b, c], r_recv.at[0, at, c],
            {"head": partner},
        )

    def give_send(b, c):
        owner, at = b // per_head, lax.rem(b, per_head)
        return remote(
            part.at[b, c], pair.at[owner // 2, at, c], r_send.at[b, c],
            pair_recv.at[owner // 2, at, c], {"head": partner},
        )

    def sum_send(b, c):
        owner, at = b // per_head, lax.rem(b, per_head)
        slot = lax.rem(my_chip - owner // 2 + chips, chips)
        return remote(
            part.at[b, c], got.at[slot, at, c], r_send.at[b, c], r_recv.at[slot, at, c],
            {"head": owner},
        )

    def term_arrival(b, c, slot):
        at = lax.rem(b, per_head)
        return remote(
            part.at[b, c], got.at[slot, at, c], r_send.at[b, c], r_recv.at[slot, at, c],
            {"head": partner},
        )

    in_copies = [
        pltpu.make_async_copy(src, dst, in_sem.at[i])
        for i, (src, dst) in enumerate(
            ((keep_hbm, keep_own), (q_ref, q_own), (k_ref, k_all.at[t]), (v_ref, v_all.at[t]))
        )
    ]

    gate_copy = pltpu.make_async_copy(gate_hbm, gate_ref, gate_sem.at[0])

    @pl.when(outer)
    def _():
        for h in range(head_count):
            for which in range(2):
                kv_first(h, which, mate_id).start()
        keep_copy.start()
        for h in range(head_count):
            q_copy(h).start()

    @pl.when(inner)
    def _():
        for h in range(head_count):
            for which in range(2):
                kv_first(h, which, mid_id).start()
        for copy in in_copies:
            copy.start()

    for c in range(pieces):
        for s in range(halves):
            first_send(c, s, 0).start()
        @pl.when(outer)
        def _(c=c):
            for s in range(halves):
                for o in range(1, groups):
                    rest_send(c, s, o).start()
    for c in range(pieces):
        own_copy(c).start()
    gate_copy.start()

    def block_of(k):
        place = jnp.where(left, t, n - 1 - t)
        b = jnp.where(k == 0, place, jnp.where(k == 1, 1 - place, k))
        return jnp.where(left, b, n - 1 - b)

    def pass_on(j):
        b, c = block_of(j // pieces), lax.rem(j, pieces)
        for s in range(halves):
            relay(b, c, s, 0).wait_recv()
            @pl.when(inner & (b == end))
            def _(s=s):
                relay(b, c, s, 1).start()
            @pl.when(inner & (b != end))
            def _(s=s):
                relay(b, c, s, 0).start()
            @pl.when(outer | (b != end))
            def _(s=s):
                for o in range(1, groups):
                    across(b, c, s, o).start()

    scale = math.log2(math.e) / math.sqrt(HD)
    reach_slabs = keep_own.shape[1] // per_slab

    def set_bias(at, ref):
        kept = ref[...]
        spread = jnp.concatenate(
            [jnp.broadcast_to(kept[:, c:c + 1], (per_slab, TILE)) for c in range(kept.shape[1])],
            axis=1,
        )
        bias[at] = jnp.where(spread > 0, 0.0, -jnp.inf).astype(jnp.float32)

    def attend(h, slab, queries, at, dst):
        for i in range(per_slab):
            q = queries[h, i * TILE:(i + 1) * TILE, :]
            scores = []
            for j in range(reach_slabs):
                other = lax.rem(slab + j - reach_slabs // 2 + n, n)
                s = lax.dot_general(
                    q, k_all[other, h], (((1,), (1,)), ((), ())),
                    preferred_element_type=jnp.float32,
                )
                scores.append(s * scale + bias[at, i:i + 1, j * tokens:(j + 1) * tokens])
            peak = functools.reduce(
                jnp.maximum, [jnp.max(s, axis=1, keepdims=True) for s in scores]
            )
            exps = [jnp.exp2(s - peak) for s in scores]
            total = functools.reduce(jnp.add, [jnp.sum(e, axis=1, keepdims=True) for e in exps])
            acc = None
            for j in range(reach_slabs):
                other = lax.rem(slab + j - reach_slabs // 2 + n, n)
                term = jnp.dot(
                    exps[j].astype(jnp.bfloat16), v_all[other, h],
                    preferred_element_type=jnp.float32,
                )
                acc = term if acc is None else acc + term
            dst[i * TILE:(i + 1) * TILE, lanes_of(h)] = (acc * (1.0 / total)).astype(jnp.bfloat16)

    def project(b, c):
        def tile(i, carry):
            at = pl.ds(pl.multiple_of(i * TILE, TILE), TILE)
            part[b, c, at, :] = jnp.dot(
                attended[at, :], w_all[b, c], preferred_element_type=jnp.float32
            ).astype(jnp.bfloat16)
            return carry

        lax.fori_loop(0, tokens // TILE, tile, 0)
        owner = b // per_head
        @pl.when(owner == partner)
        def _():
            partner_send(b, c).start()
        @pl.when((owner // 2 != my_chip) & (lax.rem(owner, 2) != my_core))
        def _():
            give_send(b, c).start()

    def collect(j):
        b, c = block_of(j // pieces), lax.rem(j, pieces)
        owner, at = b // per_head, lax.rem(b, per_head)
        @pl.when((owner // 2 != my_chip) & (lax.rem(owner, 2) == my_core))
        def _():
            give_send(b, c).wait_recv()

            def tile(i, carry):
                now = pl.ds(pl.multiple_of(i * TILE, TILE), TILE)
                part[b, c, now, :] = (
                    part[b, c, now, :].astype(jnp.float32)
                    + pair[owner // 2, at, c, now, :].astype(jnp.float32)
                ).astype(jnp.bfloat16)
                return carry

            lax.fori_loop(0, tokens // TILE, tile, 0)
            sum_send(b, c).start()

    def use(j):
        b, c = block_of(j // pieces), lax.rem(j, pieces)
        for s in range(halves):
            for o in range(1, groups):
                across_arrival(b, c, s, o).wait_recv()
        project(b, c)

    def settle(b, c, at_rows, first=0, past=wide):
        cb = lax.rem(b, per_head)
        span = gate_ref.shape[1]
        for u in range(first // span, past // span):
            lanes = slice(u * span, (u + 1) * span)
            summed = part[b, c, at_rows, lanes].astype(jnp.float32)
            for slot in range(chips):
                summed = summed + got[slot, cb, c, at_rows, lanes].astype(jnp.float32)
            block = cb * (cols // span) + c * (wide // span) + u
            at = pl.ds(pl.multiple_of(block * span, span), span)
            out_ref[at_rows, at] = (gate_ref[pl.ds(block, 1), :] * summed).astype(out_ref.dtype)

    def finish(j):
        b, c = block_of(j // pieces), lax.rem(j, pieces)
        @pl.when(b // per_head == me)
        def _():
            for slot in range(chips):
                term_arrival(b, c, slot).wait_recv()
            settle(b, c, slice(0, tokens))

    last_b, last_c = block_of(n - 1), pieces - 1
    last_owner, last_at = last_b // per_head, lax.rem(last_b, per_head)
    other_chip = last_owner // 2 != my_chip
    same_core = lax.rem(last_owner, 2) == my_core

    def tile_send(i, s, dst, recv, device):
        now = slice(i * TILE, (i + 1) * TILE)
        return remote(
            part.at[last_b, last_c, now, lanes_in(s)], dst.at[last_at, last_c, now, lanes_in(s)],
            t_send.at[s, i], recv, device,
        )

    def to_partner(i, s):
        return tile_send(i, s, got.at[0], t_recv.at[0, s, i], {"head": partner})

    def to_collector(i, s):
        return tile_send(i, s, pair.at[last_owner // 2], t_pair.at[s, i], {"head": partner})

    def to_owner(i, s):
        slot = lax.rem(my_chip - last_owner // 2 + chips, chips)
        return tile_send(i, s, got.at[slot], t_recv.at[slot, s, i], {"head": last_owner})

    def tile_arrival(i, s, slot):
        return tile_send(i, s, got.at[slot], t_recv.at[slot, s, i], {"head": partner})

    def last_terms(s):
        lanes = lanes_in(s)
        if s < halves - 1:
            for o in range(1, groups):
                across_arrival(last_b, last_c, s, o).wait_recv()
        for i in range(per_slab):
            now = slice(i * TILE, (i + 1) * TILE)
            part[last_b, last_c, now, lanes] = jnp.dot(
                attended[now, :], w_all[last_b, last_c, :, lanes],
                preferred_element_type=jnp.float32,
            ).astype(jnp.bfloat16)
            @pl.when(last_owner == partner)
            def _(i=i):
                to_partner(i, s).start()
            @pl.when(other_chip & jnp.logical_not(same_core))
            def _(i=i):
                to_collector(i, s).start()

    def last_collect(s):
        lanes = lanes_in(s)
        @pl.when(other_chip & same_core)
        def _():
            for i in range(per_slab):
                now = slice(i * TILE, (i + 1) * TILE)
                to_collector(i, s).wait_recv()
                part[last_b, last_c, now, lanes] = (
                    part[last_b, last_c, now, lanes].astype(jnp.float32)
                    + pair[last_owner // 2, last_at, last_c, now, lanes].astype(jnp.float32)
                ).astype(jnp.bfloat16)
                to_owner(i, s).start()

    def last_finish():
        lax.fori_loop(0, total_pieces - 1, do_finish, 0)
        @pl.when(last_owner == me)
        def _():
            for s in range(halves):
                for i in range(per_slab):
                    for slot in range(chips):
                        tile_arrival(i, s, slot).wait_recv()
                    settle(
                        last_b, last_c, slice(i * TILE, (i + 1) * TILE),
                        s * sub_cols, (s + 1) * sub_cols,
                    )

    def do_use(j, carry):
        use(j)
        collect(j - 1)
        return carry

    def do_finish(j, carry):
        finish(j)
        return carry

    def own_block(c, carry):
        project(t, c)
        @pl.when(c > 0)
        def _():
            collect(c - 1)
        return carry

    @pl.when(inner)
    def _():
        for copy in in_copies:
            copy.wait()
        set_bias(0, keep_own)

        def own_slab(h, carry):
            for which in range(2):
                kv_arrival(end, h, which).wait_recv()
                kv_relay(h, which).start()
            for which in range(2):
                kv_arrival(across_mid, h, which).wait_recv()
            attend(h, t, q_own, 0, attended)
            return carry

        lax.fori_loop(0, head_count, own_slab, 0)
        for c in range(pieces):
            for s in range(halves):
                first_send(c, s, 1).start()
        for c in range(pieces):
            own_copy(c).wait()
        lax.fori_loop(0, pieces, own_block, 0)
        keep_copy.wait_recv()
        set_bias(1, keep_far)

        def end_slab(h, carry):
            q_copy(h).wait_recv()
            for which in range(2):
                kv_arrival(far_end, h, which).wait_recv()
            attend(h, end, q_far, 1, far_att)
            att_copy(h).start()
            return carry

        lax.fori_loop(0, head_count, end_slab, 0)

    def early_pass(j, carry):
        pass_on(j)
        return carry

    @pl.when(outer)
    def _():
        lax.fori_loop(pieces, 2 * pieces, early_pass, 0)
        for c in range(pieces):
            own_copy(c).wait()
        for h in range(head_count):
            att_copy(h).wait_recv()
        lax.fori_loop(0, pieces, own_block, 0)

    @pl.when(outer)
    def _():
        lax.fori_loop(pieces, 2 * pieces, do_use, 0)

    def used_by(j):
        lagging = jnp.maximum(jnp.maximum(j - pieces - 1, 3 * j - 7 * pieces - 1), pieces)
        return jnp.where(inner, jnp.minimum(lagging, j - 1), jnp.maximum(j - 1, 2 * pieces))

    def step(j, carry):
        pass_on(j)
        @pl.when(inner & (j < 3 * pieces))
        def _():
            pass_on(j - pieces)
        return lax.fori_loop(used_by(j - 1), used_by(j), do_use, carry)

    lax.fori_loop(2 * pieces, total_pieces - 2, step, 0)
    pass_on(total_pieces - 2)

    @pl.when(inner)
    def _():
        for o in range(1, groups):
            theirs_on(end, o, mid_id).start()
    until = jnp.where(inner, total_pieces - 3, total_pieces - 2)
    lax.fori_loop(used_by(total_pieces - 3), until, do_use, 0)
    for s in range(halves):
        relay(last_b, last_c, s, 0).wait_recv()
        @pl.when(inner)
        def _(s=s):
            relay(last_b, last_c, s, 0).start()
        if s < halves - 1:
            for o in range(1, groups):
                across(last_b, last_c, s, o).start()
    for o in range(1, groups):
        across_arrival(last_b, last_c, halves - 1, o).wait_recv()
        @pl.when(inner)
        def _(o=o):
            theirs_on(last_b, o, mate_id).start()
    lax.fori_loop(until, total_pieces - 2, do_use, 0)
    use(total_pieces - 2)
    collect(total_pieces - 3)
    for s in range(halves):
        last_terms(s)
        if s == 0:
            collect(total_pieces - 2)
        last_collect(s)
    gate_copy.wait()
    last_finish()

    @pl.when(outer)
    def _():
        for h in range(head_count):
            for which in range(2):
                kv_first(h, which, mate_id).wait_send()
            q_copy(h).wait_send()
        keep_copy.wait_send()

    @pl.when(inner)
    def _():
        for h in range(head_count):
            for which in range(2):
                kv_first(h, which, mid_id).wait_send()
                kv_relay(h, which).wait_send()
            att_copy(h).wait_send()
        for c in range(pieces):
            for s in range(halves):
                first_send(c, s, 1).wait_send()

    @pl.when(last_owner != me)
    def _():
        for s in range(halves):
            for i in range(per_slab):
                to_partner(i, s).wait_send()

    def drain(b, carry):
        for c in range(pieces):
            for s in range(halves):
                @pl.when(b == t)
                def _(c=c, s=s):
                    first_send(c, s, 0).wait_send()
                @pl.when((b == t) & outer)
                def _(c=c, s=s):
                    for o in range(1, groups):
                        rest_send(c, s, o).wait_send()
                last_part = c == pieces - 1 and s == halves - 1
                sent = (b != t) & (outer | (b != end))
                if last_part:
                    sent = ((b != t) & (b != last_b)) | (inner & (b == last_b))
                @pl.when(sent)
                def _(c=c, s=s):
                    for o in range(1, groups):
                        across(b, c, s, o).wait_send()
                @pl.when(inner & (b == end))
                def _(c=c, s=s):
                    relay(b, c, s, 1).wait_send()
                @pl.when(inner & (b != end) & (b != t))
                def _(c=c, s=s):
                    relay(b, c, s, 0).wait_send()
            @pl.when((b // per_head != me) & ((b != last_b) | (c != last_c)))
            def _(c=c):
                partner_send(b, c).wait_send()
        return carry

    lax.fori_loop(0, n, drain, 0)


def chain_shards(queries, key_rows, value_rows, keep_tiles, out_weight, gate_scale):
    n, heads, groups = lax.axis_size("tm"), lax.axis_size("head"), lax.axis_size("groups")
    tokens = queries.shape[0]
    head_count = queries.shape[1]
    flat = head_count * HD
    rows, cols = out_weight.shape
    pieces = cols // 256 if cols % 256 == 0 else 1
    wide = cols // pieces
    per_head = n // heads
    if pieces < 4:
        return shards(queries, key_rows, value_rows, keep_tiles, out_weight, gate_scale)
    gate_lanes = 128 if wide % 128 == 0 else wide
    vmem = pl.BlockSpec(memory_space=pltpu.VMEM)
    hbm = pl.BlockSpec(memory_space=pl.ANY)
    dma = pltpu.SemaphoreType.DMA
    bf16 = jnp.bfloat16
    return pl.pallas_call(
        functools.partial(chain_kernel, (groups, n, heads, pieces)),
        out_shape=pltpu.VMEM((tokens, gate_scale.shape[0]), bf16),
        in_specs=[hbm, hbm, hbm, hbm, hbm, hbm],
        out_specs=vmem,
        scratch_shapes=[
            pltpu.VMEM((head_count, tokens, HD), bf16),
            pltpu.VMEM((head_count, tokens, HD), bf16),
            pltpu.VMEM((n, head_count, tokens, HD), bf16),
            pltpu.VMEM((n, head_count, tokens, HD), bf16),
            pltpu.VMEM((n, pieces, rows, wide), bf16),
            pltpu.VMEM((tokens, flat), bf16),
            pltpu.VMEM((tokens, flat), bf16),
            pltpu.VMEM((n, pieces, tokens, wide), bf16),
            pltpu.VMEM((heads // 2, per_head, pieces, tokens, wide), bf16),
            pltpu.VMEM((heads // 2, per_head, pieces, tokens, wide), bf16),
            pltpu.VMEM(keep_tiles.shape, jnp.int32),
            pltpu.VMEM(keep_tiles.shape, jnp.int32),
            pltpu.VMEM((gate_scale.shape[0] // gate_lanes, gate_lanes), jnp.float32),
            pltpu.VMEM((2, keep_tiles.shape[0], keep_tiles.shape[1] * TILE), jnp.float32),
            dma((2, 2, head_count)),
            dma((n, 2, head_count)),
            dma((head_count,)),
            dma((head_count,)),
            dma((2,)),
            dma((head_count,)),
            dma((head_count,)),
            dma((2, n, pieces, 2)),
            dma((n, pieces, 2)),
            dma((groups - 1, n, pieces, 2)),
            dma((groups - 1, n, pieces, 2)),
            dma((n, pieces)),
            dma((heads // 2, per_head, pieces)),
            dma((heads // 2, per_head, pieces)),
            dma((2, tokens // TILE)),
            dma((heads // 2, 2, tokens // TILE)),
            dma((2, tokens // TILE)),
            dma((pieces,)),
            dma((4,)),
            dma((1,)),
        ],
        compiler_params=pltpu.CompilerParams(
            collective_id=0, has_side_effects=True, vmem_limit_bytes=56 * 1024 * 1024
        ),
    )(
        queries.transpose(1, 0, 2),
        key_rows.transpose(1, 0, 2),
        value_rows.transpose(1, 0, 2),
        keep_tiles,
        out_weight,
        gate_scale.reshape(-1, gate_lanes),
    )


def solution(mesh):
    placed = (
        P(("groups", "tm"), "head", None),
        P(("groups", "tm"), "head", None),
        P(("groups", "tm"), "head", None),
        P(("groups", "tm"), None),
        P("head", "tm"),
        P(("groups", "head")),
    )
    n, heads = mesh.shape["tm"], mesh.shape["head"]
    chain = n == 4 and n % heads == 0 and heads % 2 == 0 and mesh.shape["groups"] > 1
    body = chain_shards if chain else shards
    return jax.shard_map(
        body, mesh=mesh, in_specs=placed, out_specs=P(("groups", "tm"), "head"), check_vma=False
    )
```

```python
import functools
import math

import jax
import jax.numpy as jnp
from jax import lax
from jax.experimental import pallas as pl
from jax.experimental.pallas import tpu as pltpu
from jax.sharding import PartitionSpec as P

HD = 128
TILE = 128
MESH = pl.DeviceIdType.MESH


def layer_kernel(
    sizes, q_ref, k_ref, v_ref, keep_ref, w_ref, gate_ref, out_ref,
    q_own, k_all, v_all, w_all, attended, part, got,
    kv_send, kv_recv, z_send, z_recv, y_send, y_recv, r_send, r_recv, own_sem, in_sem,
):
    groups, n, heads, reach, pieces = sizes
    g, t, me = lax.axis_index("groups"), lax.axis_index("tm"), lax.axis_index("head")
    rows, cols = w_ref.shape
    wide = cols // pieces
    per_head = n // heads
    part_rows = rows // groups
    head_count, tokens = q_ref.shape[0], q_ref.shape[1]
    slabs = 2 * reach + 1

    barrier = pltpu.get_barrier_semaphore()
    partners = []
    for d in range(1, reach + 1):
        partners += [{"tm": lax.rem(t + d, n)}, {"tm": lax.rem(t + n - d, n)}]
    for o in range(1, groups):
        partners.append({"groups": lax.rem(g + o, groups)})
    for o in range(1, heads):
        partners.append({"head": lax.rem(me + o, heads)})
    for partner in partners:
        pl.semaphore_signal(barrier, inc=1, device_id=partner, device_id_type=MESH)
    pl.semaphore_wait(barrier, len(partners))

    def remote(src, dst, send, recv, device):
        return pltpu.make_async_remote_copy(
            src_ref=src, dst_ref=dst, send_sem=send, recv_sem=recv,
            device_id=device, device_id_type=MESH,
        )

    kv_copies = []
    for d in range(1, reach + 1):
        for slot, to in ((reach - d, lax.rem(t + d, n)), (reach + d, lax.rem(t + n - d, n))):
            for which, (src, dst) in enumerate(((k_ref, k_all), (v_ref, v_all))):
                kv_copies.append(
                    remote(src, dst.at[slot], kv_send.at[slot, which], kv_recv.at[slot, which], {"tm": to})
                )
    @pl.when(t == 0)
    def _():
        for copy in reversed(kv_copies):
            copy.start()

    @pl.when(t != 0)
    def _():
        for copy in kv_copies:
            copy.start()

    in_copies = [
        pltpu.make_async_copy(src, dst, in_sem.at[i])
        for i, (src, dst) in enumerate(
            ((q_ref, q_own), (k_ref, k_all.at[reach]), (v_ref, v_all.at[reach]))
        )
    ]
    for copy in in_copies:
        copy.start()

    my_rows = pl.ds(pl.multiple_of(g * part_rows, part_rows), part_rows)

    def own_copy(c):
        return pltpu.make_async_copy(
            w_ref.at[:, c * wide:(c + 1) * wide], w_all.at[t, c], own_sem.at[c]
        )

    def first_send(c, side):
        to = jnp.minimum(t + 1, n - 1) if side else jnp.maximum(t - 1, 0)
        return remote(
            w_ref.at[my_rows, c * wide:(c + 1) * wide], w_all.at[t, c, my_rows],
            z_send.at[side, t, c], z_recv.at[t, c], {"tm": to},
        )

    def relay(b, c, side):
        to = jnp.minimum(t + 1, n - 1) if side else jnp.maximum(t - 1, 0)
        return remote(
            w_all.at[b, c, my_rows], w_all.at[b, c, my_rows],
            z_send.at[side, b, c], z_recv.at[b, c], {"tm": to},
        )

    def across(b, c, o):
        return remote(
            w_all.at[b, c, my_rows], w_all.at[b, c, my_rows],
            y_send.at[o - 1, b, c], y_recv.at[o - 1, b, c],
            {"groups": lax.rem(g + o, groups)},
        )

    def across_arrival(b, c, o):
        sender = lax.rem(g + groups - o, groups)
        their_rows = pl.ds(pl.multiple_of(sender * part_rows, part_rows), part_rows)
        return remote(
            w_all.at[b, c, their_rows], w_all.at[b, c, their_rows],
            y_send.at[o - 1, b, c], y_recv.at[o - 1, b, c],
            {"groups": lax.rem(g + o, groups)},
        )

    def term_send(b, c, o):
        return remote(
            part.at[b, c], got.at[o - 1, b % per_head, c],
            r_send.at[b, c], r_recv.at[o - 1, b % per_head, c],
            {"head": lax.rem(me + o, heads)},
        )

    for c in range(pieces):
        own_copy(c).start()
        @pl.when(t < n - 1)
        def _(c=c):
            first_send(c, 1).start()
        @pl.when(t > 0)
        def _(c=c):
            first_send(c, 0).start()

    for copy in in_copies:
        copy.wait()
    for copy in kv_copies:
        copy.wait_recv()

    scale = 1.0 / math.sqrt(HD)
    per_slab = tokens // TILE

    early = min(pieces, head_count - 1)

    def pass_on(j, side):
        step, c = j // pieces, j % pieces
        b = (t - 1 - step) if side else (t + 1 + step)
        @pl.when((b >= 0) & (b <= n - 1))
        def _():
            relay(b, c, side).wait_recv()
            @pl.when((t < n - 1) if side else (t > 0))
            def _():
                relay(b, c, side).start()
            for o in range(1, groups):
                across(b, c, o).start()

    def one_head(h, carry):
        lanes = pl.ds(pl.multiple_of(h * HD, HD), HD)
        for i in range(per_slab):
            q = q_own[h, i * TILE:(i + 1) * TILE, :]
            scores = []
            for j in range(slabs):
                s = lax.dot_general(
                    q, k_all[j, h], (((1,), (1,)), ((), ())), preferred_element_type=jnp.float32
                )
                bias = jnp.concatenate(
                    [
                        jnp.full(
                            (1, TILE),
                            jnp.where(keep_ref[i, j * per_slab + u] > 0, 0.0, -jnp.inf),
                            jnp.float32,
                        )
                        for u in range(per_slab)
                    ],
                    axis=1,
                )
                scores.append(s * scale + bias)
            peak = functools.reduce(
                jnp.maximum, [jnp.max(s, axis=1, keepdims=True) for s in scores]
            )
            exps = [jnp.exp(s - peak) for s in scores]
            total = functools.reduce(jnp.add, [jnp.sum(e, axis=1, keepdims=True) for e in exps])
            inverse = 1.0 / total
            acc = None
            for j in range(slabs):
                term = jnp.dot(
                    (exps[j] * inverse).astype(jnp.bfloat16), v_all[j, h],
                    preferred_element_type=jnp.float32,
                )
                acc = term if acc is None else acc + term
            attended[i * TILE:(i + 1) * TILE, lanes] = acc.astype(jnp.bfloat16)
        @pl.when(h >= head_count - early)
        def _():
            for side in (1, 0):
                pass_on(h - (head_count - early), side)
        return carry

    lax.fori_loop(0, head_count, one_head, 0)

    def project(b, c):
        def tile(i, carry):
            at = pl.ds(pl.multiple_of(i * TILE, TILE), TILE)
            part[b, c, at, :] = jnp.dot(
                attended[at, :], w_all[b, c], preferred_element_type=jnp.float32
            ).astype(jnp.bfloat16)
            return carry

        lax.fori_loop(0, tokens // TILE, tile, 0)
        owner = b // per_head
        for o in range(1, heads):
            @pl.when(owner == lax.rem(me + o, heads))
            def _():
                term_send(b, c, o).start()

    for c in range(pieces):
        own_copy(c).wait()
        project(t, c)

    def use(j, side):
        step, c = j // pieces, j % pieces
        b = (t - 1 - step) if side else (t + 1 + step)
        @pl.when((b >= 0) & (b <= n - 1))
        def _():
            for o in range(1, groups):
                across_arrival(b, c, o).wait_recv()
            project(b, c)

    count = (n - 1) * pieces

    def use_both(j, carry):
        for side in (1, 0):
            use(j, side)
        return carry

    def step(j, carry):
        for side in (1, 0):
            pass_on(j, side)
        first = jnp.minimum(2 * (j - early), j - 1)
        last = jnp.minimum(2 * (j - early) + 2, j)
        return lax.fori_loop(first, last, use_both, carry)

    lax.fori_loop(early, count, step, 0)
    lax.fori_loop(min(2 * (count - early), count - 1), count, use_both, 0)

    for cb in range(per_head):
        for c in range(pieces):
            b = me * per_head + cb
            for o in range(1, heads):
                term_send(b, c, o).wait_recv()
            span = wide if gate_ref.shape[0] == 1 else gate_ref.shape[1]
            for u in range(wide // span):
                lanes = slice(u * span, (u + 1) * span)
                summed = part[b, c, :, lanes].astype(jnp.float32)
                for o in range(1, heads):
                    summed = summed + got[o - 1, cb, c, :, lanes].astype(jnp.float32)
                at = cb * cols + c * wide + u * span
                gate = gate_ref[:, at:at + span] if span == wide else gate_ref[at // span:at // span + 1, :]
                out_ref[:, at:at + span] = (gate * summed).astype(out_ref.dtype)

    for copy in kv_copies:
        copy.wait_send()
    for c in range(pieces):
        @pl.when(t < n - 1)
        def _(c=c):
            first_send(c, 1).wait_send()
        @pl.when(t > 0)
        def _(c=c):
            first_send(c, 0).wait_send()

    def drain(b, carry):
        for c in range(pieces):
            @pl.when(b != t)
            def _(c=c):
                for o in range(1, groups):
                    across(b, c, o).wait_send()
            @pl.when((b < t) & (t < n - 1))
            def _(c=c):
                relay(b, c, 1).wait_send()
            @pl.when((b > t) & (t > 0))
            def _(c=c):
                relay(b, c, 0).wait_send()
            @pl.when(b // per_head != me)
            def _(c=c):
                term_send(b, c, 1).wait_send()
        return carry

    lax.fori_loop(0, n, drain, 0)


def shards(queries, key_rows, value_rows, keep_tiles, out_weight, gate_scale):
    n, heads, groups = lax.axis_size("tm"), lax.axis_size("head"), lax.axis_size("groups")
    reach = min(2, (n - 1) // 2)
    tokens = queries.shape[0]
    head_count = queries.shape[1]
    flat = head_count * HD
    rows, cols = out_weight.shape
    pieces = cols // 256 if cols % 256 == 0 else 1
    wide = cols // pieces
    per_head = n // heads
    slabs = 2 * reach + 1
    gate_lanes = 128 if wide % 128 == 0 else gate_scale.shape[0]
    vmem = pl.BlockSpec(memory_space=pltpu.VMEM)
    hbm = pl.BlockSpec(memory_space=pl.ANY)
    dma = pltpu.SemaphoreType.DMA
    bf16 = jnp.bfloat16
    return pl.pallas_call(
        functools.partial(layer_kernel, (groups, n, heads, reach, pieces)),
        out_shape=jax.ShapeDtypeStruct((tokens, gate_scale.shape[0]), bf16),
        in_specs=[hbm, hbm, hbm, pl.BlockSpec(memory_space=pltpu.SMEM), hbm, vmem],
        out_specs=vmem,
        scratch_shapes=[
            pltpu.VMEM((head_count, tokens, HD), bf16),
            pltpu.VMEM((slabs, head_count, tokens, HD), bf16),
            pltpu.VMEM((slabs, head_count, tokens, HD), bf16),
            pltpu.VMEM((n, pieces, rows, wide), bf16),
            pltpu.VMEM((tokens, flat), bf16),
            pltpu.VMEM((n, pieces, tokens, wide), bf16),
            pltpu.VMEM((heads - 1, per_head, pieces, tokens, wide), bf16),
            dma((slabs, 2)),
            dma((slabs, 2)),
            dma((2, n, pieces)),
            dma((n, pieces)),
            dma((groups - 1, n, pieces)),
            dma((groups - 1, n, pieces)),
            dma((n, pieces)),
            dma((heads - 1, per_head, pieces)),
            dma((pieces,)),
            dma((3,)),
        ],
        compiler_params=pltpu.CompilerParams(
            collective_id=0, has_side_effects=True, vmem_limit_bytes=56 * 1024 * 1024
        ),
    )(
        queries.transpose(1, 0, 2),
        key_rows.transpose(1, 0, 2),
        value_rows.transpose(1, 0, 2),
        keep_tiles,
        out_weight,
        gate_scale.reshape(-1, gate_lanes),
    )


def chain_kernel(
    sizes, q_ref, k_ref, v_ref, keep_hbm, w_ref, gate_hbm, out_ref,
    q_own, q_far, k_all, v_all, w_all, attended, far_att, part, got, pair, keep_own, keep_far, gate_ref, bias,
    kv_send, kv_recv, q_send, q_recv, keep_sem, att_send, att_recv,
    z_send, z_recv, y_send, y_recv, r_send, r_recv, pair_recv, t_send, t_recv, t_pair, own_sem, in_sem, gate_sem,
):
    groups, n, heads, pieces = sizes
    g, t, me = lax.axis_index("groups"), lax.axis_index("tm"), lax.axis_index("head")
    rows, cols = w_ref.shape
    wide = cols // pieces
    per_head = n // heads
    part_rows = rows // groups
    halves = 2
    sub_cols = wide // halves
    head_count, tokens = q_ref.shape[0], q_ref.shape[1]
    per_slab = tokens // TILE
    total_pieces = n * pieces
    chips = heads // 2
    my_chip, my_core = me // 2, lax.rem(me, 2)
    partner = me + 1 - 2 * my_core

    left = t < n // 2
    inner = (t > 0) & (t < n - 1)
    outer = jnp.logical_not(inner)
    end = jnp.where(left, 0, n - 1)
    near = jnp.where(left, 1, n - 2)
    across_mid = n - 1 - t
    far_end = n - 1 - end
    mate = jnp.where(inner, end, near)
    mate_id = {"tm": mate}
    mid_id = {"tm": across_mid}

    barrier = pltpu.get_barrier_semaphore()

    def greet(partner):
        pl.semaphore_signal(barrier, inc=1, device_id=partner, device_id_type=MESH)

    greet(mate_id)
    @pl.when(inner)
    def _():
        greet(mid_id)
    for o in range(1, groups):
        greet({"groups": lax.rem(g + o, groups)})
    for o in range(1, heads):
        greet({"head": lax.rem(me + o, heads)})
    @pl.when(inner)
    def _():
        pl.semaphore_wait(barrier, groups + heads)
    @pl.when(outer)
    def _():
        pl.semaphore_wait(barrier, groups + heads - 1)

    def remote(src, dst, send, recv, device):
        return pltpu.make_async_remote_copy(
            src_ref=src, dst_ref=dst, send_sem=send, recv_sem=recv,
            device_id=device, device_id_type=MESH,
        )

    kv = ((k_ref, k_all), (v_ref, v_all))

    def kv_first(h, which, device):
        src, dst = kv[which]
        return remote(
            src.at[h], dst.at[t, h], kv_send.at[0, which, h], kv_recv.at[t, which, h], device
        )

    def kv_relay(h, which):
        buf = kv[which][1]
        return remote(
            buf.at[end, h], buf.at[end, h], kv_send.at[1, which, h], kv_recv.at[end, which, h],
            mid_id,
        )

    def kv_arrival(slab, h, which):
        buf = kv[which][1]
        return remote(
            buf.at[slab, h], buf.at[slab, h], kv_send.at[1, which, h],
            kv_recv.at[slab, which, h], mid_id,
        )

    def q_copy(h):
        return remote(q_ref.at[h], q_far.at[h], q_send.at[h], q_recv.at[h], mate_id)

    keep_copy = remote(keep_hbm, keep_far, keep_sem.at[0], keep_sem.at[1], mate_id)

    def lanes_of(h):
        return pl.ds(pl.multiple_of(h * HD, HD), HD)

    def att_copy(h):
        return remote(
            far_att.at[:, lanes_of(h)], attended.at[:, lanes_of(h)],
            att_send.at[h], att_recv.at[h], mate_id,
        )

    def rows_of(sender):
        return pl.ds(pl.multiple_of(sender * part_rows, part_rows), part_rows)

    def lanes_in(s, c=0):
        return slice(c * wide + s * sub_cols, c * wide + (s + 1) * sub_cols)

    def own_copy(c):
        return pltpu.make_async_copy(
            w_ref.at[:, c * wide:(c + 1) * wide], w_all.at[t, c], own_sem.at[c]
        )

    def first_send(c, s, way):
        mine = rows_of(g)
        return remote(
            w_ref.at[mine, lanes_in(s, c)], w_all.at[t, c, mine, lanes_in(s)],
            z_send.at[way, t, c, s], z_recv.at[t, c, s], mid_id if way else mate_id,
        )

    def rest_send(c, s, o):
        theirs = rows_of(lax.rem(g + groups - o, groups))
        return remote(
            w_ref.at[theirs, lanes_in(s, c)], w_all.at[t, c, theirs, lanes_in(s)],
            y_send.at[o - 1, t, c, s], y_recv.at[o - 1, t, c, s], mate_id,
        )

    def relay(b, c, s, way):
        mine = rows_of(g)
        return remote(
            w_all.at[b, c, mine, lanes_in(s)], w_all.at[b, c, mine, lanes_in(s)],
            z_send.at[way, b, c, s], z_recv.at[b, c, s], mid_id if way else mate_id,
        )

    def across(b, c, s, o):
        mine = rows_of(g)
        return remote(
            w_all.at[b, c, mine, lanes_in(s)], w_all.at[b, c, mine, lanes_in(s)],
            y_send.at[o - 1, b, c, s], y_recv.at[o - 1, b, c, s],
            {"groups": lax.rem(g + o, groups)},
        )

    def theirs_on(b, o, device):
        c, s = pieces - 1, halves - 1
        theirs = rows_of(lax.rem(g + groups - o, groups))
        return remote(
            w_all.at[b, c, theirs, lanes_in(s)], w_all.at[b, c, theirs, lanes_in(s)],
            y_send.at[o - 1, b, c, s], y_recv.at[o - 1, b, c, s], device,
        )

    def across_arrival(b, c, s, o):
        theirs = rows_of(lax.rem(g + groups - o, groups))
        return remote(
            w_all.at[b, c, theirs, lanes_in(s)], w_all.at[b, c, theirs, lanes_in(s)],
            y_send.at[o - 1, b, c, s], y_recv.at[o - 1, b, c, s],
            {"groups": lax.rem(g + o, groups)},
        )

    def partner_send(b, c):
        at = lax.rem(b, per_head)
        return remote(
            part.at[b, c], got.at[0, at, c], r_send.at[b, c], r_recv.at[0, at, c],
            {"head": partner},
        )

    def give_send(b, c):
        owner, at = b // per_head, lax.rem(b, per_head)
        return remote(
            part.at[b, c], pair.at[owner // 2, at, c], r_send.at[b, c],
            pair_recv.at[owner // 2, at, c], {"head": partner},
        )

    def sum_send(b, c):
        owner, at = b // per_head, lax.rem(b, per_head)
        slot = lax.rem(my_chip - owner // 2 + chips, chips)
        return remote(
            part.at[b, c], got.at[slot, at, c], r_send.at[b, c], r_recv.at[slot, at, c],
            {"head": owner},
        )

    def term_arrival(b, c, slot):
        at = lax.rem(b, per_head)
        return remote(
            part.at[b, c], got.at[slot, at, c], r_send.at[b, c], r_recv.at[slot, at, c],
            {"head": partner},
        )

    in_copies = [
        pltpu.make_async_copy(src, dst, in_sem.at[i])
        for i, (src, dst) in enumerate(
            ((keep_hbm, keep_own), (q_ref, q_own), (k_ref, k_all.at[t]), (v_ref, v_all.at[t]))
        )
    ]

    gate_copy = pltpu.make_async_copy(gate_hbm, gate_ref, gate_sem.at[0])

    @pl.when(outer)
    def _():
        for h in range(head_count):
            for which in range(2):
                kv_first(h, which, mate_id).start()
        keep_copy.start()
        for h in range(head_count):
            q_copy(h).start()

    @pl.when(inner)
    def _():
        for h in range(head_count):
            for which in range(2):
                kv_first(h, which, mid_id).start()
        for copy in in_copies:
            copy.start()

    for c in range(pieces):
        for s in range(halves):
            first_send(c, s, 0).start()
        @pl.when(outer)
        def _(c=c):
            for s in range(halves):
                for o in range(1, groups):
                    rest_send(c, s, o).start()
    for c in range(pieces):
        own_copy(c).start()
    gate_copy.start()

    def block_of(k):
        place = jnp.where(left, t, n - 1 - t)
        b = jnp.where(k == 0, place, jnp.where(k == 1, 1 - place, k))
        return jnp.where(left, b, n - 1 - b)

    def pass_on(j):
        b, c = block_of(j // pieces), lax.rem(j, pieces)
        for s in range(halves):
            relay(b, c, s, 0).wait_recv()
            @pl.when(inner & (b == end))
            def _(s=s):
                relay(b, c, s, 1).start()
            @pl.when(inner & (b != end))
            def _(s=s):
                relay(b, c, s, 0).start()
            @pl.when(outer | (b != end))
            def _(s=s):
                for o in range(1, groups):
                    across(b, c, s, o).start()

    scale = math.log2(math.e) / math.sqrt(HD)
    reach_slabs = keep_own.shape[1] // per_slab

    def set_bias(at, ref):
        kept = ref[...]
        spread = jnp.concatenate(
            [jnp.broadcast_to(kept[:, c:c + 1], (per_slab, TILE)) for c in range(kept.shape[1])],
            axis=1,
        )
        bias[at] = jnp.where(spread > 0, 0.0, -jnp.inf).astype(jnp.float32)

    def attend(h, slab, queries, at, dst):
        for i in range(per_slab):
            q = queries[h, i * TILE:(i + 1) * TILE, :]
            scores = []
            for j in range(reach_slabs):
                other = lax.rem(slab + j - reach_slabs // 2 + n, n)
                s = lax.dot_general(
                    q, k_all[other, h], (((1,), (1,)), ((), ())),
                    preferred_element_type=jnp.float32,
                )
                scores.append(s * scale + bias[at, i:i + 1, j * tokens:(j + 1) * tokens])
            peak = functools.reduce(
                jnp.maximum, [jnp.max(s, axis=1, keepdims=True) for s in scores]
            )
            exps = [jnp.exp2(s - peak) for s in scores]
            total = functools.reduce(jnp.add, [jnp.sum(e, axis=1, keepdims=True) for e in exps])
            acc = None
            for j in range(reach_slabs):
                other = lax.rem(slab + j - reach_slabs // 2 + n, n)
                term = jnp.dot(
                    exps[j].astype(jnp.bfloat16), v_all[other, h],
                    preferred_element_type=jnp.float32,
                )
                acc = term if acc is None else acc + term
            dst[i * TILE:(i + 1) * TILE, lanes_of(h)] = (acc * (1.0 / total)).astype(jnp.bfloat16)

    def project(b, c):
        part[b, c] = jnp.dot(
            attended[...], w_all[b, c], preferred_element_type=jnp.float32
        ).astype(jnp.bfloat16)
        owner = b // per_head
        @pl.when(owner == partner)
        def _():
            partner_send(b, c).start()
        @pl.when((owner // 2 != my_chip) & (lax.rem(owner, 2) != my_core))
        def _():
            give_send(b, c).start()

    def collect(j):
        b, c = block_of(j // pieces), lax.rem(j, pieces)
        owner, at = b // per_head, lax.rem(b, per_head)
        @pl.when((owner // 2 != my_chip) & (lax.rem(owner, 2) == my_core))
        def _():
            give_send(b, c).wait_recv()

            def tile(i, carry):
                now = pl.ds(pl.multiple_of(i * TILE, TILE), TILE)
                part[b, c, now, :] = (
                    part[b, c, now, :].astype(jnp.float32)
                    + pair[owner // 2, at, c, now, :].astype(jnp.float32)
                ).astype(jnp.bfloat16)
                return carry

            lax.fori_loop(0, tokens // TILE, tile, 0)
            sum_send(b, c).start()

    def use(j):
        b, c = block_of(j // pieces), lax.rem(j, pieces)
        for s in range(halves):
            for o in range(1, groups):
                across_arrival(b, c, s, o).wait_recv()
        project(b, c)

    def settle(b, c, at_rows, first=0, past=wide):
        cb = lax.rem(b, per_head)
        span = gate_ref.shape[1]
        for u in range(first // span, past // span):
            lanes = slice(u * span, (u + 1) * span)
            summed = part[b, c, at_rows, lanes].astype(jnp.float32)
            for slot in range(chips):
                summed = summed + got[slot, cb, c, at_rows, lanes].astype(jnp.float32)
            block = cb * (cols // span) + c * (wide // span) + u
            at = pl.ds(pl.multiple_of(block * span, span), span)
            out_ref[at_rows, at] = (gate_ref[pl.ds(block, 1), :] * summed).astype(out_ref.dtype)

    def finish(j):
        b, c = block_of(j // pieces), lax.rem(j, pieces)
        @pl.when(b // per_head == me)
        def _():
            for slot in range(chips):
                term_arrival(b, c, slot).wait_recv()
            settle(b, c, slice(0, tokens))

    last_b, last_c = block_of(n - 1), pieces - 1
    last_owner, last_at = last_b // per_head, lax.rem(last_b, per_head)
    other_chip = last_owner // 2 != my_chip
    same_core = lax.rem(last_owner, 2) == my_core

    def tile_send(i, s, dst, recv, device):
        now = slice(i * TILE, (i + 1) * TILE)
        return remote(
            part.at[last_b, last_c, now, lanes_in(s)], dst.at[last_at, last_c, now, lanes_in(s)],
            t_send.at[s, i], recv, device,
        )

    def to_partner(i, s):
        return tile_send(i, s, got.at[0], t_recv.at[0, s, i], {"head": partner})

    def to_collector(i, s):
        return tile_send(i, s, pair.at[last_owner // 2], t_pair.at[s, i], {"head": partner})

    def to_owner(i, s):
        slot = lax.rem(my_chip - last_owner // 2 + chips, chips)
        return tile_send(i, s, got.at[slot], t_recv.at[slot, s, i], {"head": last_owner})

    def tile_arrival(i, s, slot):
        return tile_send(i, s, got.at[slot], t_recv.at[slot, s, i], {"head": partner})

    def last_terms(s):
        lanes = lanes_in(s)
        if s < halves - 1:
            for o in range(1, groups):
                across_arrival(last_b, last_c, s, o).wait_recv()
        part[last_b, last_c, :, lanes] = jnp.dot(
            attended[...], w_all[last_b, last_c, :, lanes], preferred_element_type=jnp.float32
        ).astype(jnp.bfloat16)
        for i in range(per_slab):
            @pl.when(last_owner == partner)
            def _(i=i):
                to_partner(i, s).start()
            @pl.when(other_chip & jnp.logical_not(same_core))
            def _(i=i):
                to_collector(i, s).start()

    def last_collect(s):
        lanes = lanes_in(s)
        @pl.when(other_chip & same_core)
        def _():
            for i in range(per_slab):
                now = slice(i * TILE, (i + 1) * TILE)
                to_collector(i, s).wait_recv()
                part[last_b, last_c, now, lanes] = (
                    part[last_b, last_c, now, lanes].astype(jnp.float32)
                    + pair[last_owner // 2, last_at, last_c, now, lanes].astype(jnp.float32)
                ).astype(jnp.bfloat16)
                to_owner(i, s).start()

    def last_finish():
        @pl.when(last_owner == me)
        def _():
            for s in range(halves):
                for i in range(per_slab):
                    for slot in range(chips):
                        tile_arrival(i, s, slot).wait_recv()
                    settle(
                        last_b, last_c, slice(i * TILE, (i + 1) * TILE),
                        s * sub_cols, (s + 1) * sub_cols,
                    )

    def do_use(j, carry):
        use(j)
        collect(j - 1)
        return carry

    def do_finish(j, carry):
        finish(j)
        return carry

    def own_block(c, carry):
        project(t, c)
        @pl.when(c > 0)
        def _():
            collect(c - 1)
        return carry

    @pl.when(inner)
    def _():
        for copy in in_copies:
            copy.wait()
        set_bias(0, keep_own)

        def own_slab(h, carry):
            for which in range(2):
                kv_arrival(end, h, which).wait_recv()
                kv_relay(h, which).start()
            for which in range(2):
                kv_arrival(across_mid, h, which).wait_recv()
            attend(h, t, q_own, 0, attended)
            return carry

        lax.fori_loop(0, head_count, own_slab, 0)
        for c in range(pieces):
            for s in range(halves):
                first_send(c, s, 1).start()
        for c in range(pieces):
            own_copy(c).wait()
        lax.fori_loop(0, pieces, own_block, 0)
        keep_copy.wait_recv()
        set_bias(1, keep_far)

        def end_slab(h, carry):
            q_copy(h).wait_recv()
            for which in range(2):
                kv_arrival(far_end, h, which).wait_recv()
            attend(h, end, q_far, 1, far_att)
            att_copy(h).start()
            return carry

        lax.fori_loop(0, head_count, end_slab, 0)

    def early_pass(j, carry):
        pass_on(j)
        return carry

    @pl.when(outer)
    def _():
        lax.fori_loop(pieces, 2 * pieces, early_pass, 0)
        for c in range(pieces):
            own_copy(c).wait()
        for h in range(head_count):
            att_copy(h).wait_recv()
        lax.fori_loop(0, pieces, own_block, 0)

    @pl.when(outer)
    def _():
        lax.fori_loop(pieces, 2 * pieces, do_use, 0)

    def used_by(j):
        lagging = jnp.maximum(jnp.maximum(j - pieces - 1, 3 * j - 7 * pieces - 1), pieces)
        return jnp.where(inner, jnp.minimum(lagging, j - 1), jnp.maximum(j - 1, 2 * pieces))

    def settled_by(j):
        most = jnp.where(inner, pieces, 2 * pieces)
        return jnp.clip(2 * (j - 2 * pieces) - 2, 0, most)

    def step(j, carry):
        pass_on(j)
        @pl.when(inner & (j < 3 * pieces))
        def _():
            pass_on(j - pieces)
        lax.fori_loop(used_by(j - 1), used_by(j), do_use, 0)
        return lax.fori_loop(settled_by(j - 1), settled_by(j), do_finish, carry)

    gate_copy.wait()
    lax.fori_loop(2 * pieces, total_pieces - 2, step, 0)
    pass_on(total_pieces - 2)

    @pl.when(inner)
    def _():
        for o in range(1, groups):
            theirs_on(end, o, mid_id).start()
    until = jnp.where(inner, total_pieces - 3, total_pieces - 2)
    lax.fori_loop(used_by(total_pieces - 3), until, do_use, 0)
    settled = jnp.where(inner, pieces, 3 * pieces)
    lax.fori_loop(settled_by(total_pieces - 3), settled, do_finish, 0)

    @pl.when(outer)
    def _():
        for h in range(head_count):
            for which in range(2):
                kv_first(h, which, mate_id).wait_send()
            q_copy(h).wait_send()
        keep_copy.wait_send()

    @pl.when(inner)
    def _():
        for h in range(head_count):
            for which in range(2):
                kv_first(h, which, mid_id).wait_send()
                kv_relay(h, which).wait_send()
            att_copy(h).wait_send()
        for c in range(pieces):
            for s in range(halves):
                first_send(c, s, 1).wait_send()

    @pl.when(outer)
    def _():
        collect(total_pieces - 3)

    for s in range(halves):
        relay(last_b, last_c, s, 0).wait_recv()
        @pl.when(inner)
        def _(s=s):
            relay(last_b, last_c, s, 0).start()
        if s < halves - 1:
            for o in range(1, groups):
                across(last_b, last_c, s, o).start()
            @pl.when(outer)
            def _():
                use(total_pieces - 2)
                collect(total_pieces - 2)
    for o in range(1, groups):
        across_arrival(last_b, last_c, halves - 1, o).wait_recv()
        @pl.when(inner)
        def _(o=o):
            theirs_on(last_b, o, mate_id).start()

    @pl.when(inner)
    def _():
        lax.fori_loop(until, total_pieces - 2, do_use, 0)
        use(total_pieces - 2)
        collect(total_pieces - 3)
        collect(total_pieces - 2)

    for s in range(halves):
        last_terms(s)
        last_collect(s)
    lax.fori_loop(settled, total_pieces - 1, do_finish, 0)

    def drain(b, carry):
        for c in range(pieces):
            for s in range(halves):
                @pl.when(b == t)
                def _(c=c, s=s):
                    first_send(c, s, 0).wait_send()
                @pl.when((b == t) & outer)
                def _(c=c, s=s):
                    for o in range(1, groups):
                        rest_send(c, s, o).wait_send()
                last_part = c == pieces - 1 and s == halves - 1
                sent = (b != t) & (outer | (b != end))
                if last_part:
                    sent = ((b != t) & (b != last_b)) | (inner & (b == last_b))
                @pl.when(sent)
                def _(c=c, s=s):
                    for o in range(1, groups):
                        across(b, c, s, o).wait_send()
                @pl.when(inner & (b == end))
                def _(c=c, s=s):
                    relay(b, c, s, 1).wait_send()
                @pl.when(inner & (b != end) & (b != t))
                def _(c=c, s=s):
                    relay(b, c, s, 0).wait_send()
            @pl.when((b // per_head != me) & ((b != last_b) | (c != last_c)))
            def _(c=c):
                partner_send(b, c).wait_send()
        return carry

    lax.fori_loop(0, n, drain, 0)
    last_finish()
    @pl.when(last_owner != me)
    def _():
        for s in range(halves):
            for i in range(per_slab):
                to_partner(i, s).wait_send()


def chain_shards(queries, key_rows, value_rows, keep_tiles, out_weight, gate_scale):
    n, heads, groups = lax.axis_size("tm"), lax.axis_size("head"), lax.axis_size("groups")
    tokens = queries.shape[0]
    head_count = queries.shape[1]
    flat = head_count * HD
    rows, cols = out_weight.shape
    pieces = cols // 256 if cols % 256 == 0 else 1
    wide = cols // pieces
    per_head = n // heads
    if pieces < 4 or wide % 256:
        return shards(queries, key_rows, value_rows, keep_tiles, out_weight, gate_scale)
    gate_lanes = 128 if wide % 128 == 0 else wide
    vmem = pl.BlockSpec(memory_space=pltpu.VMEM)
    hbm = pl.BlockSpec(memory_space=pl.ANY)
    dma = pltpu.SemaphoreType.DMA
    bf16 = jnp.bfloat16
    return pl.pallas_call(
        functools.partial(chain_kernel, (groups, n, heads, pieces)),
        out_shape=pltpu.VMEM((tokens, gate_scale.shape[0]), bf16),
        in_specs=[hbm, hbm, hbm, hbm, hbm, hbm],
        out_specs=vmem,
        scratch_shapes=[
            pltpu.VMEM((head_count, tokens, HD), bf16),
            pltpu.VMEM((head_count, tokens, HD), bf16),
            pltpu.VMEM((n, head_count, tokens, HD), bf16),
            pltpu.VMEM((n, head_count, tokens, HD), bf16),
            pltpu.VMEM((n, pieces, rows, wide), bf16),
            pltpu.VMEM((tokens, flat), bf16),
            pltpu.VMEM((tokens, flat), bf16),
            pltpu.VMEM((n, pieces, tokens, wide), bf16),
            pltpu.VMEM((heads // 2, per_head, pieces, tokens, wide), bf16),
            pltpu.VMEM((heads // 2, per_head, pieces, tokens, wide), bf16),
            pltpu.VMEM(keep_tiles.shape, jnp.int32),
            pltpu.VMEM(keep_tiles.shape, jnp.int32),
            pltpu.VMEM((gate_scale.shape[0] // gate_lanes, gate_lanes), jnp.float32),
            pltpu.VMEM((2, keep_tiles.shape[0], keep_tiles.shape[1] * TILE), jnp.float32),
            dma((2, 2, head_count)),
            dma((n, 2, head_count)),
            dma((head_count,)),
            dma((head_count,)),
            dma((2,)),
            dma((head_count,)),
            dma((head_count,)),
            dma((2, n, pieces, 2)),
            dma((n, pieces, 2)),
            dma((groups - 1, n, pieces, 2)),
            dma((groups - 1, n, pieces, 2)),
            dma((n, pieces)),
            dma((heads // 2, per_head, pieces)),
            dma((heads // 2, per_head, pieces)),
            dma((2, tokens // TILE)),
            dma((heads // 2, 2, tokens // TILE)),
            dma((2, tokens // TILE)),
            dma((pieces,)),
            dma((4,)),
            dma((1,)),
        ],
        compiler_params=pltpu.CompilerParams(
            collective_id=0, has_side_effects=True, vmem_limit_bytes=56 * 1024 * 1024
        ),
    )(
        queries.transpose(1, 0, 2),
        key_rows.transpose(1, 0, 2),
        value_rows.transpose(1, 0, 2),
        keep_tiles,
        out_weight,
        gate_scale.reshape(-1, gate_lanes),
    )


def solution(mesh):
    placed = (
        P(("groups", "tm"), "head", None),
        P(("groups", "tm"), "head", None),
        P(("groups", "tm"), "head", None),
        P(("groups", "tm"), None),
        P("head", "tm"),
        P(("groups", "head")),
    )
    n, heads = mesh.shape["tm"], mesh.shape["head"]
    chain = n == 4 and n % heads == 0 and heads % 2 == 0 and mesh.shape["groups"] > 1
    body = chain_shards if chain else shards
    return jax.shard_map(
        body, mesh=mesh, in_specs=placed, out_specs=P(("groups", "tm"), "head"), check_vma=False
    )
```

```python
import functools
import math

import jax
import jax.numpy as jnp
from jax import lax
from jax.experimental import pallas as pl
from jax.experimental.pallas import tpu as pltpu
from jax.sharding import PartitionSpec as P

HD = 128
TILE = 128
MESH = pl.DeviceIdType.MESH


def layer_kernel(
    sizes, q_ref, k_ref, v_ref, keep_ref, w_ref, gate_ref, out_ref,
    q_own, k_all, v_all, w_all, attended, part, got,
    kv_send, kv_recv, z_send, z_recv, y_send, y_recv, r_send, r_recv, own_sem, in_sem,
):
    groups, n, heads, reach, pieces = sizes
    g, t, me = lax.axis_index("groups"), lax.axis_index("tm"), lax.axis_index("head")
    rows, cols = w_ref.shape
    wide = cols // pieces
    per_head = n // heads
    part_rows = rows // groups
    head_count, tokens = q_ref.shape[0], q_ref.shape[1]
    slabs = 2 * reach + 1

    barrier = pltpu.get_barrier_semaphore()
    partners = []
    for d in range(1, reach + 1):
        partners += [{"tm": lax.rem(t + d, n)}, {"tm": lax.rem(t + n - d, n)}]
    for o in range(1, groups):
        partners.append({"groups": lax.rem(g + o, groups)})
    for o in range(1, heads):
        partners.append({"head": lax.rem(me + o, heads)})
    for partner in partners:
        pl.semaphore_signal(barrier, inc=1, device_id=partner, device_id_type=MESH)
    pl.semaphore_wait(barrier, len(partners))

    def remote(src, dst, send, recv, device):
        return pltpu.make_async_remote_copy(
            src_ref=src, dst_ref=dst, send_sem=send, recv_sem=recv,
            device_id=device, device_id_type=MESH,
        )

    kv_copies = []
    for d in range(1, reach + 1):
        for slot, to in ((reach - d, lax.rem(t + d, n)), (reach + d, lax.rem(t + n - d, n))):
            for which, (src, dst) in enumerate(((k_ref, k_all), (v_ref, v_all))):
                kv_copies.append(
                    remote(src, dst.at[slot], kv_send.at[slot, which], kv_recv.at[slot, which], {"tm": to})
                )
    @pl.when(t == 0)
    def _():
        for copy in reversed(kv_copies):
            copy.start()

    @pl.when(t != 0)
    def _():
        for copy in kv_copies:
            copy.start()

    in_copies = [
        pltpu.make_async_copy(src, dst, in_sem.at[i])
        for i, (src, dst) in enumerate(
            ((q_ref, q_own), (k_ref, k_all.at[reach]), (v_ref, v_all.at[reach]))
        )
    ]
    for copy in in_copies:
        copy.start()

    my_rows = pl.ds(pl.multiple_of(g * part_rows, part_rows), part_rows)

    def own_copy(c):
        return pltpu.make_async_copy(
            w_ref.at[:, c * wide:(c + 1) * wide], w_all.at[t, c], own_sem.at[c]
        )

    def first_send(c, side):
        to = jnp.minimum(t + 1, n - 1) if side else jnp.maximum(t - 1, 0)
        return remote(
            w_ref.at[my_rows, c * wide:(c + 1) * wide], w_all.at[t, c, my_rows],
            z_send.at[side, t, c], z_recv.at[t, c], {"tm": to},
        )

    def relay(b, c, side):
        to = jnp.minimum(t + 1, n - 1) if side else jnp.maximum(t - 1, 0)
        return remote(
            w_all.at[b, c, my_rows], w_all.at[b, c, my_rows],
            z_send.at[side, b, c], z_recv.at[b, c], {"tm": to},
        )

    def across(b, c, o):
        return remote(
            w_all.at[b, c, my_rows], w_all.at[b, c, my_rows],
            y_send.at[o - 1, b, c], y_recv.at[o - 1, b, c],
            {"groups": lax.rem(g + o, groups)},
        )

    def across_arrival(b, c, o):
        sender = lax.rem(g + groups - o, groups)
        their_rows = pl.ds(pl.multiple_of(sender * part_rows, part_rows), part_rows)
        return remote(
            w_all.at[b, c, their_rows], w_all.at[b, c, their_rows],
            y_send.at[o - 1, b, c], y_recv.at[o - 1, b, c],
            {"groups": lax.rem(g + o, groups)},
        )

    def term_send(b, c, o):
        return remote(
            part.at[b, c], got.at[o - 1, b % per_head, c],
            r_send.at[b, c], r_recv.at[o - 1, b % per_head, c],
            {"head": lax.rem(me + o, heads)},
        )

    for c in range(pieces):
        own_copy(c).start()
        @pl.when(t < n - 1)
        def _(c=c):
            first_send(c, 1).start()
        @pl.when(t > 0)
        def _(c=c):
            first_send(c, 0).start()

    for copy in in_copies:
        copy.wait()
    for copy in kv_copies:
        copy.wait_recv()

    scale = 1.0 / math.sqrt(HD)
    per_slab = tokens // TILE

    early = min(pieces, head_count - 1)

    def pass_on(j, side):
        step, c = j // pieces, j % pieces
        b = (t - 1 - step) if side else (t + 1 + step)
        @pl.when((b >= 0) & (b <= n - 1))
        def _():
            relay(b, c, side).wait_recv()
            @pl.when((t < n - 1) if side else (t > 0))
            def _():
                relay(b, c, side).start()
            for o in range(1, groups):
                across(b, c, o).start()

    def one_head(h, carry):
        lanes = pl.ds(pl.multiple_of(h * HD, HD), HD)
        for i in range(per_slab):
            q = q_own[h, i * TILE:(i + 1) * TILE, :]
            scores = []
            for j in range(slabs):
                s = lax.dot_general(
                    q, k_all[j, h], (((1,), (1,)), ((), ())), preferred_element_type=jnp.float32
                )
                bias = jnp.concatenate(
                    [
                        jnp.full(
                            (1, TILE),
                            jnp.where(keep_ref[i, j * per_slab + u] > 0, 0.0, -jnp.inf),
                            jnp.float32,
                        )
                        for u in range(per_slab)
                    ],
                    axis=1,
                )
                scores.append(s * scale + bias)
            peak = functools.reduce(
                jnp.maximum, [jnp.max(s, axis=1, keepdims=True) for s in scores]
            )
            exps = [jnp.exp(s - peak) for s in scores]
            total = functools.reduce(jnp.add, [jnp.sum(e, axis=1, keepdims=True) for e in exps])
            inverse = 1.0 / total
            acc = None
            for j in range(slabs):
                term = jnp.dot(
                    (exps[j] * inverse).astype(jnp.bfloat16), v_all[j, h],
                    preferred_element_type=jnp.float32,
                )
                acc = term if acc is None else acc + term
            attended[i * TILE:(i + 1) * TILE, lanes] = acc.astype(jnp.bfloat16)
        @pl.when(h >= head_count - early)
        def _():
            for side in (1, 0):
                pass_on(h - (head_count - early), side)
        return carry

    lax.fori_loop(0, head_count, one_head, 0)

    def project(b, c):
        def tile(i, carry):
            at = pl.ds(pl.multiple_of(i * TILE, TILE), TILE)
            part[b, c, at, :] = jnp.dot(
                attended[at, :], w_all[b, c], preferred_element_type=jnp.float32
            ).astype(jnp.bfloat16)
            return carry

        lax.fori_loop(0, tokens // TILE, tile, 0)
        owner = b // per_head
        for o in range(1, heads):
            @pl.when(owner == lax.rem(me + o, heads))
            def _():
                term_send(b, c, o).start()

    for c in range(pieces):
        own_copy(c).wait()
        project(t, c)

    def use(j, side):
        step, c = j // pieces, j % pieces
        b = (t - 1 - step) if side else (t + 1 + step)
        @pl.when((b >= 0) & (b <= n - 1))
        def _():
            for o in range(1, groups):
                across_arrival(b, c, o).wait_recv()
            project(b, c)

    count = (n - 1) * pieces

    def use_both(j, carry):
        for side in (1, 0):
            use(j, side)
        return carry

    def step(j, carry):
        for side in (1, 0):
            pass_on(j, side)
        first = jnp.minimum(2 * (j - early), j - 1)
        last = jnp.minimum(2 * (j - early) + 2, j)
        return lax.fori_loop(first, last, use_both, carry)

    lax.fori_loop(early, count, step, 0)
    lax.fori_loop(min(2 * (count - early), count - 1), count, use_both, 0)

    for cb in range(per_head):
        for c in range(pieces):
            b = me * per_head + cb
            for o in range(1, heads):
                term_send(b, c, o).wait_recv()
            span = wide if gate_ref.shape[0] == 1 else gate_ref.shape[1]
            for u in range(wide // span):
                lanes = slice(u * span, (u + 1) * span)
                summed = part[b, c, :, lanes].astype(jnp.float32)
                for o in range(1, heads):
                    summed = summed + got[o - 1, cb, c, :, lanes].astype(jnp.float32)
                at = cb * cols + c * wide + u * span
                gate = gate_ref[:, at:at + span] if span == wide else gate_ref[at // span:at // span + 1, :]
                out_ref[:, at:at + span] = (gate * summed).astype(out_ref.dtype)

    for copy in kv_copies:
        copy.wait_send()
    for c in range(pieces):
        @pl.when(t < n - 1)
        def _(c=c):
            first_send(c, 1).wait_send()
        @pl.when(t > 0)
        def _(c=c):
            first_send(c, 0).wait_send()

    def drain(b, carry):
        for c in range(pieces):
            @pl.when(b != t)
            def _(c=c):
                for o in range(1, groups):
                    across(b, c, o).wait_send()
            @pl.when((b < t) & (t < n - 1))
            def _(c=c):
                relay(b, c, 1).wait_send()
            @pl.when((b > t) & (t > 0))
            def _(c=c):
                relay(b, c, 0).wait_send()
            @pl.when(b // per_head != me)
            def _(c=c):
                term_send(b, c, 1).wait_send()
        return carry

    lax.fori_loop(0, n, drain, 0)


def shards(queries, key_rows, value_rows, keep_tiles, out_weight, gate_scale):
    n, heads, groups = lax.axis_size("tm"), lax.axis_size("head"), lax.axis_size("groups")
    reach = min(2, (n - 1) // 2)
    tokens = queries.shape[0]
    head_count = queries.shape[1]
    flat = head_count * HD
    rows, cols = out_weight.shape
    pieces = cols // 256 if cols % 256 == 0 else 1
    wide = cols // pieces
    per_head = n // heads
    slabs = 2 * reach + 1
    gate_lanes = 128 if wide % 128 == 0 else gate_scale.shape[0]
    vmem = pl.BlockSpec(memory_space=pltpu.VMEM)
    hbm = pl.BlockSpec(memory_space=pl.ANY)
    dma = pltpu.SemaphoreType.DMA
    bf16 = jnp.bfloat16
    return pl.pallas_call(
        functools.partial(layer_kernel, (groups, n, heads, reach, pieces)),
        out_shape=jax.ShapeDtypeStruct((tokens, gate_scale.shape[0]), bf16),
        in_specs=[hbm, hbm, hbm, pl.BlockSpec(memory_space=pltpu.SMEM), hbm, vmem],
        out_specs=vmem,
        scratch_shapes=[
            pltpu.VMEM((head_count, tokens, HD), bf16),
            pltpu.VMEM((slabs, head_count, tokens, HD), bf16),
            pltpu.VMEM((slabs, head_count, tokens, HD), bf16),
            pltpu.VMEM((n, pieces, rows, wide), bf16),
            pltpu.VMEM((tokens, flat), bf16),
            pltpu.VMEM((n, pieces, tokens, wide), bf16),
            pltpu.VMEM((heads - 1, per_head, pieces, tokens, wide), bf16),
            dma((slabs, 2)),
            dma((slabs, 2)),
            dma((2, n, pieces)),
            dma((n, pieces)),
            dma((groups - 1, n, pieces)),
            dma((groups - 1, n, pieces)),
            dma((n, pieces)),
            dma((heads - 1, per_head, pieces)),
            dma((pieces,)),
            dma((3,)),
        ],
        compiler_params=pltpu.CompilerParams(
            collective_id=0, has_side_effects=True, vmem_limit_bytes=56 * 1024 * 1024
        ),
    )(
        queries.transpose(1, 0, 2),
        key_rows.transpose(1, 0, 2),
        value_rows.transpose(1, 0, 2),
        keep_tiles,
        out_weight,
        gate_scale.reshape(-1, gate_lanes),
    )


def chain_kernel(
    sizes, q_ref, k_ref, v_ref, keep_hbm, w_ref, gate_hbm, out_ref,
    q_own, q_far, k_all, v_all, w_all, attended, far_att, part, got, pair, keep_own, keep_far, gate_ref, bias,
    kv_send, kv_recv, q_send, q_recv, keep_sem, att_send, att_recv,
    z_send, z_recv, y_send, y_recv, r_send, r_recv, pair_recv, t_send, t_recv, t_pair, own_sem, in_sem, gate_sem,
):
    groups, n, heads, pieces = sizes
    g, t, me = lax.axis_index("groups"), lax.axis_index("tm"), lax.axis_index("head")
    rows, cols = w_ref.shape
    wide = cols // pieces
    per_head = n // heads
    part_rows = rows // groups
    halves = 2
    sub_cols = wide // halves
    head_count, tokens = q_ref.shape[0], q_ref.shape[1]
    per_slab = tokens // TILE
    total_pieces = n * pieces
    chips = heads // 2
    my_chip, my_core = me // 2, lax.rem(me, 2)
    partner = me + 1 - 2 * my_core

    left = t < n // 2
    inner = (t > 0) & (t < n - 1)
    outer = jnp.logical_not(inner)
    end = jnp.where(left, 0, n - 1)
    near = jnp.where(left, 1, n - 2)
    across_mid = n - 1 - t
    far_end = n - 1 - end
    mate = jnp.where(inner, end, near)
    mate_id = {"tm": mate}
    mid_id = {"tm": across_mid}

    barrier = pltpu.get_barrier_semaphore()

    def greet(partner):
        pl.semaphore_signal(barrier, inc=1, device_id=partner, device_id_type=MESH)

    greet(mate_id)
    @pl.when(inner)
    def _():
        greet(mid_id)
    for o in range(1, groups):
        greet({"groups": lax.rem(g + o, groups)})
    for o in range(1, heads):
        greet({"head": lax.rem(me + o, heads)})
    @pl.when(inner)
    def _():
        pl.semaphore_wait(barrier, groups + heads)
    @pl.when(outer)
    def _():
        pl.semaphore_wait(barrier, groups + heads - 1)

    def remote(src, dst, send, recv, device):
        return pltpu.make_async_remote_copy(
            src_ref=src, dst_ref=dst, send_sem=send, recv_sem=recv,
            device_id=device, device_id_type=MESH,
        )

    kv = ((k_ref, k_all), (v_ref, v_all))

    def kv_first(h, which, device):
        src, dst = kv[which]
        return remote(
            src.at[h], dst.at[t, h], kv_send.at[0, which, h], kv_recv.at[t, which, h], device
        )

    def kv_relay(h, which):
        buf = kv[which][1]
        return remote(
            buf.at[end, h], buf.at[end, h], kv_send.at[1, which, h], kv_recv.at[end, which, h],
            mid_id,
        )

    def kv_arrival(slab, h, which):
        buf = kv[which][1]
        return remote(
            buf.at[slab, h], buf.at[slab, h], kv_send.at[1, which, h],
            kv_recv.at[slab, which, h], mid_id,
        )

    def q_copy(h):
        return remote(q_ref.at[h], q_far.at[h], q_send.at[h], q_recv.at[h], mate_id)

    keep_copy = remote(keep_hbm, keep_far, keep_sem.at[0], keep_sem.at[1], mate_id)

    def lanes_of(h):
        return pl.ds(pl.multiple_of(h * HD, HD), HD)

    def att_copy(h):
        return remote(
            far_att.at[:, lanes_of(h)], attended.at[:, lanes_of(h)],
            att_send.at[h], att_recv.at[h], mate_id,
        )

    def rows_of(sender):
        return pl.ds(pl.multiple_of(sender * part_rows, part_rows), part_rows)

    def lanes_in(s, c=0):
        return slice(c * wide + s * sub_cols, c * wide + (s + 1) * sub_cols)

    def own_copy(c):
        return pltpu.make_async_copy(
            w_ref.at[:, c * wide:(c + 1) * wide], w_all.at[t, c], own_sem.at[c]
        )

    def first_send(c, s, way):
        mine = rows_of(g)
        return remote(
            w_ref.at[mine, lanes_in(s, c)], w_all.at[t, c, mine, lanes_in(s)],
            z_send.at[way, t, c, s], z_recv.at[t, c, s], mid_id if way else mate_id,
        )

    def rest_send(c, s, o):
        theirs = rows_of(lax.rem(g + groups - o, groups))
        return remote(
            w_ref.at[theirs, lanes_in(s, c)], w_all.at[t, c, theirs, lanes_in(s)],
            y_send.at[o - 1, t, c, s], y_recv.at[o - 1, t, c, s], mate_id,
        )

    def relay(b, c, s, way):
        mine = rows_of(g)
        return remote(
            w_all.at[b, c, mine, lanes_in(s)], w_all.at[b, c, mine, lanes_in(s)],
            z_send.at[way, b, c, s], z_recv.at[b, c, s], mid_id if way else mate_id,
        )

    def across(b, c, s, o):
        mine = rows_of(g)
        return remote(
            w_all.at[b, c, mine, lanes_in(s)], w_all.at[b, c, mine, lanes_in(s)],
            y_send.at[o - 1, b, c, s], y_recv.at[o - 1, b, c, s],
            {"groups": lax.rem(g + o, groups)},
        )

    def theirs_on(b, o, device):
        c, s = pieces - 1, halves - 1
        theirs = rows_of(lax.rem(g + groups - o, groups))
        return remote(
            w_all.at[b, c, theirs, lanes_in(s)], w_all.at[b, c, theirs, lanes_in(s)],
            y_send.at[o - 1, b, c, s], y_recv.at[o - 1, b, c, s], device,
        )

    def across_arrival(b, c, s, o):
        theirs = rows_of(lax.rem(g + groups - o, groups))
        return remote(
            w_all.at[b, c, theirs, lanes_in(s)], w_all.at[b, c, theirs, lanes_in(s)],
            y_send.at[o - 1, b, c, s], y_recv.at[o - 1, b, c, s],
            {"groups": lax.rem(g + o, groups)},
        )

    def partner_send(b, c):
        at = lax.rem(b, per_head)
        return remote(
            part.at[b, c], got.at[0, at, c], r_send.at[b, c], r_recv.at[0, at, c],
            {"head": partner},
        )

    def give_send(b, c):
        owner, at = b // per_head, lax.rem(b, per_head)
        return remote(
            part.at[b, c], pair.at[owner // 2, at, c], r_send.at[b, c],
            pair_recv.at[owner // 2, at, c], {"head": partner},
        )

    def sum_send(b, c):
        owner, at = b // per_head, lax.rem(b, per_head)
        slot = lax.rem(my_chip - owner // 2 + chips, chips)
        return remote(
            part.at[b, c], got.at[slot, at, c], r_send.at[b, c], r_recv.at[slot, at, c],
            {"head": owner},
        )

    def term_arrival(b, c, slot):
        at = lax.rem(b, per_head)
        return remote(
            part.at[b, c], got.at[slot, at, c], r_send.at[b, c], r_recv.at[slot, at, c],
            {"head": partner},
        )

    in_copies = [
        pltpu.make_async_copy(src, dst, in_sem.at[i])
        for i, (src, dst) in enumerate(
            ((keep_hbm, keep_own), (q_ref, q_own), (k_ref, k_all.at[t]), (v_ref, v_all.at[t]))
        )
    ]

    gate_copy = pltpu.make_async_copy(gate_hbm, gate_ref, gate_sem.at[0])

    @pl.when(outer)
    def _():
        for h in range(head_count):
            for which in range(2):
                kv_first(h, which, mate_id).start()
        keep_copy.start()
        for h in range(head_count):
            q_copy(h).start()

    @pl.when(inner)
    def _():
        for h in range(head_count):
            for which in range(2):
                kv_first(h, which, mid_id).start()
        for copy in in_copies:
            copy.start()

    for c in range(pieces):
        for s in range(halves):
            first_send(c, s, 0).start()
        @pl.when(outer)
        def _(c=c):
            for s in range(halves):
                for o in range(1, groups):
                    rest_send(c, s, o).start()
    for c in range(pieces):
        own_copy(c).start()
    gate_copy.start()

    def block_of(k):
        place = jnp.where(left, t, n - 1 - t)
        b = jnp.where(k == 0, place, jnp.where(k == 1, 1 - place, k))
        return jnp.where(left, b, n - 1 - b)

    def pass_on(j):
        b, c = block_of(j // pieces), lax.rem(j, pieces)
        for s in range(halves):
            relay(b, c, s, 0).wait_recv()
            @pl.when(inner & (b == end))
            def _(s=s):
                relay(b, c, s, 1).start()
            @pl.when(inner & (b != end))
            def _(s=s):
                relay(b, c, s, 0).start()
            @pl.when(outer | (b != end))
            def _(s=s):
                for o in range(1, groups):
                    across(b, c, s, o).start()

    scale = math.log2(math.e) / math.sqrt(HD)
    reach_slabs = keep_own.shape[1] // per_slab

    def set_bias(at, ref):
        kept = ref[...]
        spread = jnp.concatenate(
            [jnp.broadcast_to(kept[:, c:c + 1], (per_slab, TILE)) for c in range(kept.shape[1])],
            axis=1,
        )
        bias[at] = jnp.where(spread > 0, 0.0, -jnp.inf).astype(jnp.float32)

    def attend(h, slab, queries, at, dst):
        for i in range(per_slab):
            q = queries[h, i * TILE:(i + 1) * TILE, :]
            scores = []
            for j in range(reach_slabs):
                other = lax.rem(slab + j - reach_slabs // 2 + n, n)
                s = lax.dot_general(
                    q, k_all[other, h], (((1,), (1,)), ((), ())),
                    preferred_element_type=jnp.float32,
                )
                scores.append(s * scale + bias[at, i:i + 1, j * tokens:(j + 1) * tokens])
            peak = functools.reduce(
                jnp.maximum, [jnp.max(s, axis=1, keepdims=True) for s in scores]
            )
            exps = [jnp.exp2(s - peak) for s in scores]
            total = functools.reduce(jnp.add, [jnp.sum(e, axis=1, keepdims=True) for e in exps])
            acc = None
            for j in range(reach_slabs):
                other = lax.rem(slab + j - reach_slabs // 2 + n, n)
                term = jnp.dot(
                    exps[j].astype(jnp.bfloat16), v_all[other, h],
                    preferred_element_type=jnp.float32,
                )
                acc = term if acc is None else acc + term
            dst[i * TILE:(i + 1) * TILE, lanes_of(h)] = (acc * (1.0 / total)).astype(jnp.bfloat16)

    def project(b, c):
        part[b, c] = jnp.dot(
            attended[...], w_all[b, c], preferred_element_type=jnp.float32
        ).astype(jnp.bfloat16)
        owner = b // per_head
        @pl.when(owner == partner)
        def _():
            partner_send(b, c).start()
        @pl.when((owner // 2 != my_chip) & (lax.rem(owner, 2) != my_core))
        def _():
            give_send(b, c).start()

    def collect(j):
        b, c = block_of(j // pieces), lax.rem(j, pieces)
        owner, at = b // per_head, lax.rem(b, per_head)
        @pl.when((owner // 2 != my_chip) & (lax.rem(owner, 2) == my_core))
        def _():
            give_send(b, c).wait_recv()

            def tile(i, carry):
                now = pl.ds(pl.multiple_of(i * TILE, TILE), TILE)
                part[b, c, now, :] = (
                    part[b, c, now, :].astype(jnp.float32)
                    + pair[owner // 2, at, c, now, :].astype(jnp.float32)
                ).astype(jnp.bfloat16)
                return carry

            lax.fori_loop(0, tokens // TILE, tile, 0)
            sum_send(b, c).start()

    def use(j):
        b, c = block_of(j // pieces), lax.rem(j, pieces)
        for s in range(halves):
            for o in range(1, groups):
                across_arrival(b, c, s, o).wait_recv()
        project(b, c)

    def settle(b, c, at_rows, first=0, past=wide):
        cb = lax.rem(b, per_head)
        span = gate_ref.shape[1]
        for u in range(first // span, past // span):
            lanes = slice(u * span, (u + 1) * span)
            summed = part[b, c, at_rows, lanes].astype(jnp.float32)
            for slot in range(chips):
                summed = summed + got[slot, cb, c, at_rows, lanes].astype(jnp.float32)
            block = cb * (cols // span) + c * (wide // span) + u
            at = pl.ds(pl.multiple_of(block * span, span), span)
            out_ref[at_rows, at] = (gate_ref[pl.ds(block, 1), :] * summed).astype(out_ref.dtype)

    def finish(j):
        b, c = block_of(j // pieces), lax.rem(j, pieces)
        @pl.when(b // per_head == me)
        def _():
            for slot in range(chips):
                term_arrival(b, c, slot).wait_recv()
            settle(b, c, slice(0, tokens))

    last_b, last_c = block_of(n - 1), pieces - 1
    last_owner, last_at = last_b // per_head, lax.rem(last_b, per_head)
    other_chip = last_owner // 2 != my_chip
    same_core = lax.rem(last_owner, 2) == my_core

    def tile_send(i, s, dst, recv, device):
        now = slice(i * TILE, (i + 1) * TILE)
        return remote(
            part.at[last_b, last_c, now, lanes_in(s)], dst.at[last_at, last_c, now, lanes_in(s)],
            t_send.at[s, i], recv, device,
        )

    def to_partner(i, s):
        return tile_send(i, s, got.at[0], t_recv.at[0, s, i], {"head": partner})

    def to_collector(i, s):
        return tile_send(i, s, pair.at[last_owner // 2], t_pair.at[s, i], {"head": partner})

    def to_owner(i, s):
        slot = lax.rem(my_chip - last_owner // 2 + chips, chips)
        return tile_send(i, s, got.at[slot], t_recv.at[slot, s, i], {"head": last_owner})

    def tile_arrival(i, s, slot):
        return tile_send(i, s, got.at[slot], t_recv.at[slot, s, i], {"head": partner})

    def last_terms(s):
        lanes = lanes_in(s)
        if s < halves - 1:
            for o in range(1, groups):
                across_arrival(last_b, last_c, s, o).wait_recv()
        part[last_b, last_c, :, lanes] = jnp.dot(
            attended[...], w_all[last_b, last_c, :, lanes], preferred_element_type=jnp.float32
        ).astype(jnp.bfloat16)
        for i in range(per_slab):
            @pl.when(last_owner == partner)
            def _(i=i):
                to_partner(i, s).start()
            @pl.when(other_chip & jnp.logical_not(same_core))
            def _(i=i):
                to_collector(i, s).start()

    def last_collect(s):
        lanes = lanes_in(s)
        @pl.when(other_chip & same_core)
        def _():
            for i in range(per_slab):
                now = slice(i * TILE, (i + 1) * TILE)
                to_collector(i, s).wait_recv()
                part[last_b, last_c, now, lanes] = (
                    part[last_b, last_c, now, lanes].astype(jnp.float32)
                    + pair[last_owner // 2, last_at, last_c, now, lanes].astype(jnp.float32)
                ).astype(jnp.bfloat16)
                to_owner(i, s).start()

    def last_finish():
        @pl.when(last_owner == me)
        def _():
            for s in range(halves):
                for i in range(per_slab):
                    for slot in range(chips):
                        tile_arrival(i, s, slot).wait_recv()
                    settle(
                        last_b, last_c, slice(i * TILE, (i + 1) * TILE),
                        s * sub_cols, (s + 1) * sub_cols,
                    )

    def do_use(j, carry):
        use(j)
        collect(j - 1)
        return carry

    def do_finish(j, carry):
        finish(j)
        return carry

    def own_block(c, carry):
        project(t, c)
        @pl.when(c > 0)
        def _():
            collect(c - 1)
        return carry

    @pl.when(inner)
    def _():
        for copy in in_copies:
            copy.wait()
        set_bias(0, keep_own)

        def own_slab(h, carry):
            for which in range(2):
                kv_arrival(end, h, which).wait_recv()
                kv_relay(h, which).start()
            for which in range(2):
                kv_arrival(across_mid, h, which).wait_recv()
            attend(h, t, q_own, 0, attended)
            return carry

        lax.fori_loop(0, head_count, own_slab, 0)
        for c in range(pieces):
            for s in range(halves):
                first_send(c, s, 1).start()
        for c in range(pieces):
            own_copy(c).wait()
        lax.fori_loop(0, pieces, own_block, 0)
        keep_copy.wait_recv()
        set_bias(1, keep_far)

        def end_slab(h, carry):
            q_copy(h).wait_recv()
            for which in range(2):
                kv_arrival(far_end, h, which).wait_recv()
            attend(h, end, q_far, 1, far_att)
            att_copy(h).start()
            return carry

        lax.fori_loop(0, head_count, end_slab, 0)

    def early_pass(j, carry):
        pass_on(j)
        return carry

    @pl.when(outer)
    def _():
        lax.fori_loop(pieces, 2 * pieces, early_pass, 0)
        for c in range(pieces):
            own_copy(c).wait()
        for h in range(head_count):
            att_copy(h).wait_recv()
        lax.fori_loop(0, pieces, own_block, 0)

    @pl.when(outer)
    def _():
        lax.fori_loop(pieces, 2 * pieces, do_use, 0)

    def used_by(j):
        lagging = jnp.maximum(jnp.maximum(j - pieces - 1, 3 * j - 7 * pieces - 1), pieces)
        return jnp.where(inner, jnp.minimum(lagging, j - 1), jnp.maximum(j - 1, 2 * pieces))

    def settled_by(j):
        most = jnp.where(inner, pieces, 2 * pieces)
        return jnp.clip(2 * (j - 2 * pieces) - 2, 0, most)

    def step(j, carry):
        pass_on(j)
        @pl.when(inner & (j >= 2 * pieces + 1) & (j < 3 * pieces + 1))
        def _():
            pass_on(j - pieces - 1)
        lax.fori_loop(used_by(j - 1), used_by(j), do_use, 0)
        return lax.fori_loop(settled_by(j - 1), settled_by(j), do_finish, carry)

    gate_copy.wait()
    lax.fori_loop(2 * pieces, total_pieces - 2, step, 0)
    pass_on(total_pieces - 2)

    @pl.when(inner)
    def _():
        for o in range(1, groups):
            theirs_on(end, o, mid_id).start()
    until = jnp.where(inner, total_pieces - 3, total_pieces - 2)
    lax.fori_loop(used_by(total_pieces - 3), until, do_use, 0)
    settled = jnp.where(inner, pieces, 3 * pieces)
    lax.fori_loop(settled_by(total_pieces - 3), settled, do_finish, 0)

    @pl.when(outer)
    def _():
        for h in range(head_count):
            for which in range(2):
                kv_first(h, which, mate_id).wait_send()
            q_copy(h).wait_send()
        keep_copy.wait_send()

    @pl.when(inner)
    def _():
        for h in range(head_count):
            for which in range(2):
                kv_first(h, which, mid_id).wait_send()
                kv_relay(h, which).wait_send()
            att_copy(h).wait_send()
        for c in range(pieces):
            for s in range(halves):
                first_send(c, s, 1).wait_send()

    @pl.when(outer)
    def _():
        collect(total_pieces - 3)

    for s in range(halves):
        relay(last_b, last_c, s, 0).wait_recv()
        @pl.when(inner)
        def _(s=s):
            relay(last_b, last_c, s, 0).start()
        if s < halves - 1:
            for o in range(1, groups):
                across(last_b, last_c, s, o).start()
            @pl.when(outer)
            def _():
                use(total_pieces - 2)
                collect(total_pieces - 2)
    for o in range(1, groups):
        across_arrival(last_b, last_c, halves - 1, o).wait_recv()
        @pl.when(inner)
        def _(o=o):
            theirs_on(last_b, o, mate_id).start()

    @pl.when(inner)
    def _():
        lax.fori_loop(until, total_pieces - 2, do_use, 0)
        use(total_pieces - 2)
        collect(total_pieces - 3)
        collect(total_pieces - 2)

    for s in range(halves):
        last_terms(s)
        last_collect(s)
    lax.fori_loop(settled, total_pieces - 1, do_finish, 0)

    def drain(b, carry):
        for c in range(pieces):
            for s in range(halves):
                @pl.when(b == t)
                def _(c=c, s=s):
                    first_send(c, s, 0).wait_send()
                @pl.when((b == t) & outer)
                def _(c=c, s=s):
                    for o in range(1, groups):
                        rest_send(c, s, o).wait_send()
                last_part = c == pieces - 1 and s == halves - 1
                sent = (b != t) & (outer | (b != end))
                if last_part:
                    sent = ((b != t) & (b != last_b)) | (inner & (b == last_b))
                @pl.when(sent)
                def _(c=c, s=s):
                    for o in range(1, groups):
                        across(b, c, s, o).wait_send()
                @pl.when(inner & (b == end))
                def _(c=c, s=s):
                    relay(b, c, s, 1).wait_send()
                @pl.when(inner & (b != end) & (b != t))
                def _(c=c, s=s):
                    relay(b, c, s, 0).wait_send()
            @pl.when((b // per_head != me) & ((b != last_b) | (c != last_c)))
            def _(c=c):
                partner_send(b, c).wait_send()
        return carry

    lax.fori_loop(0, n, drain, 0)
    last_finish()
    @pl.when(last_owner != me)
    def _():
        for s in range(halves):
            for i in range(per_slab):
                to_partner(i, s).wait_send()


def chain_shards(queries, key_rows, value_rows, keep_tiles, out_weight, gate_scale):
    n, heads, groups = lax.axis_size("tm"), lax.axis_size("head"), lax.axis_size("groups")
    tokens = queries.shape[0]
    head_count = queries.shape[1]
    flat = head_count * HD
    rows, cols = out_weight.shape
    pieces = cols // 256 if cols % 256 == 0 else 1
    wide = cols // pieces
    per_head = n // heads
    if pieces < 4 or wide % 256:
        return shards(queries, key_rows, value_rows, keep_tiles, out_weight, gate_scale)
    gate_lanes = 128 if wide % 128 == 0 else wide
    vmem = pl.BlockSpec(memory_space=pltpu.VMEM)
    hbm = pl.BlockSpec(memory_space=pl.ANY)
    dma = pltpu.SemaphoreType.DMA
    bf16 = jnp.bfloat16
    return pl.pallas_call(
        functools.partial(chain_kernel, (groups, n, heads, pieces)),
        out_shape=pltpu.VMEM((tokens, gate_scale.shape[0]), bf16),
        in_specs=[hbm, hbm, hbm, hbm, hbm, hbm],
        out_specs=vmem,
        scratch_shapes=[
            pltpu.VMEM((head_count, tokens, HD), bf16),
            pltpu.VMEM((head_count, tokens, HD), bf16),
            pltpu.VMEM((n, head_count, tokens, HD), bf16),
            pltpu.VMEM((n, head_count, tokens, HD), bf16),
            pltpu.VMEM((n, pieces, rows, wide), bf16),
            pltpu.VMEM((tokens, flat), bf16),
            pltpu.VMEM((tokens, flat), bf16),
            pltpu.VMEM((n, pieces, tokens, wide), bf16),
            pltpu.VMEM((heads // 2, per_head, pieces, tokens, wide), bf16),
            pltpu.VMEM((heads // 2, per_head, pieces, tokens, wide), bf16),
            pltpu.VMEM(keep_tiles.shape, jnp.int32),
            pltpu.VMEM(keep_tiles.shape, jnp.int32),
            pltpu.VMEM((gate_scale.shape[0] // gate_lanes, gate_lanes), jnp.float32),
            pltpu.VMEM((2, keep_tiles.shape[0], keep_tiles.shape[1] * TILE), jnp.float32),
            dma((2, 2, head_count)),
            dma((n, 2, head_count)),
            dma((head_count,)),
            dma((head_count,)),
            dma((2,)),
            dma((head_count,)),
            dma((head_count,)),
            dma((2, n, pieces, 2)),
            dma((n, pieces, 2)),
            dma((groups - 1, n, pieces, 2)),
            dma((groups - 1, n, pieces, 2)),
            dma((n, pieces)),
            dma((heads // 2, per_head, pieces)),
            dma((heads // 2, per_head, pieces)),
            dma((2, tokens // TILE)),
            dma((heads // 2, 2, tokens // TILE)),
            dma((2, tokens // TILE)),
            dma((pieces,)),
            dma((4,)),
            dma((1,)),
        ],
        compiler_params=pltpu.CompilerParams(
            collective_id=0, has_side_effects=True, vmem_limit_bytes=56 * 1024 * 1024
        ),
    )(
        queries.transpose(1, 0, 2),
        key_rows.transpose(1, 0, 2),
        value_rows.transpose(1, 0, 2),
        keep_tiles,
        out_weight,
        gate_scale.reshape(-1, gate_lanes),
    )


def solution(mesh):
    placed = (
        P(("groups", "tm"), "head", None),
        P(("groups", "tm"), "head", None),
        P(("groups", "tm"), "head", None),
        P(("groups", "tm"), None),
        P("head", "tm"),
        P(("groups", "head")),
    )
    n, heads = mesh.shape["tm"], mesh.shape["head"]
    chain = n == 4 and n % heads == 0 and heads % 2 == 0 and mesh.shape["groups"] > 1
    body = chain_shards if chain else shards
    return jax.shard_map(
        body, mesh=mesh, in_specs=placed, out_specs=P(("groups", "tm"), "head"), check_vma=False
    )
```

```python
import functools
import math

import jax
import jax.numpy as jnp
from jax import lax
from jax.experimental import pallas as pl
from jax.experimental.pallas import tpu as pltpu
from jax.sharding import PartitionSpec as P

HD = 128
TILE = 128
MESH = pl.DeviceIdType.MESH


def layer_kernel(
    sizes, q_ref, k_ref, v_ref, keep_ref, w_ref, gate_ref, out_ref,
    q_own, k_all, v_all, w_all, attended, part, got,
    kv_send, kv_recv, z_send, z_recv, y_send, y_recv, r_send, r_recv, own_sem, in_sem,
):
    groups, n, heads, reach, pieces = sizes
    g, t, me = lax.axis_index("groups"), lax.axis_index("tm"), lax.axis_index("head")
    rows, cols = w_ref.shape
    wide = cols // pieces
    per_head = n // heads
    part_rows = rows // groups
    head_count, tokens = q_ref.shape[0], q_ref.shape[1]
    slabs = 2 * reach + 1

    barrier = pltpu.get_barrier_semaphore()
    partners = []
    for d in range(1, reach + 1):
        partners += [{"tm": lax.rem(t + d, n)}, {"tm": lax.rem(t + n - d, n)}]
    for o in range(1, groups):
        partners.append({"groups": lax.rem(g + o, groups)})
    for o in range(1, heads):
        partners.append({"head": lax.rem(me + o, heads)})
    for partner in partners:
        pl.semaphore_signal(barrier, inc=1, device_id=partner, device_id_type=MESH)
    pl.semaphore_wait(barrier, len(partners))

    def remote(src, dst, send, recv, device):
        return pltpu.make_async_remote_copy(
            src_ref=src, dst_ref=dst, send_sem=send, recv_sem=recv,
            device_id=device, device_id_type=MESH,
        )

    kv_copies = []
    for d in range(1, reach + 1):
        for slot, to in ((reach - d, lax.rem(t + d, n)), (reach + d, lax.rem(t + n - d, n))):
            for which, (src, dst) in enumerate(((k_ref, k_all), (v_ref, v_all))):
                kv_copies.append(
                    remote(src, dst.at[slot], kv_send.at[slot, which], kv_recv.at[slot, which], {"tm": to})
                )
    @pl.when(t == 0)
    def _():
        for copy in reversed(kv_copies):
            copy.start()

    @pl.when(t != 0)
    def _():
        for copy in kv_copies:
            copy.start()

    in_copies = [
        pltpu.make_async_copy(src, dst, in_sem.at[i])
        for i, (src, dst) in enumerate(
            ((q_ref, q_own), (k_ref, k_all.at[reach]), (v_ref, v_all.at[reach]))
        )
    ]
    for copy in in_copies:
        copy.start()

    my_rows = pl.ds(pl.multiple_of(g * part_rows, part_rows), part_rows)

    def own_copy(c):
        return pltpu.make_async_copy(
            w_ref.at[:, c * wide:(c + 1) * wide], w_all.at[t, c], own_sem.at[c]
        )

    def first_send(c, side):
        to = jnp.minimum(t + 1, n - 1) if side else jnp.maximum(t - 1, 0)
        return remote(
            w_ref.at[my_rows, c * wide:(c + 1) * wide], w_all.at[t, c, my_rows],
            z_send.at[side, t, c], z_recv.at[t, c], {"tm": to},
        )

    def relay(b, c, side):
        to = jnp.minimum(t + 1, n - 1) if side else jnp.maximum(t - 1, 0)
        return remote(
            w_all.at[b, c, my_rows], w_all.at[b, c, my_rows],
            z_send.at[side, b, c], z_recv.at[b, c], {"tm": to},
        )

    def across(b, c, o):
        return remote(
            w_all.at[b, c, my_rows], w_all.at[b, c, my_rows],
            y_send.at[o - 1, b, c], y_recv.at[o - 1, b, c],
            {"groups": lax.rem(g + o, groups)},
        )

    def across_arrival(b, c, o):
        sender = lax.rem(g + groups - o, groups)
        their_rows = pl.ds(pl.multiple_of(sender * part_rows, part_rows), part_rows)
        return remote(
            w_all.at[b, c, their_rows], w_all.at[b, c, their_rows],
            y_send.at[o - 1, b, c], y_recv.at[o - 1, b, c],
            {"groups": lax.rem(g + o, groups)},
        )

    def term_send(b, c, o):
        return remote(
            part.at[b, c], got.at[o - 1, b % per_head, c],
            r_send.at[b, c], r_recv.at[o - 1, b % per_head, c],
            {"head": lax.rem(me + o, heads)},
        )

    for c in range(pieces):
        own_copy(c).start()
        @pl.when(t < n - 1)
        def _(c=c):
            first_send(c, 1).start()
        @pl.when(t > 0)
        def _(c=c):
            first_send(c, 0).start()

    for copy in in_copies:
        copy.wait()
    for copy in kv_copies:
        copy.wait_recv()

    scale = 1.0 / math.sqrt(HD)
    per_slab = tokens // TILE

    early = min(pieces, head_count - 1)

    def pass_on(j, side):
        step, c = j // pieces, j % pieces
        b = (t - 1 - step) if side else (t + 1 + step)
        @pl.when((b >= 0) & (b <= n - 1))
        def _():
            relay(b, c, side).wait_recv()
            @pl.when((t < n - 1) if side else (t > 0))
            def _():
                relay(b, c, side).start()
            for o in range(1, groups):
                across(b, c, o).start()

    def one_head(h, carry):
        lanes = pl.ds(pl.multiple_of(h * HD, HD), HD)
        for i in range(per_slab):
            q = q_own[h, i * TILE:(i + 1) * TILE, :]
            scores = []
            for j in range(slabs):
                s = lax.dot_general(
                    q, k_all[j, h], (((1,), (1,)), ((), ())), preferred_element_type=jnp.float32
                )
                bias = jnp.concatenate(
                    [
                        jnp.full(
                            (1, TILE),
                            jnp.where(keep_ref[i, j * per_slab + u] > 0, 0.0, -jnp.inf),
                            jnp.float32,
                        )
                        for u in range(per_slab)
                    ],
                    axis=1,
                )
                scores.append(s * scale + bias)
            peak = functools.reduce(
                jnp.maximum, [jnp.max(s, axis=1, keepdims=True) for s in scores]
            )
            exps = [jnp.exp(s - peak) for s in scores]
            total = functools.reduce(jnp.add, [jnp.sum(e, axis=1, keepdims=True) for e in exps])
            inverse = 1.0 / total
            acc = None
            for j in range(slabs):
                term = jnp.dot(
                    (exps[j] * inverse).astype(jnp.bfloat16), v_all[j, h],
                    preferred_element_type=jnp.float32,
                )
                acc = term if acc is None else acc + term
            attended[i * TILE:(i + 1) * TILE, lanes] = acc.astype(jnp.bfloat16)
        @pl.when(h >= head_count - early)
        def _():
            for side in (1, 0):
                pass_on(h - (head_count - early), side)
        return carry

    lax.fori_loop(0, head_count, one_head, 0)

    def project(b, c):
        def tile(i, carry):
            at = pl.ds(pl.multiple_of(i * TILE, TILE), TILE)
            part[b, c, at, :] = jnp.dot(
                attended[at, :], w_all[b, c], preferred_element_type=jnp.float32
            ).astype(jnp.bfloat16)
            return carry

        lax.fori_loop(0, tokens // TILE, tile, 0)
        owner = b // per_head
        for o in range(1, heads):
            @pl.when(owner == lax.rem(me + o, heads))
            def _():
                term_send(b, c, o).start()

    for c in range(pieces):
        own_copy(c).wait()
        project(t, c)

    def use(j, side):
        step, c = j // pieces, j % pieces
        b = (t - 1 - step) if side else (t + 1 + step)
        @pl.when((b >= 0) & (b <= n - 1))
        def _():
            for o in range(1, groups):
                across_arrival(b, c, o).wait_recv()
            project(b, c)

    count = (n - 1) * pieces

    def use_both(j, carry):
        for side in (1, 0):
            use(j, side)
        return carry

    def step(j, carry):
        for side in (1, 0):
            pass_on(j, side)
        first = jnp.minimum(2 * (j - early), j - 1)
        last = jnp.minimum(2 * (j - early) + 2, j)
        return lax.fori_loop(first, last, use_both, carry)

    lax.fori_loop(early, count, step, 0)
    lax.fori_loop(min(2 * (count - early), count - 1), count, use_both, 0)

    for cb in range(per_head):
        for c in range(pieces):
            b = me * per_head + cb
            for o in range(1, heads):
                term_send(b, c, o).wait_recv()
            span = wide if gate_ref.shape[0] == 1 else gate_ref.shape[1]
            for u in range(wide // span):
                lanes = slice(u * span, (u + 1) * span)
                summed = part[b, c, :, lanes].astype(jnp.float32)
                for o in range(1, heads):
                    summed = summed + got[o - 1, cb, c, :, lanes].astype(jnp.float32)
                at = cb * cols + c * wide + u * span
                gate = gate_ref[:, at:at + span] if span == wide else gate_ref[at // span:at // span + 1, :]
                out_ref[:, at:at + span] = (gate * summed).astype(out_ref.dtype)

    for copy in kv_copies:
        copy.wait_send()
    for c in range(pieces):
        @pl.when(t < n - 1)
        def _(c=c):
            first_send(c, 1).wait_send()
        @pl.when(t > 0)
        def _(c=c):
            first_send(c, 0).wait_send()

    def drain(b, carry):
        for c in range(pieces):
            @pl.when(b != t)
            def _(c=c):
                for o in range(1, groups):
                    across(b, c, o).wait_send()
            @pl.when((b < t) & (t < n - 1))
            def _(c=c):
                relay(b, c, 1).wait_send()
            @pl.when((b > t) & (t > 0))
            def _(c=c):
                relay(b, c, 0).wait_send()
            @pl.when(b // per_head != me)
            def _(c=c):
                term_send(b, c, 1).wait_send()
        return carry

    lax.fori_loop(0, n, drain, 0)


def shards(queries, key_rows, value_rows, keep_tiles, out_weight, gate_scale):
    n, heads, groups = lax.axis_size("tm"), lax.axis_size("head"), lax.axis_size("groups")
    reach = min(2, (n - 1) // 2)
    tokens = queries.shape[0]
    head_count = queries.shape[1]
    flat = head_count * HD
    rows, cols = out_weight.shape
    pieces = cols // 256 if cols % 256 == 0 else 1
    wide = cols // pieces
    per_head = n // heads
    slabs = 2 * reach + 1
    gate_lanes = 128 if wide % 128 == 0 else gate_scale.shape[0]
    vmem = pl.BlockSpec(memory_space=pltpu.VMEM)
    hbm = pl.BlockSpec(memory_space=pl.ANY)
    dma = pltpu.SemaphoreType.DMA
    bf16 = jnp.bfloat16
    return pl.pallas_call(
        functools.partial(layer_kernel, (groups, n, heads, reach, pieces)),
        out_shape=jax.ShapeDtypeStruct((tokens, gate_scale.shape[0]), bf16),
        in_specs=[hbm, hbm, hbm, pl.BlockSpec(memory_space=pltpu.SMEM), hbm, vmem],
        out_specs=vmem,
        scratch_shapes=[
            pltpu.VMEM((head_count, tokens, HD), bf16),
            pltpu.VMEM((slabs, head_count, tokens, HD), bf16),
            pltpu.VMEM((slabs, head_count, tokens, HD), bf16),
            pltpu.VMEM((n, pieces, rows, wide), bf16),
            pltpu.VMEM((tokens, flat), bf16),
            pltpu.VMEM((n, pieces, tokens, wide), bf16),
            pltpu.VMEM((heads - 1, per_head, pieces, tokens, wide), bf16),
            dma((slabs, 2)),
            dma((slabs, 2)),
            dma((2, n, pieces)),
            dma((n, pieces)),
            dma((groups - 1, n, pieces)),
            dma((groups - 1, n, pieces)),
            dma((n, pieces)),
            dma((heads - 1, per_head, pieces)),
            dma((pieces,)),
            dma((3,)),
        ],
        compiler_params=pltpu.CompilerParams(
            collective_id=0, has_side_effects=True, vmem_limit_bytes=56 * 1024 * 1024
        ),
    )(
        queries.transpose(1, 0, 2),
        key_rows.transpose(1, 0, 2),
        value_rows.transpose(1, 0, 2),
        keep_tiles,
        out_weight,
        gate_scale.reshape(-1, gate_lanes),
    )


def chain_kernel(
    sizes, q_ref, k_ref, v_ref, keep_hbm, w_ref, gate_hbm, out_ref,
    q_own, q_far, k_all, v_all, w_all, attended, far_att, part, got, pair, keep_own, keep_far, gate_ref, bias,
    kv_send, kv_recv, q_send, q_recv, keep_sem, att_send, att_recv,
    z_send, z_recv, y_send, y_recv, r_send, r_recv, pair_recv, t_send, t_recv, t_pair, own_sem, in_sem, gate_sem,
):
    groups, n, heads, pieces = sizes
    g, t, me = lax.axis_index("groups"), lax.axis_index("tm"), lax.axis_index("head")
    rows, cols = w_ref.shape
    wide = cols // pieces
    per_head = n // heads
    part_rows = rows // groups
    halves = 2
    sub_cols = wide // halves
    head_count, tokens = q_ref.shape[0], q_ref.shape[1]
    per_slab = tokens // TILE
    total_pieces = n * pieces
    chips = heads // 2
    my_chip, my_core = me // 2, lax.rem(me, 2)
    partner = me + 1 - 2 * my_core

    left = t < n // 2
    inner = (t > 0) & (t < n - 1)
    outer = jnp.logical_not(inner)
    end = jnp.where(left, 0, n - 1)
    near = jnp.where(left, 1, n - 2)
    across_mid = n - 1 - t
    far_end = n - 1 - end
    mate = jnp.where(inner, end, near)
    mate_id = {"tm": mate}
    mid_id = {"tm": across_mid}

    barrier = pltpu.get_barrier_semaphore()

    def greet(partner):
        pl.semaphore_signal(barrier, inc=1, device_id=partner, device_id_type=MESH)

    greet(mate_id)
    @pl.when(inner)
    def _():
        greet(mid_id)
    for o in range(1, groups):
        greet({"groups": lax.rem(g + o, groups)})
    for o in range(1, heads):
        greet({"head": lax.rem(me + o, heads)})
    @pl.when(inner)
    def _():
        pl.semaphore_wait(barrier, groups + heads)
    @pl.when(outer)
    def _():
        pl.semaphore_wait(barrier, groups + heads - 1)

    def remote(src, dst, send, recv, device):
        return pltpu.make_async_remote_copy(
            src_ref=src, dst_ref=dst, send_sem=send, recv_sem=recv,
            device_id=device, device_id_type=MESH,
        )

    kv = ((k_ref, k_all), (v_ref, v_all))

    def kv_first(h, which, device):
        src, dst = kv[which]
        return remote(
            src.at[h], dst.at[t, h], kv_send.at[0, which, h], kv_recv.at[t, which, h], device
        )

    def kv_relay(h, which):
        buf = kv[which][1]
        return remote(
            buf.at[end, h], buf.at[end, h], kv_send.at[1, which, h], kv_recv.at[end, which, h],
            mid_id,
        )

    def kv_arrival(slab, h, which):
        buf = kv[which][1]
        return remote(
            buf.at[slab, h], buf.at[slab, h], kv_send.at[1, which, h],
            kv_recv.at[slab, which, h], mid_id,
        )

    def q_copy(h):
        return remote(q_ref.at[h], q_far.at[h], q_send.at[h], q_recv.at[h], mate_id)

    keep_copy = remote(keep_hbm, keep_far, keep_sem.at[0], keep_sem.at[1], mate_id)

    def lanes_of(h):
        return pl.ds(pl.multiple_of(h * HD, HD), HD)

    def att_copy(h):
        return remote(
            far_att.at[:, lanes_of(h)], attended.at[:, lanes_of(h)],
            att_send.at[h], att_recv.at[h], mate_id,
        )

    def rows_of(sender):
        return pl.ds(pl.multiple_of(sender * part_rows, part_rows), part_rows)

    def lanes_in(s, c=0):
        return slice(c * wide + s * sub_cols, c * wide + (s + 1) * sub_cols)

    def own_copy(c):
        return pltpu.make_async_copy(
            w_ref.at[:, c * wide:(c + 1) * wide], w_all.at[t, c], own_sem.at[c]
        )

    def first_send(c, s, way):
        mine = rows_of(g)
        return remote(
            w_ref.at[mine, lanes_in(s, c)], w_all.at[t, c, mine, lanes_in(s)],
            z_send.at[way, t, c, s], z_recv.at[t, c, s], mid_id if way else mate_id,
        )

    def rest_send(c, s, o):
        theirs = rows_of(lax.rem(g + groups - o, groups))
        return remote(
            w_ref.at[theirs, lanes_in(s, c)], w_all.at[t, c, theirs, lanes_in(s)],
            y_send.at[o - 1, t, c, s], y_recv.at[o - 1, t, c, s], mate_id,
        )

    def relay(b, c, s, way):
        mine = rows_of(g)
        return remote(
            w_all.at[b, c, mine, lanes_in(s)], w_all.at[b, c, mine, lanes_in(s)],
            z_send.at[way, b, c, s], z_recv.at[b, c, s], mid_id if way else mate_id,
        )

    def across(b, c, s, o):
        mine = rows_of(g)
        return remote(
            w_all.at[b, c, mine, lanes_in(s)], w_all.at[b, c, mine, lanes_in(s)],
            y_send.at[o - 1, b, c, s], y_recv.at[o - 1, b, c, s],
            {"groups": lax.rem(g + o, groups)},
        )

    def theirs_on(b, o, device):
        c, s = pieces - 1, halves - 1
        theirs = rows_of(lax.rem(g + groups - o, groups))
        return remote(
            w_all.at[b, c, theirs, lanes_in(s)], w_all.at[b, c, theirs, lanes_in(s)],
            y_send.at[o - 1, b, c, s], y_recv.at[o - 1, b, c, s], device,
        )

    def across_arrival(b, c, s, o):
        theirs = rows_of(lax.rem(g + groups - o, groups))
        return remote(
            w_all.at[b, c, theirs, lanes_in(s)], w_all.at[b, c, theirs, lanes_in(s)],
            y_send.at[o - 1, b, c, s], y_recv.at[o - 1, b, c, s],
            {"groups": lax.rem(g + o, groups)},
        )

    def partner_send(b, c):
        at = lax.rem(b, per_head)
        return remote(
            part.at[b, c], got.at[0, at, c], r_send.at[b, c], r_recv.at[0, at, c],
            {"head": partner},
        )

    def give_send(b, c):
        owner, at = b // per_head, lax.rem(b, per_head)
        return remote(
            part.at[b, c], pair.at[owner // 2, at, c], r_send.at[b, c],
            pair_recv.at[owner // 2, at, c], {"head": partner},
        )

    def sum_send(b, c):
        owner, at = b // per_head, lax.rem(b, per_head)
        slot = lax.rem(my_chip - owner // 2 + chips, chips)
        return remote(
            part.at[b, c], got.at[slot, at, c], r_send.at[b, c], r_recv.at[slot, at, c],
            {"head": owner},
        )

    def term_arrival(b, c, slot):
        at = lax.rem(b, per_head)
        return remote(
            part.at[b, c], got.at[slot, at, c], r_send.at[b, c], r_recv.at[slot, at, c],
            {"head": partner},
        )

    in_copies = [
        pltpu.make_async_copy(src, dst, in_sem.at[i])
        for i, (src, dst) in enumerate(
            ((keep_hbm, keep_own), (q_ref, q_own), (k_ref, k_all.at[t]), (v_ref, v_all.at[t]))
        )
    ]

    gate_copy = pltpu.make_async_copy(gate_hbm, gate_ref, gate_sem.at[0])

    @pl.when(outer)
    def _():
        for h in range(head_count):
            for which in range(2):
                kv_first(h, which, mate_id).start()
        keep_copy.start()
        for h in range(head_count):
            q_copy(h).start()

    @pl.when(inner)
    def _():
        for h in range(head_count):
            for which in range(2):
                kv_first(h, which, mid_id).start()
        for copy in in_copies:
            copy.start()

    for c in range(pieces):
        for s in range(halves):
            first_send(c, s, 0).start()
        @pl.when(outer)
        def _(c=c):
            for s in range(halves):
                for o in range(1, groups):
                    rest_send(c, s, o).start()
    for c in range(pieces):
        own_copy(c).start()
    gate_copy.start()

    def block_of(k):
        place = jnp.where(left, t, n - 1 - t)
        b = jnp.where(k == 0, place, jnp.where(k == 1, 1 - place, k))
        return jnp.where(left, b, n - 1 - b)

    def pass_on(j):
        b, c = block_of(j // pieces), lax.rem(j, pieces)
        for s in range(halves):
            relay(b, c, s, 0).wait_recv()
            @pl.when(inner & (b == end))
            def _(s=s):
                relay(b, c, s, 1).start()
            @pl.when(inner & (b != end))
            def _(s=s):
                relay(b, c, s, 0).start()
            @pl.when(outer | (b != end))
            def _(s=s):
                for o in range(1, groups):
                    across(b, c, s, o).start()

    scale = math.log2(math.e) / math.sqrt(HD)
    reach_slabs = keep_own.shape[1] // per_slab

    def set_bias(at, ref):
        kept = ref[...]
        spread = jnp.concatenate(
            [jnp.broadcast_to(kept[:, c:c + 1], (per_slab, TILE)) for c in range(kept.shape[1])],
            axis=1,
        )
        bias[at] = jnp.where(spread > 0, 0.0, -jnp.inf).astype(jnp.float32)

    def attend(h, slab, queries, at, dst):
        for i in range(per_slab):
            q = queries[h, i * TILE:(i + 1) * TILE, :]
            scores = []
            for j in range(reach_slabs):
                other = lax.rem(slab + j - reach_slabs // 2 + n, n)
                s = lax.dot_general(
                    q, k_all[other, h], (((1,), (1,)), ((), ())),
                    preferred_element_type=jnp.float32,
                )
                scores.append(s * scale + bias[at, i:i + 1, j * tokens:(j + 1) * tokens])
            peak = functools.reduce(
                jnp.maximum, [jnp.max(s, axis=1, keepdims=True) for s in scores]
            )
            exps = [jnp.exp2(s - peak) for s in scores]
            total = functools.reduce(jnp.add, [jnp.sum(e, axis=1, keepdims=True) for e in exps])
            acc = None
            for j in range(reach_slabs):
                other = lax.rem(slab + j - reach_slabs // 2 + n, n)
                term = jnp.dot(
                    exps[j].astype(jnp.bfloat16), v_all[other, h],
                    preferred_element_type=jnp.float32,
                )
                acc = term if acc is None else acc + term
            dst[i * TILE:(i + 1) * TILE, lanes_of(h)] = (acc * (1.0 / total)).astype(jnp.bfloat16)

    def project(b, c):
        part[b, c] = jnp.dot(
            attended[...], w_all[b, c], preferred_element_type=jnp.float32
        ).astype(jnp.bfloat16)
        owner = b // per_head
        @pl.when(owner == partner)
        def _():
            partner_send(b, c).start()
        @pl.when((owner // 2 != my_chip) & (lax.rem(owner, 2) != my_core))
        def _():
            give_send(b, c).start()

    def collect(j):
        b, c = block_of(j // pieces), lax.rem(j, pieces)
        owner, at = b // per_head, lax.rem(b, per_head)
        @pl.when((owner // 2 != my_chip) & (lax.rem(owner, 2) == my_core))
        def _():
            give_send(b, c).wait_recv()

            def tile(i, carry):
                now = pl.ds(pl.multiple_of(i * TILE, TILE), TILE)
                part[b, c, now, :] = (
                    part[b, c, now, :].astype(jnp.float32)
                    + pair[owner // 2, at, c, now, :].astype(jnp.float32)
                ).astype(jnp.bfloat16)
                return carry

            lax.fori_loop(0, tokens // TILE, tile, 0)
            sum_send(b, c).start()

    def use(j):
        b, c = block_of(j // pieces), lax.rem(j, pieces)
        for s in range(halves):
            for o in range(1, groups):
                across_arrival(b, c, s, o).wait_recv()
        project(b, c)

    def settle(b, c, at_rows, first=0, past=wide):
        cb = lax.rem(b, per_head)
        span = gate_ref.shape[1]
        for u in range(first // span, past // span):
            lanes = slice(u * span, (u + 1) * span)
            summed = part[b, c, at_rows, lanes].astype(jnp.float32)
            for slot in range(chips):
                summed = summed + got[slot, cb, c, at_rows, lanes].astype(jnp.float32)
            block = cb * (cols // span) + c * (wide // span) + u
            at = pl.ds(pl.multiple_of(block * span, span), span)
            out_ref[at_rows, at] = (gate_ref[pl.ds(block, 1), :] * summed).astype(out_ref.dtype)

    def finish(j):
        b, c = block_of(j // pieces), lax.rem(j, pieces)
        @pl.when(b // per_head == me)
        def _():
            for slot in range(chips):
                term_arrival(b, c, slot).wait_recv()
            settle(b, c, slice(0, tokens))

    last_b, last_c = block_of(n - 1), pieces - 1
    last_owner, last_at = last_b // per_head, lax.rem(last_b, per_head)
    other_chip = last_owner // 2 != my_chip
    same_core = lax.rem(last_owner, 2) == my_core

    def tile_send(i, s, dst, recv, device):
        now = slice(i * TILE, (i + 1) * TILE)
        return remote(
            part.at[last_b, last_c, now, lanes_in(s)], dst.at[last_at, last_c, now, lanes_in(s)],
            t_send.at[s, i], recv, device,
        )

    def to_partner(i, s):
        return tile_send(i, s, got.at[0], t_recv.at[0, s, i], {"head": partner})

    def to_collector(i, s):
        return tile_send(i, s, pair.at[last_owner // 2], t_pair.at[s, i], {"head": partner})

    def to_owner(i, s):
        slot = lax.rem(my_chip - last_owner // 2 + chips, chips)
        return tile_send(i, s, got.at[slot], t_recv.at[slot, s, i], {"head": last_owner})

    def tile_arrival(i, s, slot):
        return tile_send(i, s, got.at[slot], t_recv.at[slot, s, i], {"head": partner})

    def last_terms(s):
        lanes = lanes_in(s)
        if s < halves - 1:
            for o in range(1, groups):
                across_arrival(last_b, last_c, s, o).wait_recv()
        part[last_b, last_c, :, lanes] = jnp.dot(
            attended[...], w_all[last_b, last_c, :, lanes], preferred_element_type=jnp.float32
        ).astype(jnp.bfloat16)
        for i in range(per_slab):
            @pl.when(last_owner == partner)
            def _(i=i):
                to_partner(i, s).start()
            @pl.when(other_chip & jnp.logical_not(same_core))
            def _(i=i):
                to_collector(i, s).start()

    def last_collect(s):
        lanes = lanes_in(s)
        @pl.when(other_chip & same_core)
        def _():
            for i in range(per_slab):
                now = slice(i * TILE, (i + 1) * TILE)
                to_collector(i, s).wait_recv()
                part[last_b, last_c, now, lanes] = (
                    part[last_b, last_c, now, lanes].astype(jnp.float32)
                    + pair[last_owner // 2, last_at, last_c, now, lanes].astype(jnp.float32)
                ).astype(jnp.bfloat16)
                to_owner(i, s).start()

    def last_finish():
        @pl.when(last_owner == me)
        def _():
            for s in range(halves):
                for i in range(per_slab):
                    for slot in range(chips):
                        tile_arrival(i, s, slot).wait_recv()
                    settle(
                        last_b, last_c, slice(i * TILE, (i + 1) * TILE),
                        s * sub_cols, (s + 1) * sub_cols,
                    )

    def do_use(j, carry):
        use(j)
        collect(j - 1)
        return carry

    def do_finish(j, carry):
        finish(j)
        return carry

    def own_block(c, carry):
        project(t, c)
        @pl.when(c > 0)
        def _():
            collect(c - 1)
        return carry

    @pl.when(inner)
    def _():
        for copy in in_copies:
            copy.wait()
        set_bias(0, keep_own)

        def own_slab(h, carry):
            for which in range(2):
                kv_arrival(end, h, which).wait_recv()
                kv_relay(h, which).start()
            for which in range(2):
                kv_arrival(across_mid, h, which).wait_recv()
            attend(h, t, q_own, 0, attended)
            return carry

        lax.fori_loop(0, head_count, own_slab, 0)
        for c in range(pieces):
            for s in range(halves):
                first_send(c, s, 1).start()
        for c in range(pieces):
            own_copy(c).wait()
        lax.fori_loop(0, pieces, own_block, 0)
        keep_copy.wait_recv()
        set_bias(1, keep_far)

        def end_slab(h, carry):
            q_copy(h).wait_recv()
            for which in range(2):
                kv_arrival(far_end, h, which).wait_recv()
            attend(h, end, q_far, 1, far_att)
            att_copy(h).start()
            return carry

        lax.fori_loop(0, head_count, end_slab, 0)

    def early_pass(j, carry):
        pass_on(j)
        return carry

    @pl.when(outer)
    def _():
        lax.fori_loop(pieces, 2 * pieces, early_pass, 0)
        for c in range(pieces):
            own_copy(c).wait()
        for h in range(head_count):
            att_copy(h).wait_recv()
        lax.fori_loop(0, pieces, own_block, 0)

    @pl.when(outer)
    def _():
        lax.fori_loop(pieces, 2 * pieces, do_use, 0)

    def used_by(j):
        lagging = jnp.maximum(jnp.maximum(j - pieces - 1, 3 * j - 7 * pieces - 1), pieces)
        return jnp.where(inner, jnp.minimum(lagging, j - 1), jnp.maximum(j - 1, 2 * pieces))

    def settled_by(j):
        most = jnp.where(inner, pieces, 2 * pieces)
        return jnp.clip(2 * (j - 2 * pieces) - 2, 0, most)

    def step(j, carry):
        pass_on(j)
        lax.fori_loop(used_by(j - 1), used_by(j), do_use, 0)
        @pl.when(inner & (j >= 2 * pieces + 1) & (j < 3 * pieces + 1))
        def _():
            pass_on(j - pieces - 1)
        return lax.fori_loop(settled_by(j - 1), settled_by(j), do_finish, carry)

    gate_copy.wait()
    lax.fori_loop(2 * pieces, total_pieces - 2, step, 0)
    pass_on(total_pieces - 2)

    @pl.when(inner)
    def _():
        for o in range(1, groups):
            theirs_on(end, o, mid_id).start()
    until = total_pieces - 2
    lax.fori_loop(used_by(total_pieces - 3), until, do_use, 0)
    settled = jnp.where(inner, pieces, 3 * pieces)
    lax.fori_loop(settled_by(total_pieces - 3), settled, do_finish, 0)

    @pl.when(outer)
    def _():
        for h in range(head_count):
            for which in range(2):
                kv_first(h, which, mate_id).wait_send()
            q_copy(h).wait_send()
        keep_copy.wait_send()

    @pl.when(inner)
    def _():
        for h in range(head_count):
            for which in range(2):
                kv_first(h, which, mid_id).wait_send()
                kv_relay(h, which).wait_send()
            att_copy(h).wait_send()
        for c in range(pieces):
            for s in range(halves):
                first_send(c, s, 1).wait_send()

    @pl.when(outer)
    def _():
        collect(total_pieces - 3)

    for s in range(halves):
        relay(last_b, last_c, s, 0).wait_recv()
        @pl.when(inner)
        def _(s=s):
            relay(last_b, last_c, s, 0).start()
        if s < halves - 1:
            for o in range(1, groups):
                across(last_b, last_c, s, o).start()
            @pl.when(outer)
            def _():
                use(total_pieces - 2)
                collect(total_pieces - 2)
    for o in range(1, groups):
        across_arrival(last_b, last_c, halves - 1, o).wait_recv()
        @pl.when(inner)
        def _(o=o):
            theirs_on(last_b, o, mate_id).start()

    @pl.when(inner)
    def _():
        lax.fori_loop(until, total_pieces - 2, do_use, 0)
        use(total_pieces - 2)
        collect(total_pieces - 3)
        collect(total_pieces - 2)

    for s in range(halves):
        last_terms(s)
        last_collect(s)
    lax.fori_loop(settled, total_pieces - 1, do_finish, 0)

    def drain(b, carry):
        for c in range(pieces):
            for s in range(halves):
                @pl.when(b == t)
                def _(c=c, s=s):
                    first_send(c, s, 0).wait_send()
                @pl.when((b == t) & outer)
                def _(c=c, s=s):
                    for o in range(1, groups):
                        rest_send(c, s, o).wait_send()
                last_part = c == pieces - 1 and s == halves - 1
                sent = (b != t) & (outer | (b != end))
                if last_part:
                    sent = ((b != t) & (b != last_b)) | (inner & (b == last_b))
                @pl.when(sent)
                def _(c=c, s=s):
                    for o in range(1, groups):
                        across(b, c, s, o).wait_send()
                @pl.when(inner & (b == end))
                def _(c=c, s=s):
                    relay(b, c, s, 1).wait_send()
                @pl.when(inner & (b != end) & (b != t))
                def _(c=c, s=s):
                    relay(b, c, s, 0).wait_send()
            @pl.when((b // per_head != me) & ((b != last_b) | (c != last_c)))
            def _(c=c):
                partner_send(b, c).wait_send()
        return carry

    lax.fori_loop(0, n, drain, 0)
    last_finish()
    @pl.when(last_owner != me)
    def _():
        for s in range(halves):
            for i in range(per_slab):
                to_partner(i, s).wait_send()


def chain_shards(queries, key_rows, value_rows, keep_tiles, out_weight, gate_scale):
    n, heads, groups = lax.axis_size("tm"), lax.axis_size("head"), lax.axis_size("groups")
    tokens = queries.shape[0]
    head_count = queries.shape[1]
    flat = head_count * HD
    rows, cols = out_weight.shape
    pieces = cols // 256 if cols % 256 == 0 else 1
    wide = cols // pieces
    per_head = n // heads
    if pieces < 4 or wide % 256:
        return shards(queries, key_rows, value_rows, keep_tiles, out_weight, gate_scale)
    gate_lanes = 128 if wide % 128 == 0 else wide
    vmem = pl.BlockSpec(memory_space=pltpu.VMEM)
    hbm = pl.BlockSpec(memory_space=pl.ANY)
    dma = pltpu.SemaphoreType.DMA
    bf16 = jnp.bfloat16
    return pl.pallas_call(
        functools.partial(chain_kernel, (groups, n, heads, pieces)),
        out_shape=pltpu.VMEM((tokens, gate_scale.shape[0]), bf16),
        in_specs=[hbm, hbm, hbm, hbm, hbm, hbm],
        out_specs=vmem,
        scratch_shapes=[
            pltpu.VMEM((head_count, tokens, HD), bf16),
            pltpu.VMEM((head_count, tokens, HD), bf16),
            pltpu.VMEM((n, head_count, tokens, HD), bf16),
            pltpu.VMEM((n, head_count, tokens, HD), bf16),
            pltpu.VMEM((n, pieces, rows, wide), bf16),
            pltpu.VMEM((tokens, flat), bf16),
            pltpu.VMEM((tokens, flat), bf16),
            pltpu.VMEM((n, pieces, tokens, wide), bf16),
            pltpu.VMEM((heads // 2, per_head, pieces, tokens, wide), bf16),
            pltpu.VMEM((heads // 2, per_head, pieces, tokens, wide), bf16),
            pltpu.VMEM(keep_tiles.shape, jnp.int32),
            pltpu.VMEM(keep_tiles.shape, jnp.int32),
            pltpu.VMEM((gate_scale.shape[0] // gate_lanes, gate_lanes), jnp.float32),
            pltpu.VMEM((2, keep_tiles.shape[0], keep_tiles.shape[1] * TILE), jnp.float32),
            dma((2, 2, head_count)),
            dma((n, 2, head_count)),
            dma((head_count,)),
            dma((head_count,)),
            dma((2,)),
            dma((head_count,)),
            dma((head_count,)),
            dma((2, n, pieces, 2)),
            dma((n, pieces, 2)),
            dma((groups - 1, n, pieces, 2)),
            dma((groups - 1, n, pieces, 2)),
            dma((n, pieces)),
            dma((heads // 2, per_head, pieces)),
            dma((heads // 2, per_head, pieces)),
            dma((2, tokens // TILE)),
            dma((heads // 2, 2, tokens // TILE)),
            dma((2, tokens // TILE)),
            dma((pieces,)),
            dma((4,)),
            dma((1,)),
        ],
        compiler_params=pltpu.CompilerParams(
            collective_id=0, has_side_effects=True, vmem_limit_bytes=56 * 1024 * 1024
        ),
    )(
        queries.transpose(1, 0, 2),
        key_rows.transpose(1, 0, 2),
        value_rows.transpose(1, 0, 2),
        keep_tiles,
        out_weight,
        gate_scale.reshape(-1, gate_lanes),
    )


def solution(mesh):
    placed = (
        P(("groups", "tm"), "head", None),
        P(("groups", "tm"), "head", None),
        P(("groups", "tm"), "head", None),
        P(("groups", "tm"), None),
        P("head", "tm"),
        P(("groups", "head")),
    )
    n, heads = mesh.shape["tm"], mesh.shape["head"]
    chain = n == 4 and n % heads == 0 and heads % 2 == 0 and mesh.shape["groups"] > 1
    body = chain_shards if chain else shards
    return jax.shard_map(
        body, mesh=mesh, in_specs=placed, out_specs=P(("groups", "tm"), "head"), check_vma=False
    )
```
